32 devices in a mesh: dp: 4 (over x, core), tensor: 8 (over z, y).
Axes of the slice: x: 2, y: 2, z: 4, core: 2. Of those that a mesh axis runs over, the one named last changes fastest.
Arguments:
- activations: bfloat16 [512, 7168], P('dp', 'tensor'), may hold values from -6 to 6
- cotangent: bfloat16 [512, 7168], P('dp', 'tensor'), may hold values from -6 to 6
- up_weight_blocks: bfloat16 [1792, 128, 128], P('tensor'), may hold values from -0.125 to 0.125
- down_weight_blocks: bfloat16 [1792, 128, 128], P('tensor'), may hold values from -0.09375 to 0.09375
- up_first_moment: float32 [1792, 128, 128], P('tensor', 'dp'), may hold values from -60 to 60
- up_second_moment: float32 [1792, 128, 128], P('tensor', 'dp'), may hold values from 16 to 400
- down_first_moment: float32 [1792, 128, 128], P('tensor', 'dp'), may hold values from -60 to 60
- down_second_moment: float32 [1792, 128, 128], P('tensor', 'dp'), may hold values from 16 to 400
- source: int32 [1792], replicated, may hold values from -1 to 1791, as said below
- new_row: int32 [1792], P('tensor'), may hold values from 0 to 55, as said below
- new_col: int32 [1792], P('tensor'), may hold values from 0 to 127, as said below
- col_owner: int32 [128], replicated, may hold values from 0 to 7, as said below
Outputs:
- output: bfloat16 [512, 7168], P('dp', 'tensor')
- input_grad: bfloat16 [512, 7168], P('dp', 'tensor')
- up_step: float32 [1792, 128, 128], P('tensor', 'dp')
- down_step: float32 [1792, 128, 128], P('tensor', 'dp')
The draws below stay inside these ranges and needn't reach their ends.
Inputs may be any that keep to these rules, and one draw needn't show every extreme that they name: source names each old slot (device of tensor * 224 + slot) at most once; the blocks that move from one device of tensor to another device number at most 28, and exactly 28 for some pairs in every draw; the share of regrown blocks differs from device to device. `new_row`: the blocks of one column block lie in distinct row blocks. `new_col`: every slot of a device of tensor holds a column block that col_owner gives to that device; a column block holds 1 to 27 blocks. `col_owner`: each device of tensor owns exactly 16 column blocks.
All inputs are finite; a program needn't handle non-finite values.
Results may differ from the reference program's by a relative error of at most 0.012.
Values may be sent and summed in bfloat16 or wider, within the bound.
No kernel may reach another device: no remote copies, remote signals or barrier semaphores. Data moves between devices by JAX's collectives and lax.ppermute only.
A program may use at most 256 MiB of HBM per device.

```python
import math
import jax
import jax.numpy as jnp
from jax import lax

D = 7168
HIDDEN_UNITS = 16384
BLOCK_SIDE = 128
TOKENS = 512
RB = 56
NC = 128
LIVE_PER_COLUMN = 14
COLS_DEV = 16
SLOTS = 224
LIVE_TOTAL = 1792
N_TENSOR = 8


def permute_each(one_key, length):

    def single(sub_key):
        return jax.random.permutation(sub_key, length).astype(jnp.int32)
    return jax.vmap(single)(jax.random.split(one_key, N_TENSOR))


def layout_tables(key):
    keys = jax.random.split(key, 9)
    devices = jnp.arange(N_TENSOR, dtype=jnp.int32)
    col_order = jax.random.permutation(keys[0], NC).astype(jnp.int32)
    col_owner = jnp.zeros((NC,), jnp.int32).at[col_order].set(jnp.arange(NC, dtype=jnp.int32) // COLS_DEV)
    shifts = jax.random.randint(keys[1], (N_TENSOR, COLS_DEV // 2), 1 - LIVE_PER_COLUMN, LIVE_PER_COLUMN)
    counts = jnp.stack([LIVE_PER_COLUMN + shifts, LIVE_PER_COLUMN - shifts], axis=2).reshape(N_TENSOR, COLS_DEV)
    ends = jnp.cumsum(counts, axis=1)
    starts = ends - counts
    places = jnp.arange(SLOTS, dtype=jnp.int32)
    column_local = jnp.sum((places[None, None, :] >= ends[:, :, None]).astype(jnp.int32), axis=1)
    within = places[None, :] - jnp.take_along_axis(starts, column_local, axis=1)

    def row_perm(sub_key):
        return jax.random.permutation(sub_key, RB).astype(jnp.int32)
    row_orders = jax.vmap(row_perm)(jax.random.split(keys[2], N_TENSOR * COLS_DEV)).reshape(N_TENSOR, COLS_DEV * RB)
    rows_at = jnp.take_along_axis(row_orders, column_local * RB + within, axis=1)
    cols_at = jnp.take(col_order, devices[:, None] * COLS_DEV + column_local)
    spread = permute_each(keys[3], SLOTS)
    new_row = jnp.take_along_axis(rows_at, spread, axis=1)
    new_col = jnp.take_along_axis(cols_at, spread, axis=1)
    order_src = permute_each(keys[4], SLOTS)
    shift_ids = jnp.arange(N_TENSOR, dtype=jnp.int32)
    shift_counts = (SLOTS - shift_ids + N_TENSOR - 1) // N_TENSOR
    shift_starts = jnp.cumsum(shift_counts) - shift_counts
    shift = order_src % N_TENSOR
    depth = order_src // N_TENSOR
    sender = (devices[:, None] + shift) % N_TENSOR
    spot = jnp.take(shift_starts, shift) + depth
    old_layout = permute_each(keys[5], SLOTS)
    old_slot = old_layout[sender, spot]
    rates = jax.random.randint(keys[6], (N_TENSOR, 1), 0, 5)
    coins = jax.random.randint(keys[7], (N_TENSOR, SLOTS), 0, 8)
    spared = jax.random.randint(keys[8], (), 0, N_TENSOR)
    regrown = (coins < rates) & (devices[:, None] != spared)
    source = jnp.where(regrown, -1, sender * SLOTS + old_slot).astype(jnp.int32)
    return (source.reshape(-1), new_row.reshape(-1).astype(jnp.int32), new_col.reshape(-1).astype(jnp.int32), col_owner)


def draw_source(key, part):
    return layout_tables(jax.random.fold_in(key, 17))[0]


def draw_new_row(key, part):
    return layout_tables(jax.random.fold_in(key, 17))[1]


def draw_new_col(key, part):
    return layout_tables(jax.random.fold_in(key, 17))[2]


def draw_col_owner(key, part):
    return layout_tables(jax.random.fold_in(key, 17))[3]


def shard_levels(rng, dims, cuts, smallest, top_value):
    level = 1.0
    for axis_at, shards_of in cuts:
        draws = jax.random.uniform(jax.random.fold_in(jax.random.fold_in(rng, 6), axis_at), (shards_of,), jnp.float32, smallest / len(cuts), top_value / len(cuts))
        level = level * jnp.repeat(jnp.exp(draws), dims[axis_at] // shards_of).reshape((-1,) + (1,) * (len(dims) - 1 - axis_at))
    return level


def normal_values(key, extent, scale, limit, cuts=(), kind=jnp.bfloat16):
    gain = shard_levels(key, extent, cuts, -0.22, 0.18) if cuts else 1.0
    values = jax.random.normal(key, extent, jnp.float32) * scale * gain
    return jnp.minimum(jnp.maximum(values, -limit), limit).astype(kind)


def setup_inputs(seed: int = 0) -> dict:
    streams_of = jax.random.split(jax.random.key(seed), 13)
    activations = normal_values(streams_of[0], (TOKENS, D), 1.0, 6.0, ((0, 4), (1, 8)))
    cotangent = normal_values(streams_of[1], (TOKENS, D), 1.0, 6.0, ((0, 4), (1, 8)))
    up_weight_blocks = normal_values(streams_of[2], (LIVE_TOTAL, BLOCK_SIDE, BLOCK_SIDE), (LIVE_PER_COLUMN * BLOCK_SIDE) ** -0.5, 0.125, ((0, 8),))
    down_weight_blocks = normal_values(streams_of[3], (LIVE_TOTAL, BLOCK_SIDE, BLOCK_SIDE), (HIDDEN_UNITS // 4) ** -0.5, 0.09375, ((0, 8),))
    up_first_moment = normal_values(streams_of[4], (LIVE_TOTAL, BLOCK_SIDE, BLOCK_SIDE), 10.0, 60.0, ((0, 8), (1, 4)), jnp.float32)
    up_second_moment = jnp.clip(jnp.exp(math.log(400.0) - 3.218876 * jax.random.uniform(streams_of[5], (LIVE_TOTAL, BLOCK_SIDE, BLOCK_SIDE), jnp.float32) ** shard_levels(streams_of[5], (LIVE_TOTAL, BLOCK_SIDE, BLOCK_SIDE), ((0, 8), (1, 4)), -0.2, 0.2)), 16.0, 400.0)
    down_first_moment = normal_values(streams_of[6], (LIVE_TOTAL, BLOCK_SIDE, BLOCK_SIDE), 10.0, 60.0, ((0, 8), (1, 4)), jnp.float32)
    down_second_moment = jnp.clip(jnp.exp(math.log(400.0) - 3.218876 * jax.random.uniform(streams_of[7], (LIVE_TOTAL, BLOCK_SIDE, BLOCK_SIDE), jnp.float32) ** shard_levels(streams_of[7], (LIVE_TOTAL, BLOCK_SIDE, BLOCK_SIDE), ((0, 8), (1, 4)), -0.2, 0.2)), 16.0, 400.0)
    source = draw_source(jax.random.fold_in(streams_of[12], 71), 0)
    new_row = draw_new_row(jax.random.fold_in(streams_of[12], 71), 0)
    new_col = draw_new_col(jax.random.fold_in(streams_of[12], 71), 0)
    col_owner = draw_col_owner(jax.random.fold_in(streams_of[12], 71), 0)
    return {"activations": activations, "cotangent": cotangent, "up_weight_blocks": up_weight_blocks, "down_weight_blocks": down_weight_blocks, "up_first_moment": up_first_moment, "up_second_moment": up_second_moment, "down_first_moment": down_first_moment, "down_second_moment": down_second_moment, "source": source, "new_row": new_row, "new_col": new_col, "col_owner": col_owner}


gelu_scale = math.sqrt(2.0 / math.pi)

def gelu_pair(pre_act):
    inner = gelu_scale * (pre_act + 0.044715 * pre_act * pre_act * pre_act)
    tangent = jnp.tanh(inner)
    gelu_value = 0.5 * pre_act * (1.0 + tangent)
    gelu_slope = 0.5 * (1.0 + tangent) + 0.5 * pre_act * (1.0 - tangent * tangent) * gelu_scale * (1.0 + 3.0 * 0.044715 * pre_act * pre_act)
    return (gelu_value, gelu_slope)

def local_columns(col_owner):
    count_all = col_owner.shape[0]
    order = jnp.arange(count_all, dtype=jnp.int32)
    same = (col_owner[None, :] == col_owner[:, None]) & (order[None, :] < order[:, None])
    return lax.optimization_barrier(jnp.sum(same.astype(jnp.int32), axis=1)).astype(jnp.int32)

def rounded(values):
    narrow = values.astype(jnp.bfloat16)
    narrow = lax.optimization_barrier(narrow)
    return narrow.astype(jnp.float32)

def reference(activations, cotangent, up_weight_blocks, down_weight_blocks, up_first_moment, up_second_moment, down_first_moment, down_second_moment, source, new_row, new_col, col_owner):
    is_live = source >= 0
    picks = jnp.where(is_live, source, 0).astype(jnp.int32)

    def relocate(tiles):
        taken = jnp.take(tiles, picks, axis=0)
        return jnp.where(is_live[:, None, None], taken, jnp.zeros_like(taken))
    moved_up = relocate(up_weight_blocks).astype(jnp.float32)
    moved_down = relocate(down_weight_blocks).astype(jnp.float32)
    moved_up_first = relocate(up_first_moment)
    moved_up_second = relocate(up_second_moment)
    moved_down_first = relocate(down_first_moment)
    moved_down_second = relocate(down_second_moment)
    col_index = jnp.take(local_columns(col_owner), new_col).astype(jnp.int32)
    col_count = NC // N_TENSOR
    token_count = activations.shape[0]
    feat_blocks = activations.astype(jnp.float32).reshape(token_count, RB, BLOCK_SIDE)
    back_blocks = cotangent.astype(jnp.float32).reshape(token_count, RB, BLOCK_SIDE)
    highest = lax.Precision.HIGHEST
    pieces = (moved_up.reshape(N_TENSOR, SLOTS, BLOCK_SIDE, BLOCK_SIDE), moved_down.reshape(N_TENSOR, SLOTS, BLOCK_SIDE, BLOCK_SIDE), new_row.reshape(N_TENSOR, SLOTS), col_index.reshape(N_TENSOR, SLOTS))

    def one_group(carry, group):
        out_total, in_total = carry
        up_group, down_group, row_slot, col_slot = group
        feat_slots = jnp.take(feat_blocks, row_slot, axis=1)
        col_hot = (col_slot[:, None] == jnp.arange(col_count, dtype=jnp.int32)[None, :]).astype(jnp.float32)
        row_hot = (row_slot[:, None] == jnp.arange(RB, dtype=jnp.int32)[None, :]).astype(jnp.float32)
        up_part = jnp.einsum('tsk,skn->tsn', feat_slots, up_group, precision=highest)
        pre_act = jnp.einsum('tsn,sc->tcn', up_part, col_hot, precision=highest)
        gelu_value, gelu_slope = gelu_pair(pre_act)
        hidden_act = rounded(gelu_value)
        act_slots = jnp.take(hidden_act, col_slot, axis=1)
        down_part = jnp.einsum('tsn,snk->tsk', act_slots, down_group, precision=highest)
        out_term = jnp.einsum('tsk,sr->trk', down_part, row_hot, precision=highest).reshape(token_count, D)
        back_slots = jnp.take(back_blocks, row_slot, axis=1)
        down_weight_gradient = jnp.einsum('tsn,tsk->snk', act_slots, back_slots, precision=highest)
        back_part = jnp.einsum('tsk,snk->tsn', back_slots, down_group, precision=highest)
        back_act = jnp.einsum('tsn,sc->tcn', back_part, col_hot, precision=highest)
        back_pre = rounded(back_act * gelu_slope)
        pre_slots = jnp.take(back_pre, col_slot, axis=1)
        up_weight_gradient = jnp.einsum('tsk,tsn->skn', feat_slots, pre_slots, precision=highest)
        in_part = jnp.einsum('tsn,skn->tsk', pre_slots, up_group, precision=highest)
        in_term = jnp.einsum('tsk,sr->trk', in_part, row_hot, precision=highest).reshape(token_count, D)
        return ((out_total + rounded(out_term), in_total + rounded(in_term)), (up_weight_gradient, down_weight_gradient))
    start = (jnp.zeros((token_count, D), jnp.float32), jnp.zeros((token_count, D), jnp.float32))
    (out_total, in_total), (up_weight_gradient, down_weight_gradient) = lax.scan(one_group, start, pieces)
    up_weight_gradient = up_weight_gradient.reshape(LIVE_TOTAL, BLOCK_SIDE, BLOCK_SIDE)
    down_weight_gradient = down_weight_gradient.reshape(LIVE_TOTAL, BLOCK_SIDE, BLOCK_SIDE)
    first_up = 0.9 * moved_up_first + 0.1 * up_weight_gradient
    second_up = 0.95 * moved_up_second + 0.05 * up_weight_gradient * up_weight_gradient
    first_down = 0.9 * moved_down_first + 0.1 * down_weight_gradient
    second_down = 0.95 * moved_down_second + 0.05 * down_weight_gradient * down_weight_gradient
    up_step = first_up / (jnp.sqrt(second_up) + 1.0)
    down_step = first_down / (jnp.sqrt(second_down) + 1.0)
    return (out_total.astype(jnp.bfloat16), in_total.astype(jnp.bfloat16), up_step, down_step)
```

```python
import functools
import math

import jax
import jax.numpy as jnp
from jax import lax
from jax.experimental import pallas as pl
from jax.experimental.pallas import tpu as pltpu
from jax.sharding import PartitionSpec as P

gelu_scale = math.sqrt(2.0 / math.pi)
VMEM_LIMIT = 60 * 1024 * 1024

F32 = jnp.float32
BF16 = jnp.bfloat16
ANY = pl.BlockSpec(memory_space=pl.ANY)


def gelu_pair(pre_act):
    inner = gelu_scale * (pre_act + 0.044715 * pre_act * pre_act * pre_act)
    tangent = jnp.tanh(inner)
    gelu_value = 0.5 * pre_act * (1.0 + tangent)
    gelu_slope = 0.5 * (1.0 + tangent) + 0.5 * pre_act * (1.0 - tangent * tangent) * gelu_scale * (
        1.0 + 3.0 * 0.044715 * pre_act * pre_act
    )
    return (gelu_value, gelu_slope)


def local_columns(col_owner):
    count_all = col_owner.shape[0]
    order = jnp.arange(count_all, dtype=jnp.int32)
    same = (col_owner[None, :] == col_owner[:, None]) & (order[None, :] < order[:, None])
    return jnp.sum(same.astype(jnp.int32), axis=1)


def pack_weight(tiles, send_slots, dp_index, rows):
    slots, _, width = tiles.shape
    count = send_slots.shape[0]

    def kernel(send_ref, dp_ref, in_ref, out_ref):
        def step(i, carry):
            out_ref[i] = in_ref[send_ref[i]]
            return carry

        lax.fori_loop(0, count, step, 0, unroll=8)

    return pl.pallas_call(
        kernel,
        out_shape=jax.ShapeDtypeStruct((count, rows, width), tiles.dtype),
        grid_spec=pltpu.PrefetchScalarGridSpec(
            num_scalar_prefetch=2,
            grid=(1,),
            in_specs=[pl.BlockSpec((slots, rows, width), lambda i, s, d: (0, d[0], 0))],
            out_specs=pl.BlockSpec((count, rows, width), lambda i, s, d: (0, 0, 0)),
        ),
        compiler_params=pltpu.CompilerParams(vmem_limit_bytes=VMEM_LIMIT),
        cost_estimate=pl.CostEstimate(flops=0, transcendentals=0, bytes_accessed=4 * count * rows * width),
        name="pack_weight",
    )(send_slots, dp_index, tiles)


def pack_moments(arrays, send_slots):
    slots, rows, width = arrays[0].shape
    count = send_slots.shape[0]
    kinds = len(arrays)

    def kernel(send_ref, *refs):
        out_ref = refs[-1]

        def step(i, carry):
            s = send_ref[i]
            for k in range(kinds):
                out_ref[i, k] = refs[k][s].astype(BF16)
            return carry

        lax.fori_loop(0, count, step, 0, unroll=4)

    whole = pl.BlockSpec((slots, rows, width), lambda i, s: (0, 0, 0))
    return pl.pallas_call(
        kernel,
        out_shape=jax.ShapeDtypeStruct((count, kinds, rows, width), BF16),
        grid_spec=pltpu.PrefetchScalarGridSpec(
            num_scalar_prefetch=1,
            grid=(1,),
            in_specs=[whole] * kinds,
            out_specs=pl.BlockSpec((count, kinds, rows, width), lambda i, s: (0, 0, 0, 0)),
        ),
        compiler_params=pltpu.CompilerParams(vmem_limit_bytes=VMEM_LIMIT),
        cost_estimate=pl.CostEstimate(
            flops=0, transcendentals=0, bytes_accessed=6 * kinds * count * rows * width
        ),
        name="pack_moments",
    )(send_slots, *arrays)


def products_kernel(
    n_dp,
    slots,
    arrived,
    row_blocks,
    col_count,
    shard,
    chunk,
    row_ref,
    col_ref,
    home_ref,
    came_ref,
    kind_ref,
    place_ref,
    x_hbm,
    back_hbm,
    up_hbm,
    down_hbm,
    *refs,
):
    nx = n_dp // 2
    up_parts = refs[:n_dp]
    down_parts = refs[n_dp : 2 * n_dp]
    out_ref, in_ref = refs[2 * n_dp : 2 * n_dp + 2]
    grad_refs = refs[2 * n_dp + 2 : 2 * n_dp + 2 + n_dp]
    (
        x_v,
        back_v,
        up_v,
        down_v,
        up_a,
        down_a,
        x_t,
        pre,
        back,
        act,
        act_t,
        bpre,
        out_acc,
        in_acc,
        stage,
        in_sem,
        out_sem,
    ) = refs[2 * n_dp + 2 + n_dp :]
    block = up_v.shape[1]
    rows = block // n_dp
    per = shard // block
    my_x = place_ref[0]
    my_core = place_ref[1]

    first = [pltpu.make_async_copy(x_hbm, x_v, in_sem.at[0]), pltpu.make_async_copy(up_hbm, up_v, in_sem.at[1])]
    second = [
        pltpu.make_async_copy(back_hbm, back_v, in_sem.at[2]),
        pltpu.make_async_copy(down_hbm, down_v, in_sem.at[3]),
    ]
    for j in range(nx):
        for other in range(2):
            k = 2 * j + other
            owner = lax.rem(my_x + nx - j, nx) * 2 + (my_core + other) % 2
            first.append(pltpu.make_async_copy(up_parts[k], up_a.at[owner], in_sem.at[4 + k]))
            second.append(pltpu.make_async_copy(down_parts[k], down_a.at[owner], in_sem.at[4 + n_dp + k]))
    for copy in first + second:
        copy.start()

    zero_tile = jnp.zeros((block, block), F32)

    def clear_cols(c, carry):
        pre[c] = zero_tile
        back[c] = zero_tile
        return carry

    lax.fori_loop(0, col_count, clear_cols, 0)

    def clear_rows(r, carry):
        out_acc[r] = zero_tile
        in_acc[r] = zero_tile
        return carry

    lax.fori_loop(0, row_blocks, clear_rows, 0)

    def weight(own, came, g):
        kind = kind_ref[g]
        mine = own[home_ref[g]]
        at = came_ref[g]
        theirs = jnp.concatenate([came[q, at] for q in range(n_dp)], axis=0)
        picked = lax.select(kind == 1, mine, theirs)
        return lax.select(kind == 0, jnp.zeros_like(picked), picked)

    def columns(ref, r):
        a = lax.div(r, per)
        off = pl.multiple_of((r - a * per) * block, block)
        return ref[a, :, pl.ds(off, block)]

    unroll = 4
    for copy in first:
        copy.wait()

    def forward(i, carry):
        got = []
        for u in range(unroll):
            g = i * unroll + u
            w = weight(up_v, up_a, g)
            got.append(jnp.dot(columns(x_v, row_ref[g]), w, preferred_element_type=F32))
        for u in range(unroll):
            c = col_ref[i * unroll + u]
            pre[c] = pre[c] + got[u]
        return carry

    lax.fori_loop(0, slots // unroll, forward, 0)

    def turn_x(r, carry):
        x_t[r] = columns(x_v, r).T
        return carry

    lax.fori_loop(0, row_blocks, turn_x, 0)

    for copy in second:
        copy.wait()

    def backward(i, carry):
        got = []
        for u in range(unroll):
            g = i * unroll + u
            w = weight(down_v, down_a, g)
            got.append(
                lax.dot_general(
                    columns(back_v, row_ref[g]), w, (((1,), (1,)), ((), ())), preferred_element_type=F32
                )
            )
        for u in range(unroll):
            c = col_ref[i * unroll + u]
            back[c] = back[c] + got[u]
        return carry

    lax.fori_loop(0, slots // unroll, backward, 0)

    def bend(c, carry):
        value, slope = gelu_pair(pre[c])
        narrow = value.astype(BF16)
        act[c] = narrow
        act_t[c] = narrow.T
        bpre[c] = (back[c] * slope).astype(BF16)
        return carry

    lax.fori_loop(0, col_count, bend, 0)

    def ship(i, slot):
        copies = []
        for j in range(nx):
            for other in range(2):
                owner = lax.rem(my_x + j, nx) * 2 + (my_core + other) % 2
                start = pl.multiple_of(owner * rows, rows)
                for p in range(2):
                    copies.append(
                        pltpu.make_async_copy(
                            stage.at[slot, p, :, pl.ds(start, rows), :],
                            grad_refs[2 * j + other].at[p, pl.ds(i * chunk, chunk)],
                            out_sem.at[slot, 2 * (2 * j + other) + p],
                        )
                    )
        return copies

    def last(i, carry):
        slot = lax.rem(i, 2)

        @pl.when(i >= 2)
        def _():
            for copy in ship(i - 2, slot):
                copy.wait()

        for v in range(chunk // 2):
            got = []
            for u in range(2):
                g = i * chunk + v * 2 + u
                r = row_ref[g]
                c = col_ref[g]
                wd = weight(down_v, down_a, g)
                wu = weight(up_v, up_a, g)
                a = act[c]
                b = bpre[c]
                got.append(
                    (
                        r,
                        jnp.dot(a, wd, preferred_element_type=F32),
                        lax.dot_general(b, wu, (((1,), (1,)), ((), ())), preferred_element_type=F32),
                    )
                )
                stage[slot, 0, v * 2 + u] = jnp.dot(x_t[r], b, preferred_element_type=F32).astype(BF16)
                stage[slot, 1, v * 2 + u] = jnp.dot(
                    act_t[c], columns(back_v, r), preferred_element_type=F32
                ).astype(BF16)
            for r, o, n in got:
                out_acc[r] = out_acc[r] + o
                in_acc[r] = in_acc[r] + n
        for copy in ship(i, slot):
            copy.start()
        return carry

    chunks = slots // chunk
    lax.fori_loop(0, chunks, last, 0)

    for r in range(row_blocks):
        a, off = r // per, (r % per) * block
        out_ref[a, :, off : off + block] = out_acc[r].astype(BF16)
        in_ref[a, :, off : off + block] = in_acc[r].astype(BF16)

    for i in range(max(chunks - 2, 0), chunks):
        for copy in ship(i, i % 2):
            copy.wait()


def block_products(tables, place, x, back, up, down, up_parts, down_parts, row_blocks, col_count):
    n_dp = len(up_parts)
    slots, block, _ = up.shape
    arrived = up_parts[0].shape[0]
    shards_, tokens, shard = x.shape
    rows = block // n_dp
    chunk = 8
    grad = jax.ShapeDtypeStruct((2, slots, rows, block), BF16)
    vmem = pl.BlockSpec(memory_space=pltpu.VMEM)
    scratch = [
        pltpu.VMEM(x.shape, BF16),
        pltpu.VMEM(x.shape, BF16),
        pltpu.VMEM(up.shape, BF16),
        pltpu.VMEM(up.shape, BF16),
        pltpu.VMEM((n_dp, arrived, rows, block), BF16),
        pltpu.VMEM((n_dp, arrived, rows, block), BF16),
        pltpu.VMEM((row_blocks, block, tokens), BF16),
        pltpu.VMEM((col_count, tokens, block), F32),
        pltpu.VMEM((col_count, tokens, block), F32),
        pltpu.VMEM((col_count, tokens, block), BF16),
        pltpu.VMEM((col_count, block, tokens), BF16),
        pltpu.VMEM((col_count, tokens, block), BF16),
        pltpu.VMEM((row_blocks, tokens, block), F32),
        pltpu.VMEM((row_blocks, tokens, block), F32),
        pltpu.VMEM((2, 2, chunk, block, block), BF16),
        pltpu.SemaphoreType.DMA((4 + 2 * n_dp,)),
        pltpu.SemaphoreType.DMA((2, 2 * n_dp)),
    ]
    return pl.pallas_call(
        functools.partial(products_kernel, n_dp, slots, arrived, row_blocks, col_count, shard, chunk),
        out_shape=[jax.ShapeDtypeStruct(x.shape, BF16)] * 2 + [grad] * n_dp,
        grid_spec=pltpu.PrefetchScalarGridSpec(
            num_scalar_prefetch=6,
            grid=(1,),
            in_specs=[ANY] * (4 + 2 * n_dp),
            out_specs=[pl.BlockSpec(x.shape, lambda i, *_: (0, 0, 0), pipeline_mode=pl.Buffered(1))] * 2
            + [ANY] * n_dp,
            scratch_shapes=scratch,
        ),
        compiler_params=pltpu.CompilerParams(vmem_limit_bytes=VMEM_LIMIT),
        cost_estimate=pl.CostEstimate(
            flops=12 * slots * tokens * block * block,
            transcendentals=col_count * tokens * block,
            bytes_accessed=8 * slots * block * block * 2,
        ),
        name="block_products",
    )(*tables, place, x, back, up, down, *up_parts, *down_parts)


def adam_step(tables, grads, moments, arrived):
    home, came, kind = tables
    slots, rows, block = moments[0].shape
    n_grads = len(grads)

    def kernel(home_ref, came_ref, kind_ref, *refs):
        grad_refs = refs[:n_grads]
        moment_refs = refs[n_grads : n_grads + 4]
        arrived_ref = refs[n_grads + 4]
        outs = refs[n_grads + 5 :]

        def step(g, carry):
            at = came_ref[g]
            own = home_ref[g]
            kind = kind_ref[g]

            def moved(k):
                picked = lax.select(kind == 1, moment_refs[k][own], arrived_ref[at, k].astype(F32))
                return lax.select(kind == 0, jnp.zeros_like(picked), picked)

            for p in range(2):
                total = grad_refs[0][p, g].astype(F32)
                for ref in grad_refs[1:]:
                    total = total + ref[p, g].astype(F32)
                first = 0.9 * moved(2 * p) + 0.1 * total
                second = 0.95 * moved(2 * p + 1) + 0.05 * total * total
                outs[p][g] = first / (jnp.sqrt(second) + 1.0)
            return carry

        lax.fori_loop(0, slots, step, 0, unroll=2)

    vmem = pl.BlockSpec(memory_space=pltpu.VMEM)
    return pl.pallas_call(
        kernel,
        out_shape=[jax.ShapeDtypeStruct(moments[0].shape, F32)] * 2,
        grid_spec=pltpu.PrefetchScalarGridSpec(
            num_scalar_prefetch=3,
            grid=(),
            in_specs=[vmem] * (n_grads + 5),
            out_specs=[vmem] * 2,
        ),
        compiler_params=pltpu.CompilerParams(vmem_limit_bytes=VMEM_LIMIT),
        cost_estimate=pl.CostEstimate(
            flops=30 * slots * rows * block,
            transcendentals=4 * slots * rows * block,
            bytes_accessed=34 * slots * rows * block,
        ),
        name="adam_step",
    )(home, came, kind, *grads, *moments, arrived)


def shards(
    activations,
    cotangent,
    up_weight_blocks,
    down_weight_blocks,
    up_first_moment,
    up_second_moment,
    down_first_moment,
    down_second_moment,
    source,
    new_row,
    new_col,
    col_owner,
):
    tensor_size = lax.axis_size("tensor")
    n_dp = lax.axis_size("dp")
    nx = n_dp // 2
    my_index = lax.axis_index("tensor")
    my_dp = lax.axis_index("dp")
    slot_count, block, _ = up_weight_blocks.shape
    rows = block // n_dp
    bucket = (slot_count + tensor_size - 2) // tensor_size

    sources = source.reshape(tensor_size, slot_count)
    is_live = sources >= 0
    sender_dev = jnp.where(is_live, sources // slot_count, -1)
    sender_slot = jnp.where(is_live, sources % slot_count, 0)
    targets = jnp.arange(tensor_size, dtype=jnp.int32)[:, None]
    outgoing = is_live & (sender_dev == my_index) & (targets != my_index)
    out_flags = outgoing.astype(jnp.int32)
    out_rank = jnp.cumsum(out_flags, axis=1) - out_flags
    chosen = outgoing[:, :, None] & (
        out_rank[:, :, None] == jnp.arange(bucket, dtype=jnp.int32)[None, None, :]
    )
    send_slots = jnp.sum(jnp.where(chosen, sender_slot[:, :, None], 0), axis=1).reshape(-1)
    mine_dev = lax.dynamic_index_in_dim(sender_dev, my_index, 0, keepdims=False)
    mine_slot = lax.dynamic_index_in_dim(sender_slot, my_index, 0, keepdims=False)
    mine_live = mine_dev >= 0
    stays = mine_live & (mine_dev == my_index)
    positions = jnp.arange(slot_count, dtype=jnp.int32)
    earlier = (
        (mine_dev[:, None] == mine_dev[None, :])
        & mine_live[None, :]
        & (positions[None, :] < positions[:, None])
    )
    recv_rank = jnp.minimum(jnp.sum(earlier.astype(jnp.int32), axis=1), bucket - 1)
    home = jnp.where(stays, mine_slot, 0)
    came = jnp.where(mine_live & ~stays, mine_dev * bucket + recv_rank, 0)
    kind = jnp.where(stays, 1, jnp.where(mine_live, 2, 0)).astype(jnp.int32)
    col_count = col_owner.shape[0] // tensor_size
    col_slot = jnp.take(local_columns(col_owner), new_col)
    place = jnp.stack([my_dp // 2, my_dp % 2]).astype(jnp.int32)
    dp_index = my_dp.reshape(1).astype(jnp.int32)

    def exchange(packed):
        shaped = packed.reshape((tensor_size, bucket) + packed.shape[1:])
        got = lax.all_to_all(shaped, "tensor", split_axis=0, concat_axis=0, tiled=True)
        return got.reshape((tensor_size * bucket,) + packed.shape[1:])

    core_pairs = [(d, d ^ 1) for d in range(n_dp)]

    def x_pairs(j):
        return [(d, ((d // 2 + j) % nx) * 2 + d % 2) for d in range(n_dp)]

    def spread(own):
        parts = []
        for j in range(nx):
            mine = own if j == 0 else lax.ppermute(own, "dp", x_pairs(j))
            parts += [mine, lax.ppermute(mine, "dp", core_pairs)]
        return parts

    up_in = exchange(pack_weight(up_weight_blocks, send_slots, dp_index, rows))
    down_in = exchange(pack_weight(down_weight_blocks, send_slots, dp_index, rows))
    up_parts = spread(up_in)
    down_parts = spread(down_in)

    shard = activations.shape[1]
    stacked = shard % block == 0
    if stacked:
        x = lax.all_gather(activations, "tensor", axis=0, tiled=False)
        back = lax.all_gather(cotangent, "tensor", axis=0, tiled=False)
        row_blocks = tensor_size * shard // block
    else:
        x = lax.all_gather(activations, "tensor", axis=1, tiled=True)[None]
        back = lax.all_gather(cotangent, "tensor", axis=1, tiled=True)[None]
        row_blocks = x.shape[2] // block

    moments = (up_first_moment, up_second_moment, down_first_moment, down_second_moment)
    moments_in = exchange(pack_moments(moments, send_slots))

    got = block_products(
        (new_row, col_slot, home, came, kind),
        place,
        x,
        back,
        up_weight_blocks,
        down_weight_blocks,
        up_parts,
        down_parts,
        row_blocks,
        col_count,
    )
    out_part, in_part = got[:2]
    if stacked:
        out_sum = lax.psum_scatter(out_part, "tensor", scatter_dimension=0, tiled=False)
        in_sum = lax.psum_scatter(in_part, "tensor", scatter_dimension=0, tiled=False)
    else:
        out_sum = lax.psum_scatter(out_part[0], "tensor", scatter_dimension=1, tiled=True)
        in_sum = lax.psum_scatter(in_part[0], "tensor", scatter_dimension=1, tiled=True)

    grads = got[2:]
    terms = [grads[0], lax.ppermute(grads[1], "dp", core_pairs)]
    for j in range(1, nx):
        there = lax.ppermute(grads[2 * j + 1], "dp", core_pairs)
        both = (grads[2 * j].astype(F32) + there.astype(F32)).astype(BF16)
        terms.append(lax.ppermute(both, "dp", x_pairs(j)))

    up_step, down_step = adam_step((home, came, kind), terms, moments, moments_in)
    return (out_sum, in_sum, up_step, down_step)


def solution(mesh):
    placed = (
        P("dp", "tensor"),
        P("dp", "tensor"),
        P("tensor", None, None),
        P("tensor", None, None),
        P("tensor", "dp", None),
        P("tensor", "dp", None),
        P("tensor", "dp", None),
        P("tensor", "dp", None),
        P(),
        P("tensor"),
        P("tensor"),
        P(),
    )
    return jax.shard_map(
        shards,
        mesh=mesh,
        in_specs=placed,
        out_specs=(
            P("dp", "tensor"),
            P("dp", "tensor"),
            P("tensor", "dp", None),
            P("tensor", "dp", None),
        ),
        check_vma=False,
    )
```

```python
import functools
import math

import jax
import jax.numpy as jnp
from jax import lax
from jax.experimental import pallas as pl
from jax.experimental.pallas import tpu as pltpu
from jax.sharding import PartitionSpec as P


gelu_scale = math.sqrt(2.0 / math.pi)
VMEM_LIMIT = 60 * 1024 * 1024

F32 = jnp.float32
BF16 = jnp.bfloat16
ANY = pl.BlockSpec(memory_space=pl.ANY)


def gelu_pair(pre_act):
    inner = gelu_scale * (pre_act + 0.044715 * pre_act * pre_act * pre_act)
    tangent = jnp.tanh(inner)
    gelu_value = 0.5 * pre_act * (1.0 + tangent)
    gelu_slope = 0.5 * (1.0 + tangent) + 0.5 * pre_act * (1.0 - tangent * tangent) * gelu_scale * (
        1.0 + 3.0 * 0.044715 * pre_act * pre_act
    )
    return (gelu_value, gelu_slope)


def local_columns(col_owner):
    count_all = col_owner.shape[0]
    order = jnp.arange(count_all, dtype=jnp.int32)
    same = (col_owner[None, :] == col_owner[:, None]) & (order[None, :] < order[:, None])
    return jnp.sum(same.astype(jnp.int32), axis=1)


def pack_weight(tiles, send_slots, dp_index, rows):
    slots, _, width = tiles.shape
    count = send_slots.shape[0]

    def kernel(send_ref, dp_ref, in_ref, out_ref):
        def step(i, carry):
            out_ref[i] = in_ref[send_ref[i]]
            return carry

        lax.fori_loop(0, count, step, 0, unroll=8)

    return pl.pallas_call(
        kernel,
        out_shape=jax.ShapeDtypeStruct((count, rows, width), tiles.dtype),
        grid_spec=pltpu.PrefetchScalarGridSpec(
            num_scalar_prefetch=2,
            grid=(1,),
            in_specs=[pl.BlockSpec((slots, rows, width), lambda i, s, d: (0, d[0], 0))],
            out_specs=pl.BlockSpec((count, rows, width), lambda i, s, d: (0, 0, 0)),
        ),
        compiler_params=pltpu.CompilerParams(vmem_limit_bytes=VMEM_LIMIT),
        cost_estimate=pl.CostEstimate(flops=0, transcendentals=0, bytes_accessed=4 * count * rows * width),
        name="pack_weight",
    )(send_slots, dp_index, tiles)


def pack_moments(arrays, send_slots):
    slots, rows, width = arrays[0].shape
    count = send_slots.shape[0]
    kinds = len(arrays)

    def kernel(send_ref, *refs):
        out_ref = refs[-1]

        def step(i, carry):
            s = send_ref[i]
            for k in range(kinds):
                out_ref[i, k] = refs[k][s].astype(BF16)
            return carry

        lax.fori_loop(0, count, step, 0, unroll=4)

    whole = pl.BlockSpec((slots, rows, width), lambda i, s: (0, 0, 0))
    return pl.pallas_call(
        kernel,
        out_shape=jax.ShapeDtypeStruct((count, kinds, rows, width), BF16),
        grid_spec=pltpu.PrefetchScalarGridSpec(
            num_scalar_prefetch=1,
            grid=(1,),
            in_specs=[whole] * kinds,
            out_specs=pl.BlockSpec((count, kinds, rows, width), lambda i, s: (0, 0, 0, 0)),
        ),
        compiler_params=pltpu.CompilerParams(vmem_limit_bytes=VMEM_LIMIT),
        cost_estimate=pl.CostEstimate(
            flops=0, transcendentals=0, bytes_accessed=6 * kinds * count * rows * width
        ),
        name="pack_moments",
    )(send_slots, *arrays)


def columns(ref, r, block):
    per = ref.shape[2] // block
    a = lax.div(r, per)
    off = pl.multiple_of((r - a * per) * block, block)
    return ref[a, :, pl.ds(off, block)]


def weight(own, came, home_ref, came_ref, kind_ref, g):
    kind = kind_ref[g]
    mine = own[home_ref[g]]
    at = came_ref[g]
    theirs = jnp.concatenate([came[q, at] for q in range(came.shape[0])], axis=0)
    picked = lax.select(kind == 1, mine, theirs)
    return lax.select(kind == 0, jnp.zeros_like(picked), picked)


def feature_copies(parts, which, place_ref, buf, sem):
    copies = []
    for m, part in enumerate(parts):
        at = (place_ref[2] ^ m) if len(parts) > 1 else 0
        copies.append(pltpu.make_async_copy(part.at[which], buf.at[at], sem.at[m]))
    return copies


def weight_copies(own, own_v, parts, parts_v, place_ref, sem):
    n_dp = len(parts)
    nx = n_dp // 2
    copies = [pltpu.make_async_copy(own, own_v, sem.at[0])]
    for j in range(nx):
        for other in range(2):
            k = 2 * j + other
            owner = lax.rem(place_ref[0] + nx - j, nx) * 2 + (place_ref[1] + other) % 2
            copies.append(pltpu.make_async_copy(parts[k], parts_v.at[owner], sem.at[1 + k]))
    return copies


def forward_kernel(n_feat, n_dp, row_blocks, *refs):
    row_ref, col_ref, home_ref, came_ref, kind_ref, place_ref = refs[:6]
    feats = refs[6 : 6 + n_feat]
    up_hbm = refs[6 + n_feat]
    parts = refs[7 + n_feat : 7 + n_feat + n_dp]
    pre, x_t, wu_hbm, x_v, up_v, up_a, wu, feat_sem, in_sem, out_sem = refs[7 + n_feat + n_dp :]
    slots, block, _ = up_v.shape
    copies = feature_copies(feats, 0, place_ref, x_v, feat_sem)
    copies += weight_copies(up_hbm, up_v, parts, up_a, place_ref, in_sem)
    for copy in copies:
        copy.start()
    pre[...] = jnp.zeros(pre.shape, F32)
    for copy in copies:
        copy.wait()
    unroll = 4

    def step(i, carry):
        got = []
        for u in range(unroll):
            g = i * unroll + u
            w = weight(up_v, up_a, home_ref, came_ref, kind_ref, g)
            wu[g] = w
            got.append(jnp.dot(columns(x_v, row_ref[g], block), w, preferred_element_type=F32))
        for u in range(unroll):
            c = col_ref[i * unroll + u]
            pre[c] = pre[c] + got[u]
        return carry

    lax.fori_loop(0, slots // unroll, step, 0)
    keep = pltpu.make_async_copy(wu, wu_hbm, out_sem)
    keep.start()

    def turn(r, carry):
        x_t[r] = columns(x_v, r, block).T
        return carry

    lax.fori_loop(0, row_blocks, turn, 0)
    keep.wait()


def gradient_kernel(n_feat, n_dp, *refs):
    row_ref, col_ref, home_ref, came_ref, kind_ref, place_ref = refs[:6]
    feats = refs[6 : 6 + n_feat]
    down_hbm = refs[6 + n_feat]
    parts = refs[7 + n_feat : 7 + n_feat + n_dp]
    pre, x_t = refs[7 + n_feat + n_dp : 9 + n_feat + n_dp]
    outs = refs[9 + n_feat + n_dp :]
    act, bpre, wd_hbm = outs[:3]
    grad_refs = outs[3 : 3 + n_dp]
    back_v, down_v, down_a, wd, back, act_t, stage, feat_sem, in_sem, keep_sem, out_sem = outs[3 + n_dp :]
    slots, block, _ = down_v.shape
    rows = block // n_dp
    nx = n_dp // 2
    chunk = stage.shape[2]
    copies = feature_copies(feats, 1, place_ref, back_v, feat_sem)
    copies += weight_copies(down_hbm, down_v, parts, down_a, place_ref, in_sem)
    for copy in copies:
        copy.start()
    back[...] = jnp.zeros(back.shape, F32)
    for copy in copies:
        copy.wait()
    unroll = 4

    def backward(i, carry):
        got = []
        for u in range(unroll):
            g = i * unroll + u
            w = weight(down_v, down_a, home_ref, came_ref, kind_ref, g)
            wd[g] = w
            got.append(
                lax.dot_general(
                    columns(back_v, row_ref[g], block), w, (((1,), (1,)), ((), ())), preferred_element_type=F32
                )
            )
        for u in range(unroll):
            c = col_ref[i * unroll + u]
            back[c] = back[c] + got[u]
        return carry

    lax.fori_loop(0, slots // unroll, backward, 0)
    keep = pltpu.make_async_copy(wd, wd_hbm, keep_sem)
    keep.start()

    def bend(c, carry):
        value, slope = gelu_pair(pre[c])
        narrow = value.astype(BF16)
        act[c] = narrow
        act_t[c] = narrow.T
        bpre[c] = (back[c] * slope).astype(BF16)
        return carry

    lax.fori_loop(0, pre.shape[0], bend, 0)

    def ship(i, slot):
        out = []
        for j in range(nx):
            for other in range(2):
                owner = lax.rem(place_ref[0] + j, nx) * 2 + (place_ref[1] + other) % 2
                start = pl.multiple_of(owner * rows, rows)
                for p in range(2):
                    out.append(
                        pltpu.make_async_copy(
                            stage.at[slot, p, :, pl.ds(start, rows), :],
                            grad_refs[2 * j + other].at[p, pl.ds(i * chunk, chunk)],
                            out_sem.at[slot, 2 * (2 * j + other) + p],
                        )
                    )
        return out

    def last(i, carry):
        slot = lax.rem(i, 2)

        @pl.when(i >= 2)
        def _():
            for copy in ship(i - 2, slot):
                copy.wait()

        for u in range(chunk):
            g = i * chunk + u
            r = row_ref[g]
            c = col_ref[g]
            stage[slot, 0, u] = jnp.dot(x_t[r], bpre[c], preferred_element_type=F32).astype(BF16)
            stage[slot, 1, u] = jnp.dot(
                act_t[c], columns(back_v, r, block), preferred_element_type=F32
            ).astype(BF16)
        for copy in ship(i, slot):
            copy.start()
        return carry

    chunks = slots // chunk
    lax.fori_loop(0, chunks, last, 0)
    for i in range(max(chunks - 2, 0), chunks):
        for copy in ship(i, i % 2):
            copy.wait()
    keep.wait()


def output_kernel(pieces, *refs):
    row_ref, col_ref, place_ref = refs[:3]
    wu_hbm, wd_hbm, act, bpre = refs[3:7]
    outs = refs[7 : 7 + len(pieces)]
    wu, wd, out_acc, in_acc, staged, in_sem, out_sem = refs[7 + len(pieces) :]
    slots, block, _ = wu.shape
    parts = 4
    some = slots // parts
    loads = []
    for k in range(parts):
        for hbm, buf, s in ((wd_hbm, wd, 0), (wu_hbm, wu, 1)):
            at = pl.ds(k * some, some)
            loads.append(pltpu.make_async_copy(hbm.at[at], buf.at[at], in_sem.at[2 * k + s]))
    for copy in loads:
        copy.start()
    out_acc[...] = jnp.zeros(out_acc.shape, F32)
    in_acc[...] = jnp.zeros(in_acc.shape, F32)
    unroll = 2

    def step(i, carry):
        got = []
        for u in range(unroll):
            g = i * unroll + u
            r = row_ref[g]
            c = col_ref[g]
            got.append(
                (
                    r,
                    jnp.dot(act[c], wd[g], preferred_element_type=F32),
                    lax.dot_general(bpre[c], wu[g], (((1,), (1,)), ((), ())), preferred_element_type=F32),
                )
            )
        for r, o, n in got:
            out_acc[r] = out_acc[r] + o
            in_acc[r] = in_acc[r] + n
        return carry

    for k in range(parts):
        loads[2 * k].wait()
        loads[2 * k + 1].wait()
        lax.fori_loop(k * some // unroll, (k + 1) * some // unroll, step, 0)

    count = staged.shape[0]
    per = staged.shape[3] // block
    bits = count.bit_length() - 1
    for a in range(count):
        if count == 1:
            at = 0
        else:
            far = place_ref[2] ^ a
            at = 0
            for b in range(bits):
                at = at + ((far >> b) & 1) * (count >> (b + 1))
        for q in range(per):
            staged[at, 0, :, q * block : (q + 1) * block] = out_acc[a * per + q].astype(BF16)
            staged[at, 1, :, q * block : (q + 1) * block] = in_acc[a * per + q].astype(BF16)
    copies = [
        pltpu.make_async_copy(staged.at[pl.ds(start, size)], out, out_sem.at[k])
        for k, ((start, size), out) in enumerate(zip(pieces, outs))
    ]
    for copy in copies:
        copy.start()
    for copy in copies:
        copy.wait()


VMEM = pl.BlockSpec(memory_space=pltpu.VMEM)
SMEM = pl.BlockSpec(memory_space=pltpu.SMEM)


def cost(flops, size):
    return pl.CostEstimate(flops=flops, transcendentals=0, bytes_accessed=size)


def forward_products(tables, place, feats, up, parts, col_count, row_blocks, feat_shape):
    slots, block, _ = up.shape
    n_dp, n_feat = len(parts), len(feats)
    tokens = feat_shape[1]
    return pl.pallas_call(
        functools.partial(forward_kernel, n_feat, n_dp, row_blocks),
        out_shape=[
            jax.ShapeDtypeStruct((col_count, tokens, block), F32),
            jax.ShapeDtypeStruct((row_blocks, block, tokens), BF16),
            jax.ShapeDtypeStruct(up.shape, BF16),
        ],
        in_specs=[SMEM] * 6 + [ANY] * (n_feat + 1 + n_dp),
        out_specs=[VMEM, VMEM, ANY],
        scratch_shapes=[
            pltpu.VMEM(feat_shape, BF16),
            pltpu.VMEM(up.shape, BF16),
            pltpu.VMEM((n_dp,) + parts[0].shape, BF16),
            pltpu.VMEM(up.shape, BF16),
            pltpu.SemaphoreType.DMA((n_feat,)),
            pltpu.SemaphoreType.DMA((1 + n_dp,)),
            pltpu.SemaphoreType.DMA,
        ],
        compiler_params=pltpu.CompilerParams(vmem_limit_bytes=VMEM_LIMIT),
        cost_estimate=cost(2 * slots * tokens * block * block, 12 * slots * block * block),
        name="forward_products",
    )(*tables, place, *feats, up, *parts)


def gradient_products(tables, place, feats, down, parts, pre, x_t, feat_shape):
    slots, block, _ = down.shape
    n_dp, n_feat = len(parts), len(feats)
    rows = block // n_dp
    chunk = 8
    col_count, tokens, _ = pre.shape
    grad = jax.ShapeDtypeStruct((2, slots, rows, block), BF16)
    return pl.pallas_call(
        functools.partial(gradient_kernel, n_feat, n_dp),
        out_shape=[jax.ShapeDtypeStruct(pre.shape, BF16)] * 2
        + [jax.ShapeDtypeStruct(down.shape, BF16)]
        + [grad] * n_dp,
        in_specs=[SMEM] * 6 + [ANY] * (n_feat + 1 + n_dp) + [VMEM] * 2,
        out_specs=[VMEM, VMEM] + [ANY] * (1 + n_dp),
        scratch_shapes=[
            pltpu.VMEM(feat_shape, BF16),
            pltpu.VMEM(down.shape, BF16),
            pltpu.VMEM((n_dp,) + parts[0].shape, BF16),
            pltpu.VMEM(down.shape, BF16),
            pltpu.VMEM(pre.shape, F32),
            pltpu.VMEM((col_count, block, tokens), BF16),
            pltpu.VMEM((2, 2, chunk, block, block), BF16),
            pltpu.SemaphoreType.DMA((n_feat,)),
            pltpu.SemaphoreType.DMA((1 + n_dp,)),
            pltpu.SemaphoreType.DMA,
            pltpu.SemaphoreType.DMA((2, 2 * n_dp)),
        ],
        compiler_params=pltpu.CompilerParams(vmem_limit_bytes=VMEM_LIMIT),
        cost_estimate=cost(6 * slots * tokens * block * block, 20 * slots * block * block),
        name="gradient_products",
    )(*tables, place, *feats, down, *parts, pre, x_t)


def output_products(row, col, place, wu, wd, act, bpre, pieces, feat_shape, row_blocks):
    slots, block, _ = wu.shape
    count, tokens, shard = feat_shape
    return pl.pallas_call(
        functools.partial(output_kernel, pieces),
        out_shape=[jax.ShapeDtypeStruct((size, 2, tokens, shard), BF16) for _, size in pieces],
        in_specs=[SMEM] * 3 + [ANY] * 2 + [VMEM] * 2,
        out_specs=[ANY] * len(pieces),
        scratch_shapes=[
            pltpu.VMEM(wu.shape, BF16),
            pltpu.VMEM(wd.shape, BF16),
            pltpu.VMEM((row_blocks, tokens, block), F32),
            pltpu.VMEM((row_blocks, tokens, block), F32),
            pltpu.VMEM((count, 2, tokens, shard), BF16),
            pltpu.SemaphoreType.DMA((8,)),
            pltpu.SemaphoreType.DMA((len(pieces),)),
        ],
        compiler_params=pltpu.CompilerParams(vmem_limit_bytes=VMEM_LIMIT),
        cost_estimate=cost(4 * slots * tokens * block * block, 8 * slots * block * block),
        name="output_products",
    )(row, col, place, wu, wd, act, bpre)


def adam_step(tables, grads, which, moments, arrived):
    slots, rows, block = moments[0].shape
    n_grads = len(grads)

    def kernel(home_ref, came_ref, kind_ref, *refs):
        grad_refs = refs[:n_grads]
        moment_refs = refs[n_grads : n_grads + 2]
        arrived_ref = refs[n_grads + 2]
        out = refs[n_grads + 3]

        def step(g, carry):
            at = came_ref[g]
            own = home_ref[g]
            kind = kind_ref[g]

            def moved(k):
                picked = lax.select(kind == 1, moment_refs[k][own], arrived_ref[at, k].astype(F32))
                return lax.select(kind == 0, jnp.zeros_like(picked), picked)

            total = grad_refs[0][0, g].astype(F32)
            for ref in grad_refs[1:]:
                total = total + ref[0, g].astype(F32)
            first = 0.9 * moved(0) + 0.1 * total
            second = 0.95 * moved(1) + 0.05 * total * total
            out[g] = first / (jnp.sqrt(second) + 1.0)
            return carry

        lax.fori_loop(0, slots, step, 0, unroll=4)

    half = pl.BlockSpec((1, slots, rows, block), lambda i: (which, 0, 0, 0))

    def whole(array):
        return pl.BlockSpec(array.shape, lambda i: (0,) * array.ndim)

    return pl.pallas_call(
        kernel,
        out_shape=jax.ShapeDtypeStruct(moments[0].shape, F32),
        grid=(1,),
        in_specs=[SMEM] * 3 + [half] * n_grads + [whole(m) for m in moments] + [whole(arrived)],
        out_specs=whole(moments[0]),
        compiler_params=pltpu.CompilerParams(vmem_limit_bytes=VMEM_LIMIT),
        cost_estimate=cost(15 * slots * rows * block, 17 * slots * rows * block),
        name="adam_step",
    )(*tables, *grads, *moments, arrived)


def layer(
    activations,
    cotangent,
    up_weight_blocks,
    down_weight_blocks,
    up_first_moment,
    up_second_moment,
    down_first_moment,
    down_second_moment,
    source,
    new_row,
    new_col,
    col_owner,
):
    tensor_size = lax.axis_size("tensor")
    n_dp = lax.axis_size("dp")
    nx = n_dp // 2
    my_index = lax.axis_index("tensor")
    my_dp = lax.axis_index("dp")
    slot_count, block, _ = up_weight_blocks.shape
    rows = block // n_dp
    bucket = (slot_count + tensor_size - 2) // tensor_size

    sources = source.reshape(tensor_size, slot_count)
    is_live = sources >= 0
    sender_dev = jnp.where(is_live, sources // slot_count, -1)
    sender_slot = jnp.where(is_live, sources % slot_count, 0)
    targets = jnp.arange(tensor_size, dtype=jnp.int32)[:, None]
    outgoing = is_live & (sender_dev == my_index) & (targets != my_index)
    out_flags = outgoing.astype(jnp.int32)
    out_rank = jnp.cumsum(out_flags, axis=1) - out_flags
    chosen = outgoing[:, :, None] & (
        out_rank[:, :, None] == jnp.arange(bucket, dtype=jnp.int32)[None, None, :]
    )
    send_slots = jnp.sum(jnp.where(chosen, sender_slot[:, :, None], 0), axis=1).reshape(-1)
    mine_dev = lax.dynamic_index_in_dim(sender_dev, my_index, 0, keepdims=False)
    mine_slot = lax.dynamic_index_in_dim(sender_slot, my_index, 0, keepdims=False)
    mine_live = mine_dev >= 0
    stays = mine_live & (mine_dev == my_index)
    positions = jnp.arange(slot_count, dtype=jnp.int32)
    earlier = (
        (mine_dev[:, None] == mine_dev[None, :])
        & mine_live[None, :]
        & (positions[None, :] < positions[:, None])
    )
    recv_rank = jnp.minimum(jnp.sum(earlier.astype(jnp.int32), axis=1), bucket - 1)
    home = jnp.where(stays, mine_slot, 0)
    came = jnp.where(mine_live & ~stays, mine_dev * bucket + recv_rank, 0)
    kind = jnp.where(stays, 1, jnp.where(mine_live, 2, 0)).astype(jnp.int32)
    col_count = col_owner.shape[0] // tensor_size
    col_slot = jnp.take(local_columns(col_owner), new_col)
    place = jnp.stack([my_dp // 2, my_dp % 2, my_index]).astype(jnp.int32)
    dp_index = my_dp.reshape(1).astype(jnp.int32)
    tables = (new_row, col_slot, home, came, kind)

    def exchange(packed):
        shaped = packed.reshape((tensor_size, bucket) + packed.shape[1:])
        got = lax.all_to_all(shaped, "tensor", split_axis=0, concat_axis=0, tiled=True)
        return got.reshape((tensor_size * bucket,) + packed.shape[1:])

    core_pairs = [(d, d ^ 1) for d in range(n_dp)]

    def x_pairs(j):
        return [(d, ((d // 2 + j) % nx) * 2 + d % 2) for d in range(n_dp)]

    def far_pairs(bit):
        return [(t, t ^ bit) for t in range(tensor_size)]

    def spread(own):
        parts = []
        for j in range(nx):
            mine = own
            if j:
                mine = lax.ppermute(own, "dp", x_pairs(j))
            parts += [mine, lax.ppermute(mine, "dp", core_pairs)]
        return parts

    up_pack = pack_weight(up_weight_blocks, send_slots, dp_index, rows)
    down_pack = pack_weight(down_weight_blocks, send_slots, dp_index, rows)
    up_in = exchange(up_pack)
    down_in = exchange(down_pack)
    up_parts = spread(up_in)
    down_parts = spread(down_in)

    shard = activations.shape[1]
    stacked = shard % block == 0 and tensor_size & (tensor_size - 1) == 0
    if stacked:
        bits = [1 << k for k in reversed(range(tensor_size.bit_length() - 1))]
        held = {0: jnp.stack([activations, cotangent])}
        for bit in bits:
            for m in list(held):
                held[m ^ bit] = lax.ppermute(held[m], "tensor", far_pairs(bit))
        feats = [held[m] for m in range(tensor_size)]
        feat_shape = (tensor_size,) + activations.shape
    else:
        x = lax.all_gather(activations, "tensor", axis=1, tiled=True)
        back = lax.all_gather(cotangent, "tensor", axis=1, tiled=True)
        feats = [jnp.stack([x, back])[:, None].reshape((2,) + x.shape)]
        feat_shape = (1,) + x.shape
    row_blocks = feat_shape[0] * feat_shape[2] // block

    ups = (up_first_moment, up_second_moment)
    downs = (down_first_moment, down_second_moment)
    ups_pack = pack_moments(ups, send_slots)
    downs_pack = pack_moments(downs, send_slots)
    ups_in = exchange(ups_pack)
    downs_in = exchange(downs_pack)

    pre, x_t, wu = forward_products(
        tables, place, feats, up_weight_blocks, up_parts, col_count, row_blocks, feat_shape
    )
    act, bpre, wd, *grads = gradient_products(
        tables, place, feats, down_weight_blocks, down_parts, pre, x_t, feat_shape
    )
    terms = []
    for j in range(nx):
        there = lax.ppermute(grads[2 * j + 1], "dp", core_pairs)
        if j == 0:
            terms += [grads[0], there]
        else:
            both = (grads[2 * j].astype(F32) + there.astype(F32)).astype(BF16)
            terms.append(lax.ppermute(both, "dp", x_pairs(j)))

    if stacked:
        half = tensor_size // 2
        keep, send = output_products(
            new_row, col_slot, place, wu, wd, act, bpre, ((0, half), (half, half)), feat_shape, row_blocks
        )
        sums = [keep]
        bit = 1
        while True:
            sums.append(lax.ppermute(send, "tensor", far_pairs(bit)))
            bit *= 2
            if bit >= tensor_size:
                break
            half = sums[-1].shape[0] // 2
            total = sum(s[half : 2 * half].astype(F32) for s in sums)
            send = total.astype(BF16)
            sums = [s[:half] for s in sums]
        total = sum(s[0].astype(F32) for s in sums).astype(BF16)
        out_sum, in_sum = total[0], total[1]
    else:
        (whole,) = output_products(
            new_row, col_slot, place, wu, wd, act, bpre, ((0, 1),), feat_shape, row_blocks
        )
        out_sum = lax.psum_scatter(whole[0, 0], "tensor", scatter_dimension=1, tiled=True)
        in_sum = lax.psum_scatter(whole[0, 1], "tensor", scatter_dimension=1, tiled=True)

    up_step = adam_step((home, came, kind), terms, 0, ups, ups_in)
    down_step = adam_step((home, came, kind), terms, 1, downs, downs_in)
    return (out_sum, in_sum, up_step, down_step)


def solution(mesh):
    placed = (
        P("dp", "tensor"),
        P("dp", "tensor"),
        P("tensor", None, None),
        P("tensor", None, None),
        P("tensor", "dp", None),
        P("tensor", "dp", None),
        P("tensor", "dp", None),
        P("tensor", "dp", None),
        P(),
        P("tensor"),
        P("tensor"),
        P(),
    )
    return jax.shard_map(
        layer,
        mesh=mesh,
        in_specs=placed,
        out_specs=(
            P("dp", "tensor"),
            P("dp", "tensor"),
            P("tensor", "dp", None),
            P("tensor", "dp", None),
        ),
        check_vma=False,
    )
```

```python
import functools
import math

import jax
import jax.numpy as jnp
from jax import lax
from jax.experimental import pallas as pl
from jax.experimental.pallas import tpu as pltpu
from jax.sharding import PartitionSpec as P


gelu_scale = math.sqrt(2.0 / math.pi)
VMEM_LIMIT = 60 * 1024 * 1024

F32 = jnp.float32
BF16 = jnp.bfloat16
ANY = pl.BlockSpec(memory_space=pl.ANY)


def gelu_pair(pre_act):
    inner = gelu_scale * (pre_act + 0.044715 * pre_act * pre_act * pre_act)
    tangent = jnp.tanh(inner)
    gelu_value = 0.5 * pre_act * (1.0 + tangent)
    gelu_slope = 0.5 * (1.0 + tangent) + 0.5 * pre_act * (1.0 - tangent * tangent) * gelu_scale * (
        1.0 + 3.0 * 0.044715 * pre_act * pre_act
    )
    return (gelu_value, gelu_slope)


def local_columns(col_owner):
    count_all = col_owner.shape[0]
    order = jnp.arange(count_all, dtype=jnp.int32)
    same = (col_owner[None, :] == col_owner[:, None]) & (order[None, :] < order[:, None])
    return jnp.sum(same.astype(jnp.int32), axis=1)


def pack_weight(tiles, send_slots, dp_index, rows):
    slots, _, width = tiles.shape
    count = send_slots.shape[0]

    def kernel(send_ref, dp_ref, in_ref, out_ref):
        def step(i, carry):
            out_ref[i] = in_ref[send_ref[i]]
            return carry

        lax.fori_loop(0, count, step, 0, unroll=8)

    return pl.pallas_call(
        kernel,
        out_shape=jax.ShapeDtypeStruct((count, rows, width), tiles.dtype),
        grid_spec=pltpu.PrefetchScalarGridSpec(
            num_scalar_prefetch=2,
            grid=(1,),
            in_specs=[pl.BlockSpec((slots, rows, width), lambda i, s, d: (0, d[0], 0))],
            out_specs=pl.BlockSpec((count, rows, width), lambda i, s, d: (0, 0, 0)),
        ),
        compiler_params=pltpu.CompilerParams(vmem_limit_bytes=VMEM_LIMIT),
        cost_estimate=pl.CostEstimate(flops=0, transcendentals=0, bytes_accessed=4 * count * rows * width),
        name="pack_weight",
    )(send_slots, dp_index, tiles)


def pack_moments(arrays, send_slots):
    slots, rows, width = arrays[0].shape
    count = send_slots.shape[0]
    kinds = len(arrays)

    def kernel(send_ref, *refs):
        out_ref = refs[-1]

        def step(i, carry):
            s = send_ref[i]
            for k in range(kinds):
                out_ref[i, k] = refs[k][s].astype(BF16)
            return carry

        lax.fori_loop(0, count, step, 0, unroll=4)

    whole = pl.BlockSpec((slots, rows, width), lambda i, s: (0, 0, 0))
    return pl.pallas_call(
        kernel,
        out_shape=jax.ShapeDtypeStruct((count, kinds, rows, width), BF16),
        grid_spec=pltpu.PrefetchScalarGridSpec(
            num_scalar_prefetch=1,
            grid=(1,),
            in_specs=[whole] * kinds,
            out_specs=pl.BlockSpec((count, kinds, rows, width), lambda i, s: (0, 0, 0, 0)),
        ),
        compiler_params=pltpu.CompilerParams(vmem_limit_bytes=VMEM_LIMIT),
        cost_estimate=pl.CostEstimate(
            flops=0, transcendentals=0, bytes_accessed=6 * kinds * count * rows * width
        ),
        name="pack_moments",
    )(send_slots, *arrays)


def columns(ref, r, block):
    per = ref.shape[2] // block
    a = lax.div(r, per)
    off = pl.multiple_of((r - a * per) * block, block)
    return ref[a, :, pl.ds(off, block)]


def weight(own, came, home_ref, came_ref, kind_ref, g):
    kind = kind_ref[g]
    mine = own[home_ref[g]]
    at = came_ref[g]
    theirs = jnp.concatenate([came[q, at] for q in range(came.shape[0])], axis=0)
    picked = lax.select(kind == 1, mine, theirs)
    return lax.select(kind == 0, jnp.zeros_like(picked), picked)


def feature_copies(parts, which, place_ref, buf, sem):
    copies = []
    for m, part in enumerate(parts):
        at = (place_ref[2] ^ m) if len(parts) > 1 else 0
        copies.append(pltpu.make_async_copy(part.at[which], buf.at[at], sem.at[m]))
    return copies


def weight_copies(own, own_v, parts, parts_v, place_ref, sem):
    n_dp = len(parts)
    nx = n_dp // 2
    copies = [pltpu.make_async_copy(own, own_v, sem.at[0])]
    for j in range(nx):
        for other in range(2):
            k = 2 * j + other
            owner = lax.rem(place_ref[0] + nx - j, nx) * 2 + (place_ref[1] + other) % 2
            copies.append(pltpu.make_async_copy(parts[k], parts_v.at[owner], sem.at[1 + k]))
    return copies


def forward_kernel(n_feat, n_dp, row_blocks, *refs):
    row_ref, col_ref, home_ref, came_ref, kind_ref, place_ref = refs[:6]
    feats = refs[6 : 6 + n_feat]
    up_hbm = refs[6 + n_feat]
    parts = refs[7 + n_feat : 7 + n_feat + n_dp]
    pre, x_t, wu_hbm, x_v, up_v, up_a, wu, feat_sem, in_sem, out_sem = refs[7 + n_feat + n_dp :]
    slots, block, _ = up_v.shape
    copies = feature_copies(feats, 0, place_ref, x_v, feat_sem)
    copies += weight_copies(up_hbm, up_v, parts, up_a, place_ref, in_sem)
    for copy in copies:
        copy.start()
    pre[...] = jnp.zeros(pre.shape, F32)
    for copy in copies:
        copy.wait()
    unroll = 4

    def step(i, carry):
        got = []
        for u in range(unroll):
            g = i * unroll + u
            w = weight(up_v, up_a, home_ref, came_ref, kind_ref, g)
            wu[g] = w
            got.append(jnp.dot(columns(x_v, row_ref[g], block), w, preferred_element_type=F32))
        for u in range(unroll):
            c = col_ref[i * unroll + u]
            pre[c] = pre[c] + got[u]
        return carry

    lax.fori_loop(0, slots // unroll, step, 0)
    keep = pltpu.make_async_copy(wu, wu_hbm, out_sem)
    keep.start()

    def turn(r, carry):
        x_t[r] = columns(x_v, r, block).T
        return carry

    lax.fori_loop(0, row_blocks, turn, 0)
    keep.wait()


def gradient_kernel(n_feat, n_dp, *refs):
    row_ref, col_ref, home_ref, came_ref, kind_ref, place_ref = refs[:6]
    feats = refs[6 : 6 + n_feat]
    down_hbm = refs[6 + n_feat]
    parts = refs[7 + n_feat : 7 + n_feat + n_dp]
    pre, x_t = refs[7 + n_feat + n_dp : 9 + n_feat + n_dp]
    outs = refs[9 + n_feat + n_dp :]
    act, bpre, wd_hbm = outs[:3]
    grad_refs = outs[3 : 3 + n_dp]
    back_v, down_v, down_a, wd, back, act_t, stage, feat_sem, in_sem, keep_sem, out_sem = outs[3 + n_dp :]
    slots, block, _ = down_v.shape
    rows = block // n_dp
    nx = n_dp // 2
    chunk = stage.shape[2]
    copies = feature_copies(feats, 1, place_ref, back_v, feat_sem)
    copies += weight_copies(down_hbm, down_v, parts, down_a, place_ref, in_sem)
    for copy in copies:
        copy.start()
    back[...] = jnp.zeros(back.shape, F32)
    for copy in copies:
        copy.wait()
    unroll = 4

    def backward(i, carry):
        got = []
        for u in range(unroll):
            g = i * unroll + u
            w = weight(down_v, down_a, home_ref, came_ref, kind_ref, g)
            wd[g] = w
            got.append(
                lax.dot_general(
                    columns(back_v, row_ref[g], block), w, (((1,), (1,)), ((), ())), preferred_element_type=F32
                )
            )
        for u in range(unroll):
            c = col_ref[i * unroll + u]
            back[c] = back[c] + got[u]
        return carry

    lax.fori_loop(0, slots // unroll, backward, 0)
    keep = pltpu.make_async_copy(wd, wd_hbm, keep_sem)
    keep.start()

    def bend(c, carry):
        value, slope = gelu_pair(pre[c])
        narrow = value.astype(BF16)
        act[c] = narrow
        act_t[c] = narrow.T
        bpre[c] = (back[c] * slope).astype(BF16)
        return carry

    lax.fori_loop(0, pre.shape[0], bend, 0)

    def ship(i, slot):
        out = []
        for j in range(nx):
            for other in range(2):
                owner = lax.rem(place_ref[0] + j, nx) * 2 + (place_ref[1] + other) % 2
                start = pl.multiple_of(owner * rows, rows)
                for p in range(2):
                    out.append(
                        pltpu.make_async_copy(
                            stage.at[slot, p, :, pl.ds(start, rows), :],
                            grad_refs[2 * j + other].at[p, pl.ds(i * chunk, chunk)],
                            out_sem.at[slot, 2 * (2 * j + other) + p],
                        )
                    )
        return out

    def last(i, carry):
        slot = lax.rem(i, 2)

        @pl.when(i >= 2)
        def _():
            for copy in ship(i - 2, slot):
                copy.wait()

        for u in range(chunk):
            g = i * chunk + u
            r = row_ref[g]
            c = col_ref[g]
            stage[slot, 0, u] = jnp.dot(x_t[r], bpre[c], preferred_element_type=F32).astype(BF16)
            stage[slot, 1, u] = jnp.dot(
                act_t[c], columns(back_v, r, block), preferred_element_type=F32
            ).astype(BF16)
        for copy in ship(i, slot):
            copy.start()
        return carry

    chunks = slots // chunk
    lax.fori_loop(0, chunks, last, 0)
    for i in range(max(chunks - 2, 0), chunks):
        for copy in ship(i, i % 2):
            copy.wait()
    keep.wait()


def output_kernel(pieces, turned, *refs):
    row_ref, col_ref, place_ref = refs[:3]
    w_hbm, left = refs[3:5]
    outs = refs[5 : 5 + len(pieces)]
    w_v, acc, staged, in_sem, out_sem = refs[5 + len(pieces) :]
    slots, block, _ = w_v.shape
    parts = 4
    some = slots // parts
    loads = []
    for k in range(parts):
        at = pl.ds(k * some, some)
        loads.append(pltpu.make_async_copy(w_hbm.at[at], w_v.at[at], in_sem.at[k]))
    for copy in loads:
        copy.start()
    acc[...] = jnp.zeros(acc.shape, F32)
    unroll = 2
    dims = (((1,), (1 if turned else 0,)), ((), ()))

    def step(i, carry):
        got = []
        for u in range(unroll):
            g = i * unroll + u
            got.append(lax.dot_general(left[col_ref[g]], w_v[g], dims, preferred_element_type=F32))
        for u in range(unroll):
            r = row_ref[i * unroll + u]
            acc[r] = acc[r] + got[u]
        return carry

    for k in range(parts):
        loads[k].wait()
        lax.fori_loop(k * some // unroll, (k + 1) * some // unroll, step, 0)

    count = staged.shape[0]
    per = staged.shape[2] // block
    bits = count.bit_length() - 1
    for a in range(count):
        if count == 1:
            at = 0
        else:
            far = place_ref[2] ^ a
            at = 0
            for b in range(bits):
                at = at + ((far >> b) & 1) * (count >> (b + 1))
        for q in range(per):
            staged[at, :, q * block : (q + 1) * block] = acc[a * per + q].astype(BF16)
    copies = [
        pltpu.make_async_copy(staged.at[pl.ds(start, size)], out, out_sem.at[k])
        for k, ((start, size), out) in enumerate(zip(pieces, outs))
    ]
    for copy in copies:
        copy.start()
    for copy in copies:
        copy.wait()


VMEM = pl.BlockSpec(memory_space=pltpu.VMEM)
SMEM = pl.BlockSpec(memory_space=pltpu.SMEM)


def cost(flops, size):
    return pl.CostEstimate(flops=flops, transcendentals=0, bytes_accessed=size)


def forward_products(tables, place, feats, up, parts, col_count, row_blocks, feat_shape):
    slots, block, _ = up.shape
    n_dp, n_feat = len(parts), len(feats)
    tokens = feat_shape[1]
    return pl.pallas_call(
        functools.partial(forward_kernel, n_feat, n_dp, row_blocks),
        out_shape=[
            jax.ShapeDtypeStruct((col_count, tokens, block), F32),
            jax.ShapeDtypeStruct((row_blocks, block, tokens), BF16),
            jax.ShapeDtypeStruct(up.shape, BF16),
        ],
        in_specs=[SMEM] * 6 + [ANY] * (n_feat + 1 + n_dp),
        out_specs=[VMEM, VMEM, ANY],
        scratch_shapes=[
            pltpu.VMEM(feat_shape, BF16),
            pltpu.VMEM(up.shape, BF16),
            pltpu.VMEM((n_dp,) + parts[0].shape, BF16),
            pltpu.VMEM(up.shape, BF16),
            pltpu.SemaphoreType.DMA((n_feat,)),
            pltpu.SemaphoreType.DMA((1 + n_dp,)),
            pltpu.SemaphoreType.DMA,
        ],
        compiler_params=pltpu.CompilerParams(vmem_limit_bytes=VMEM_LIMIT),
        cost_estimate=cost(2 * slots * tokens * block * block, 12 * slots * block * block),
        name="forward_products",
    )(*tables, place, *feats, up, *parts)


def gradient_products(tables, place, feats, down, parts, pre, x_t, feat_shape):
    slots, block, _ = down.shape
    n_dp, n_feat = len(parts), len(feats)
    rows = block // n_dp
    chunk = 8
    col_count, tokens, _ = pre.shape
    grad = jax.ShapeDtypeStruct((2, slots, rows, block), BF16)
    return pl.pallas_call(
        functools.partial(gradient_kernel, n_feat, n_dp),
        out_shape=[jax.ShapeDtypeStruct(pre.shape, BF16)] * 2
        + [jax.ShapeDtypeStruct(down.shape, BF16)]
        + [grad] * n_dp,
        in_specs=[SMEM] * 6 + [ANY] * (n_feat + 1 + n_dp) + [VMEM] * 2,
        out_specs=[VMEM, VMEM] + [ANY] * (1 + n_dp),
        scratch_shapes=[
            pltpu.VMEM(feat_shape, BF16),
            pltpu.VMEM(down.shape, BF16),
            pltpu.VMEM((n_dp,) + parts[0].shape, BF16),
            pltpu.VMEM(down.shape, BF16),
            pltpu.VMEM(pre.shape, F32),
            pltpu.VMEM((col_count, block, tokens), BF16),
            pltpu.VMEM((2, 2, chunk, block, block), BF16),
            pltpu.SemaphoreType.DMA((n_feat,)),
            pltpu.SemaphoreType.DMA((1 + n_dp,)),
            pltpu.SemaphoreType.DMA,
            pltpu.SemaphoreType.DMA((2, 2 * n_dp)),
        ],
        compiler_params=pltpu.CompilerParams(vmem_limit_bytes=VMEM_LIMIT),
        cost_estimate=cost(6 * slots * tokens * block * block, 20 * slots * block * block),
        name="gradient_products",
    )(*tables, place, *feats, down, *parts, pre, x_t)


def output_products(row, col, place, w, left, turned, pieces, feat_shape, row_blocks):
    slots, block, _ = w.shape
    count, tokens, shard = feat_shape
    return pl.pallas_call(
        functools.partial(output_kernel, pieces, turned),
        out_shape=[jax.ShapeDtypeStruct((size, tokens, shard), BF16) for _, size in pieces],
        in_specs=[SMEM] * 3 + [ANY, VMEM],
        out_specs=[ANY] * len(pieces),
        scratch_shapes=[
            pltpu.VMEM(w.shape, BF16),
            pltpu.VMEM((row_blocks, tokens, block), F32),
            pltpu.VMEM((count, tokens, shard), BF16),
            pltpu.SemaphoreType.DMA((4,)),
            pltpu.SemaphoreType.DMA((len(pieces),)),
        ],
        compiler_params=pltpu.CompilerParams(vmem_limit_bytes=VMEM_LIMIT),
        cost_estimate=cost(2 * slots * tokens * block * block, 4 * slots * block * block),
        name="output_products",
    )(row, col, place, w, left)


def adam_step(tables, grads, which, moments, arrived):
    slots, rows, block = moments[0].shape
    n_grads = len(grads)

    def kernel(home_ref, came_ref, kind_ref, *refs):
        grad_refs = refs[:n_grads]
        moment_refs = refs[n_grads : n_grads + 2]
        arrived_ref = refs[n_grads + 2]
        out = refs[n_grads + 3]

        def step(g, carry):
            at = came_ref[g]
            own = home_ref[g]
            kind = kind_ref[g]

            def moved(k):
                picked = lax.select(kind == 1, moment_refs[k][own], arrived_ref[at, k].astype(F32))
                return lax.select(kind == 0, jnp.zeros_like(picked), picked)

            total = grad_refs[0][0, g].astype(F32)
            for ref in grad_refs[1:]:
                total = total + ref[0, g].astype(F32)
            first = 0.9 * moved(0) + 0.1 * total
            second = 0.95 * moved(1) + 0.05 * total * total
            out[g] = first / (jnp.sqrt(second) + 1.0)
            return carry

        lax.fori_loop(0, slots, step, 0, unroll=4)

    half = pl.BlockSpec((1, slots, rows, block), lambda i: (which, 0, 0, 0))

    def whole(array):
        return pl.BlockSpec(array.shape, lambda i: (0,) * array.ndim)

    return pl.pallas_call(
        kernel,
        out_shape=jax.ShapeDtypeStruct(moments[0].shape, F32),
        grid=(1,),
        in_specs=[SMEM] * 3 + [half] * n_grads + [whole(m) for m in moments] + [whole(arrived)],
        out_specs=whole(moments[0]),
        compiler_params=pltpu.CompilerParams(vmem_limit_bytes=VMEM_LIMIT),
        cost_estimate=cost(15 * slots * rows * block, 17 * slots * rows * block),
        name="adam_step",
    )(*tables, *grads, *moments, arrived)


def layer(
    activations,
    cotangent,
    up_weight_blocks,
    down_weight_blocks,
    up_first_moment,
    up_second_moment,
    down_first_moment,
    down_second_moment,
    source,
    new_row,
    new_col,
    col_owner,
):
    tensor_size = lax.axis_size("tensor")
    n_dp = lax.axis_size("dp")
    nx = n_dp // 2
    my_index = lax.axis_index("tensor")
    my_dp = lax.axis_index("dp")
    slot_count, block, _ = up_weight_blocks.shape
    rows = block // n_dp
    bucket = (slot_count + tensor_size - 2) // tensor_size

    sources = source.reshape(tensor_size, slot_count)
    is_live = sources >= 0
    sender_dev = jnp.where(is_live, sources // slot_count, -1)
    sender_slot = jnp.where(is_live, sources % slot_count, 0)
    targets = jnp.arange(tensor_size, dtype=jnp.int32)[:, None]
    outgoing = is_live & (sender_dev == my_index) & (targets != my_index)
    out_flags = outgoing.astype(jnp.int32)
    out_rank = jnp.cumsum(out_flags, axis=1) - out_flags
    chosen = outgoing[:, :, None] & (
        out_rank[:, :, None] == jnp.arange(bucket, dtype=jnp.int32)[None, None, :]
    )
    send_slots = jnp.sum(jnp.where(chosen, sender_slot[:, :, None], 0), axis=1).reshape(-1)
    mine_dev = lax.dynamic_index_in_dim(sender_dev, my_index, 0, keepdims=False)
    mine_slot = lax.dynamic_index_in_dim(sender_slot, my_index, 0, keepdims=False)
    mine_live = mine_dev >= 0
    stays = mine_live & (mine_dev == my_index)
    positions = jnp.arange(slot_count, dtype=jnp.int32)
    earlier = (
        (mine_dev[:, None] == mine_dev[None, :])
        & mine_live[None, :]
        & (positions[None, :] < positions[:, None])
    )
    recv_rank = jnp.minimum(jnp.sum(earlier.astype(jnp.int32), axis=1), bucket - 1)
    home = jnp.where(stays, mine_slot, 0)
    came = jnp.where(mine_live & ~stays, mine_dev * bucket + recv_rank, 0)
    kind = jnp.where(stays, 1, jnp.where(mine_live, 2, 0)).astype(jnp.int32)
    col_count = col_owner.shape[0] // tensor_size
    col_slot = jnp.take(local_columns(col_owner), new_col)
    place = jnp.stack([my_dp // 2, my_dp % 2, my_index]).astype(jnp.int32)
    dp_index = my_dp.reshape(1).astype(jnp.int32)
    tables = (new_row, col_slot, home, came, kind)

    def exchange(packed):
        shaped = packed.reshape((tensor_size, bucket) + packed.shape[1:])
        got = lax.all_to_all(shaped, "tensor", split_axis=0, concat_axis=0, tiled=True)
        return got.reshape((tensor_size * bucket,) + packed.shape[1:])

    core_pairs = [(d, d ^ 1) for d in range(n_dp)]

    def x_pairs(j):
        return [(d, ((d // 2 + j) % nx) * 2 + d % 2) for d in range(n_dp)]

    def far_pairs(bit):
        return [(t, t ^ bit) for t in range(tensor_size)]

    def spread(own):
        parts = []
        for j in range(nx):
            mine = own
            if j:
                mine = lax.ppermute(own, "dp", x_pairs(j))
            parts += [mine, lax.ppermute(mine, "dp", core_pairs)]
        return parts

    up_pack = pack_weight(up_weight_blocks, send_slots, dp_index, rows)
    down_pack = pack_weight(down_weight_blocks, send_slots, dp_index, rows)
    up_in = exchange(up_pack)
    down_in = exchange(down_pack)
    up_parts = spread(up_in)
    down_parts = spread(down_in)

    shard = activations.shape[1]
    stacked = shard % block == 0 and tensor_size & (tensor_size - 1) == 0
    if stacked:
        bits = [1 << k for k in reversed(range(tensor_size.bit_length() - 1))]
        held = {0: jnp.stack([activations, cotangent])}
        for bit in bits:
            for m in list(held):
                held[m ^ bit] = lax.ppermute(held[m], "tensor", far_pairs(bit))
        feats = [held[m] for m in range(tensor_size)]
        feat_shape = (tensor_size,) + activations.shape
    else:
        x = lax.all_gather(activations, "tensor", axis=1, tiled=True)
        back = lax.all_gather(cotangent, "tensor", axis=1, tiled=True)
        feats = [jnp.stack([x, back])[:, None].reshape((2,) + x.shape)]
        feat_shape = (1,) + x.shape
    row_blocks = feat_shape[0] * feat_shape[2] // block

    ups = (up_first_moment, up_second_moment)
    downs = (down_first_moment, down_second_moment)
    ups_pack = pack_moments(ups, send_slots)
    downs_pack = pack_moments(downs, send_slots)
    ups_in = exchange(ups_pack)
    downs_in = exchange(downs_pack)

    pre, x_t, wu = forward_products(
        tables, place, feats, up_weight_blocks, up_parts, col_count, row_blocks, feat_shape
    )
    act, bpre, wd, *grads = gradient_products(
        tables, place, feats, down_weight_blocks, down_parts, pre, x_t, feat_shape
    )
    terms = []
    for j in range(nx):
        there = lax.ppermute(grads[2 * j + 1], "dp", core_pairs)
        if j == 0:
            terms += [grads[0], there]
        else:
            both = (grads[2 * j].astype(F32) + there.astype(F32)).astype(BF16)
            terms.append(lax.ppermute(both, "dp", x_pairs(j)))

    sums = []
    for w, left, turned in ((wd, act, False), (wu, bpre, True)):
        half = tensor_size // 2
        pieces = ((0, half), (half, half)) if stacked else ((0, 1),)
        got = output_products(
            new_row, col_slot, place, w, left, turned, pieces, feat_shape, row_blocks
        )
        if not stacked:
            sums.append(lax.psum_scatter(got[0][0], "tensor", scatter_dimension=1, tiled=True))
            continue
        held, send = got
        held = [held]
        bit = 1
        while True:
            held.append(lax.ppermute(send, "tensor", far_pairs(bit)))
            bit *= 2
            if bit >= tensor_size:
                break
            half = held[-1].shape[0] // 2
            send = sum(s[half : 2 * half].astype(F32) for s in held).astype(BF16)
            held = [s[:half] for s in held]
        sums.append(sum(s[0].astype(F32) for s in held).astype(BF16))
    out_sum, in_sum = sums

    up_step = adam_step((home, came, kind), terms, 0, ups, ups_in)
    down_step = adam_step((home, came, kind), terms, 1, downs, downs_in)
    return (out_sum, in_sum, up_step, down_step)


def solution(mesh):
    placed = (
        P("dp", "tensor"),
        P("dp", "tensor"),
        P("tensor", None, None),
        P("tensor", None, None),
        P("tensor", "dp", None),
        P("tensor", "dp", None),
        P("tensor", "dp", None),
        P("tensor", "dp", None),
        P(),
        P("tensor"),
        P("tensor"),
        P(),
    )
    return jax.shard_map(
        layer,
        mesh=mesh,
        in_specs=placed,
        out_specs=(
            P("dp", "tensor"),
            P("dp", "tensor"),
            P("tensor", "dp", None),
            P("tensor", "dp", None),
        ),
        check_vma=False,
    )
```

```python
import functools
import math

import jax
import jax.numpy as jnp
from jax import lax
from jax.experimental import pallas as pl
from jax.experimental.pallas import tpu as pltpu
from jax.sharding import PartitionSpec as P


gelu_scale = math.sqrt(2.0 / math.pi)
VMEM_LIMIT = 60 * 1024 * 1024
IN_UNROLL = 32
OUT_UNROLL = 56
CHUNK = 28
ADAM_UNROLL = 8
ADAM_PARTS = 4

F32 = jnp.float32
BF16 = jnp.bfloat16
ANY = pl.BlockSpec(memory_space=pl.ANY)


def gelu_pair(pre_act):
    inner = gelu_scale * (pre_act + 0.044715 * pre_act * pre_act * pre_act)
    tangent = jnp.tanh(inner)
    gelu_value = 0.5 * pre_act * (1.0 + tangent)
    gelu_slope = 0.5 * (1.0 + tangent) + 0.5 * pre_act * (1.0 - tangent * tangent) * gelu_scale * (
        1.0 + 3.0 * 0.044715 * pre_act * pre_act
    )
    return (gelu_value, gelu_slope)


def local_columns(col_owner):
    count_all = col_owner.shape[0]
    order = jnp.arange(count_all, dtype=jnp.int32)
    same = (col_owner[None, :] == col_owner[:, None]) & (order[None, :] < order[:, None])
    return jnp.sum(same.astype(jnp.int32), axis=1)


def pack_weight(tiles, send_slots, dp_index, rows):
    slots, _, width = tiles.shape
    count = send_slots.shape[0]

    def kernel(send_ref, dp_ref, in_ref, out_ref):
        def step(i, carry):
            out_ref[i] = in_ref[send_ref[i]]
            return carry

        lax.fori_loop(0, count, step, 0, unroll=8)

    return pl.pallas_call(
        kernel,
        out_shape=jax.ShapeDtypeStruct((count, rows, width), tiles.dtype),
        grid_spec=pltpu.PrefetchScalarGridSpec(
            num_scalar_prefetch=2,
            grid=(1,),
            in_specs=[pl.BlockSpec((slots, rows, width), lambda i, s, d: (0, d[0], 0))],
            out_specs=pl.BlockSpec((count, rows, width), lambda i, s, d: (0, 0, 0)),
        ),
        compiler_params=pltpu.CompilerParams(vmem_limit_bytes=VMEM_LIMIT),
        cost_estimate=pl.CostEstimate(flops=0, transcendentals=0, bytes_accessed=4 * count * rows * width),
        name="pack_weight",
    )(send_slots, dp_index, tiles)


def pack_moments(arrays, send_slots, bucket):
    _, rows, width = arrays[0].shape
    targets = send_slots.shape[0] // bucket
    kinds = len(arrays)

    def kernel(send_ref, *refs):
        outs = refs[kinds:]
        unroll = math.gcd(bucket, 4)
        for m in range(targets):

            def step(i, carry, m=m):
                for u in range(unroll):
                    s = send_ref[m * bucket + i * unroll + u]
                    for k in range(kinds):
                        outs[m][i * unroll + u, k] = refs[k][s].astype(BF16)
                return carry

            lax.fori_loop(0, bucket // unroll, step, 0)

    return pl.pallas_call(
        kernel,
        out_shape=[jax.ShapeDtypeStruct((bucket, kinds, rows, width), BF16)] * targets,
        in_specs=[SMEM] + [pl.BlockSpec(memory_space=pltpu.VMEM)] * kinds,
        out_specs=[pl.BlockSpec(memory_space=pltpu.VMEM)] * targets,
        compiler_params=pltpu.CompilerParams(vmem_limit_bytes=VMEM_LIMIT),
        cost_estimate=pl.CostEstimate(
            flops=0, transcendentals=0, bytes_accessed=6 * kinds * targets * bucket * rows * width
        ),
        name="pack_moments",
    )(send_slots, *arrays)


def columns(ref, r, block):
    per = ref.shape[2] // block
    a = lax.div(r, per)
    off = pl.multiple_of((r - a * per) * block, block)
    return ref[a, :, pl.ds(off, block)]


def weight(own, came, home_ref, came_ref, kind_ref, g):
    kind = kind_ref[g]
    mine = own[home_ref[g]]
    at = came_ref[g]
    theirs = jnp.concatenate([came[q, at] for q in range(came.shape[0])], axis=0)
    picked = lax.select(kind == 1, mine, theirs)
    return lax.select(kind == 0, jnp.zeros_like(picked), picked)


def feature_copies(parts, which, place_ref, buf, sem):
    copies = []
    for m, part in enumerate(parts):
        at = (place_ref[2] ^ m) if len(parts) > 1 else 0
        copies.append(pltpu.make_async_copy(part.at[which], buf.at[at], sem.at[m]))
    return copies


def weight_copies(own, own_v, parts, parts_v, place_ref, sem):
    n_dp = len(parts)
    nx = n_dp // 2
    copies = [pltpu.make_async_copy(own, own_v, sem.at[0])]
    for j in range(nx):
        for other in range(2):
            k = 2 * j + other
            owner = lax.rem(place_ref[0] + nx - j, nx) * 2 + (place_ref[1] + other) % 2
            copies.append(pltpu.make_async_copy(parts[k], parts_v.at[owner], sem.at[1 + k]))
    return copies


def forward_kernel(n_feat, n_dp, row_blocks, *refs):
    row_ref, col_ref, home_ref, came_ref, kind_ref, place_ref = refs[:6]
    feats = refs[6 : 6 + n_feat]
    up_hbm = refs[6 + n_feat]
    parts = refs[7 + n_feat : 7 + n_feat + n_dp]
    act, act_t, slopes, x_t, wu_hbm, x_v, up_v, up_a, wu, pre, feat_sem, in_sem, out_sem = refs[7 + n_feat + n_dp :]
    slots, block, _ = up_v.shape
    copies = feature_copies(feats, 0, place_ref, x_v, feat_sem)
    copies += weight_copies(up_hbm, up_v, parts, up_a, place_ref, in_sem)
    for copy in copies:
        copy.start()
    pre[...] = jnp.zeros(pre.shape, F32)
    for copy in copies:
        copy.wait()
    unroll = math.gcd(slots, IN_UNROLL)

    def step(i, carry):
        got = []
        for u in range(unroll):
            g = i * unroll + u
            w = weight(up_v, up_a, home_ref, came_ref, kind_ref, g)
            wu[g] = w
            got.append(jnp.dot(columns(x_v, row_ref[g], block), w, preferred_element_type=F32))
        for u in range(unroll):
            c = col_ref[i * unroll + u]
            pre[c] = pre[c] + got[u]
        return carry

    lax.fori_loop(0, slots // unroll, step, 0)
    keep = pltpu.make_async_copy(wu, wu_hbm, out_sem)
    keep.start()

    def turn(r, carry):
        x_t[r] = columns(x_v, r, block).T
        return carry

    lax.fori_loop(0, row_blocks, turn, 0)

    def bend(c, carry):
        value, slope = gelu_pair(pre[c])
        narrow = value.astype(BF16)
        act[c] = narrow
        act_t[c] = narrow.T
        slopes[c] = slope
        return carry

    lax.fori_loop(0, pre.shape[0], bend, 0)
    keep.wait()


def gradient_kernel(n_feat, n_dp, *refs):
    row_ref, col_ref, home_ref, came_ref, kind_ref, place_ref = refs[:6]
    feats = refs[6 : 6 + n_feat]
    down_hbm = refs[6 + n_feat]
    parts = refs[7 + n_feat : 7 + n_feat + n_dp]
    act_t, slopes, x_t = refs[7 + n_feat + n_dp : 10 + n_feat + n_dp]
    outs = refs[10 + n_feat + n_dp :]
    bpre, wd_hbm = outs[:2]
    grad_refs = outs[2 : 2 + n_dp]
    back_v, down_v, down_a, wd, back, stage, feat_sem, in_sem, keep_sem, out_sem = outs[2 + n_dp :]
    slots, block, _ = down_v.shape
    rows = block // n_dp
    nx = n_dp // 2
    chunk = stage.shape[2]
    copies = feature_copies(feats, 1, place_ref, back_v, feat_sem)
    copies += weight_copies(down_hbm, down_v, parts, down_a, place_ref, in_sem)
    for copy in copies:
        copy.start()
    back[...] = jnp.zeros(back.shape, F32)
    for copy in copies:
        copy.wait()
    unroll = math.gcd(slots, IN_UNROLL)

    def backward(i, carry):
        got = []
        for u in range(unroll):
            g = i * unroll + u
            w = weight(down_v, down_a, home_ref, came_ref, kind_ref, g)
            wd[g] = w
            got.append(
                lax.dot_general(
                    columns(back_v, row_ref[g], block), w, (((1,), (1,)), ((), ())), preferred_element_type=F32
                )
            )
        for u in range(unroll):
            c = col_ref[i * unroll + u]
            back[c] = back[c] + got[u]
        return carry

    lax.fori_loop(0, slots // unroll, backward, 0)
    keep = pltpu.make_async_copy(wd, wd_hbm, keep_sem)
    keep.start()

    def bend(c, carry):
        bpre[c] = (back[c] * slopes[c]).astype(BF16)
        return carry

    lax.fori_loop(0, slopes.shape[0], bend, 0)

    def ship(i, slot):
        out = []
        for j in range(nx):
            for other in range(2):
                owner = lax.rem(place_ref[0] + j, nx) * 2 + (place_ref[1] + other) % 2
                start = pl.multiple_of(owner * rows, rows)
                for p in range(2):
                    out.append(
                        pltpu.make_async_copy(
                            stage.at[slot, p, :, pl.ds(start, rows), :],
                            grad_refs[2 * j + other].at[p, pl.ds(i * chunk, chunk)],
                            out_sem.at[slot, 2 * (2 * j + other) + p],
                        )
                    )
        return out

    def last(i, carry):
        slot = lax.rem(i, 2)

        @pl.when(i >= 2)
        def _():
            for copy in ship(i - 2, slot):
                copy.wait()

        for u in range(chunk):
            g = i * chunk + u
            r = row_ref[g]
            c = col_ref[g]
            stage[slot, 0, u] = jnp.dot(x_t[r], bpre[c], preferred_element_type=F32).astype(BF16)
            stage[slot, 1, u] = jnp.dot(
                act_t[c], columns(back_v, r, block), preferred_element_type=F32
            ).astype(BF16)
        for copy in ship(i, slot):
            copy.start()
        return carry

    chunks = slots // chunk
    lax.fori_loop(0, chunks, last, 0)
    for i in range(max(chunks - 2, 0), chunks):
        for copy in ship(i, i % 2):
            copy.wait()
    keep.wait()


def output_kernel(pieces, turned, *refs):
    row_ref, col_ref, place_ref = refs[:3]
    w_hbm, left = refs[3:5]
    outs = refs[5 : 5 + len(pieces)]
    w_v, acc, staged, in_sem, out_sem = refs[5 + len(pieces) :]
    slots, block, _ = w_v.shape
    parts = 4
    some = slots // parts
    loads = []
    for k in range(parts):
        at = pl.ds(k * some, some)
        loads.append(pltpu.make_async_copy(w_hbm.at[at], w_v.at[at], in_sem.at[k]))
    for copy in loads:
        copy.start()
    acc[...] = jnp.zeros(acc.shape, F32)
    unroll = math.gcd(some, OUT_UNROLL)
    dims = (((1,), (1 if turned else 0,)), ((), ()))

    def step(i, carry):
        got = []
        for u in range(unroll):
            g = i * unroll + u
            got.append(lax.dot_general(left[col_ref[g]], w_v[g], dims, preferred_element_type=F32))
        for u in range(unroll):
            r = row_ref[i * unroll + u]
            acc[r] = acc[r] + got[u]
        return carry

    for k in range(parts):
        loads[k].wait()
        lax.fori_loop(k * some // unroll, (k + 1) * some // unroll, step, 0)

    count = staged.shape[0]
    per = staged.shape[2] // block
    bits = count.bit_length() - 1
    for a in range(count):
        if count == 1:
            at = 0
        else:
            far = place_ref[2] ^ a
            at = 0
            for b in range(bits):
                at = at + ((far >> b) & 1) * (count >> (b + 1))
        for q in range(per):
            staged[at, :, q * block : (q + 1) * block] = acc[a * per + q].astype(BF16)
    copies = [
        pltpu.make_async_copy(staged.at[pl.ds(start, size)], out, out_sem.at[k])
        for k, ((start, size), out) in enumerate(zip(pieces, outs))
    ]
    for copy in copies:
        copy.start()
    for copy in copies:
        copy.wait()


VMEM = pl.BlockSpec(memory_space=pltpu.VMEM)
SMEM = pl.BlockSpec(memory_space=pltpu.SMEM)


def cost(flops, size):
    return pl.CostEstimate(flops=flops, transcendentals=0, bytes_accessed=size)


def forward_products(tables, place, feats, up, parts, col_count, row_blocks, feat_shape):
    slots, block, _ = up.shape
    n_dp, n_feat = len(parts), len(feats)
    tokens = feat_shape[1]
    return pl.pallas_call(
        functools.partial(forward_kernel, n_feat, n_dp, row_blocks),
        out_shape=[
            jax.ShapeDtypeStruct((col_count, tokens, block), BF16),
            jax.ShapeDtypeStruct((col_count, block, tokens), BF16),
            jax.ShapeDtypeStruct((col_count, tokens, block), F32),
            jax.ShapeDtypeStruct((row_blocks, block, tokens), BF16),
            jax.ShapeDtypeStruct(up.shape, BF16),
        ],
        in_specs=[SMEM] * 6 + [ANY] * (n_feat + 1 + n_dp),
        out_specs=[VMEM] * 4 + [ANY],
        scratch_shapes=[
            pltpu.VMEM(feat_shape, BF16),
            pltpu.VMEM(up.shape, BF16),
            pltpu.VMEM((n_dp,) + parts[0].shape, BF16),
            pltpu.VMEM(up.shape, BF16),
            pltpu.VMEM((col_count, tokens, block), F32),
            pltpu.SemaphoreType.DMA((n_feat,)),
            pltpu.SemaphoreType.DMA((1 + n_dp,)),
            pltpu.SemaphoreType.DMA,
        ],
        compiler_params=pltpu.CompilerParams(vmem_limit_bytes=VMEM_LIMIT),
        cost_estimate=cost(2 * slots * tokens * block * block, 12 * slots * block * block),
        name="forward_products",
    )(*tables, place, *feats, up, *parts)


def gradient_products(tables, place, feats, down, parts, act_t, slopes, x_t, feat_shape):
    slots, block, _ = down.shape
    n_dp, n_feat = len(parts), len(feats)
    rows = block // n_dp
    chunk = math.gcd(slots, CHUNK)
    tokens = slopes.shape[1]
    grad = jax.ShapeDtypeStruct((2, slots, rows, block), BF16)
    return pl.pallas_call(
        functools.partial(gradient_kernel, n_feat, n_dp),
        out_shape=[jax.ShapeDtypeStruct(slopes.shape, BF16)]
        + [jax.ShapeDtypeStruct(down.shape, BF16)]
        + [grad] * n_dp,
        in_specs=[SMEM] * 6 + [ANY] * (n_feat + 1 + n_dp) + [VMEM] * 3,
        out_specs=[VMEM] + [ANY] * (1 + n_dp),
        scratch_shapes=[
            pltpu.VMEM(feat_shape, BF16),
            pltpu.VMEM(down.shape, BF16),
            pltpu.VMEM((n_dp,) + parts[0].shape, BF16),
            pltpu.VMEM(down.shape, BF16),
            pltpu.VMEM(slopes.shape, F32),
            pltpu.VMEM((2, 2, chunk, block, block), BF16),
            pltpu.SemaphoreType.DMA((n_feat,)),
            pltpu.SemaphoreType.DMA((1 + n_dp,)),
            pltpu.SemaphoreType.DMA,
            pltpu.SemaphoreType.DMA((2, 2 * n_dp)),
        ],
        compiler_params=pltpu.CompilerParams(vmem_limit_bytes=VMEM_LIMIT),
        cost_estimate=cost(6 * slots * tokens * block * block, 20 * slots * block * block),
        name="gradient_products",
    )(*tables, place, *feats, down, *parts, act_t, slopes, x_t)


def output_products(row, col, place, w, left, turned, pieces, feat_shape, row_blocks):
    slots, block, _ = w.shape
    count, tokens, shard = feat_shape
    return pl.pallas_call(
        functools.partial(output_kernel, pieces, turned),
        out_shape=[jax.ShapeDtypeStruct((size, tokens, shard), BF16) for _, size in pieces],
        in_specs=[SMEM] * 3 + [ANY, VMEM],
        out_specs=[ANY] * len(pieces),
        scratch_shapes=[
            pltpu.VMEM(w.shape, BF16),
            pltpu.VMEM((row_blocks, tokens, block), F32),
            pltpu.VMEM((count, tokens, shard), BF16),
            pltpu.SemaphoreType.DMA((4,)),
            pltpu.SemaphoreType.DMA((len(pieces),)),
        ],
        compiler_params=pltpu.CompilerParams(vmem_limit_bytes=VMEM_LIMIT),
        cost_estimate=cost(2 * slots * tokens * block * block, 4 * slots * block * block),
        name="output_products",
    )(row, col, place, w, left)


def adam_step(tables, grads, which, moments, arrived):
    slots, rows, block = moments[0].shape
    n_grads = len(grads)
    n_from = len(arrived)
    bucket = arrived[0].shape[0]
    parts = math.gcd(slots, ADAM_PARTS)
    some = slots // parts

    def kernel(home_ref, came_ref, kind_ref, *refs):
        grad_refs = refs[:n_grads]
        moment_refs = refs[n_grads : n_grads + 2]
        arrived_refs = refs[n_grads + 2 : n_grads + 2 + n_from]
        out_hbm, grad_v, moment_v, arrived_v, out_v, grad_sem, moment_sem, arrived_sem, out_sem = refs[
            n_grads + 2 + n_from :
        ]
        first = [
            pltpu.make_async_copy(moment_refs[k], moment_v.at[k], moment_sem.at[k]) for k in range(2)
        ] + [
            pltpu.make_async_copy(arrived_refs[m], arrived_v.at[pl.ds(m * bucket, bucket)], arrived_sem.at[m])
            for m in range(n_from)
        ]
        later = [
            [
                pltpu.make_async_copy(
                    grad_refs[k].at[which, pl.ds(q * some, some)],
                    grad_v.at[k, pl.ds(q * some, some)],
                    grad_sem.at[q, k],
                )
                for k in range(n_grads)
            ]
            for q in range(parts)
        ]
        outs = [
            pltpu.make_async_copy(
                out_v.at[pl.ds(q * some, some)], out_hbm.at[pl.ds(q * some, some)], out_sem.at[q]
            )
            for q in range(parts)
        ]
        for copy in first + sum(later, []):
            copy.start()

        def step(g, carry):
            at = came_ref[g]
            own = home_ref[g]
            kind = kind_ref[g]

            def moved(k):
                picked = lax.select(kind == 1, moment_v[k, own], arrived_v[at, k].astype(F32))
                return lax.select(kind == 0, jnp.zeros_like(picked), picked)

            total = grad_v[0, g].astype(F32)
            for k in range(1, n_grads):
                total = total + grad_v[k, g].astype(F32)
            first_moment = 0.9 * moved(0) + 0.1 * total
            second_moment = 0.95 * moved(1) + 0.05 * total * total
            out_v[g] = first_moment / (jnp.sqrt(second_moment) + 1.0)
            return carry

        for copy in first:
            copy.wait()
        unroll = math.gcd(some, ADAM_UNROLL)
        for q in range(parts):
            for copy in later[q]:
                copy.wait()

            def trip(i, carry, q=q):
                for u in range(unroll):
                    step(q * some + i * unroll + u, carry)
                return carry

            lax.fori_loop(0, some // unroll, trip, 0)
            outs[q].start()
        for copy in outs:
            copy.wait()

    return pl.pallas_call(
        kernel,
        out_shape=jax.ShapeDtypeStruct(moments[0].shape, F32),
        in_specs=[SMEM] * 3 + [ANY] * (n_grads + 2 + n_from),
        out_specs=ANY,
        scratch_shapes=[
            pltpu.VMEM((n_grads, slots, rows, block), BF16),
            pltpu.VMEM((2, slots, rows, block), F32),
            pltpu.VMEM((n_from * bucket, 2, rows, block), BF16),
            pltpu.VMEM((slots, rows, block), F32),
            pltpu.SemaphoreType.DMA((parts, n_grads)),
            pltpu.SemaphoreType.DMA((2,)),
            pltpu.SemaphoreType.DMA((n_from,)),
            pltpu.SemaphoreType.DMA((parts,)),
        ],
        compiler_params=pltpu.CompilerParams(vmem_limit_bytes=VMEM_LIMIT),
        cost_estimate=cost(15 * slots * rows * block, 17 * slots * rows * block),
        name="adam_step",
    )(*tables, *grads, *moments, *arrived)


def layer(
    activations,
    cotangent,
    up_weight_blocks,
    down_weight_blocks,
    up_first_moment,
    up_second_moment,
    down_first_moment,
    down_second_moment,
    source,
    new_row,
    new_col,
    col_owner,
):
    tensor_size = lax.axis_size("tensor")
    n_dp = lax.axis_size("dp")
    nx = n_dp // 2
    my_index = lax.axis_index("tensor")
    my_dp = lax.axis_index("dp")
    slot_count, block, _ = up_weight_blocks.shape
    rows = block // n_dp
    bucket = (slot_count + tensor_size - 2) // tensor_size

    sources = source.reshape(tensor_size, slot_count)
    is_live = sources >= 0
    sender_dev = jnp.where(is_live, sources // slot_count, -1)
    sender_slot = jnp.where(is_live, sources % slot_count, 0)
    targets = jnp.arange(tensor_size, dtype=jnp.int32)[:, None]
    outgoing = is_live & (sender_dev == my_index) & (targets != my_index)
    out_flags = outgoing.astype(jnp.int32)
    out_rank = jnp.cumsum(out_flags, axis=1) - out_flags
    chosen = outgoing[:, :, None] & (
        out_rank[:, :, None] == jnp.arange(bucket, dtype=jnp.int32)[None, None, :]
    )
    send_slots = jnp.sum(jnp.where(chosen, sender_slot[:, :, None], 0), axis=1).reshape(-1)
    mine_dev = lax.dynamic_index_in_dim(sender_dev, my_index, 0, keepdims=False)
    mine_slot = lax.dynamic_index_in_dim(sender_slot, my_index, 0, keepdims=False)
    mine_live = mine_dev >= 0
    stays = mine_live & (mine_dev == my_index)
    positions = jnp.arange(slot_count, dtype=jnp.int32)
    earlier = (
        (mine_dev[:, None] == mine_dev[None, :])
        & mine_live[None, :]
        & (positions[None, :] < positions[:, None])
    )
    recv_rank = jnp.minimum(jnp.sum(earlier.astype(jnp.int32), axis=1), bucket - 1)
    home = jnp.where(stays, mine_slot, 0)
    came = jnp.where(mine_live & ~stays, mine_dev * bucket + recv_rank, 0)
    kind = jnp.where(stays, 1, jnp.where(mine_live, 2, 0)).astype(jnp.int32)
    distance = lax.rem(my_index - mine_dev + tensor_size, tensor_size)
    came_moment = jnp.where(mine_live & ~stays, (distance - 1) * bucket + recv_rank, 0)
    by_target = send_slots.reshape(tensor_size, bucket)
    by_distance = lax.dynamic_slice_in_dim(
        jnp.concatenate([by_target, by_target], axis=0), my_index + 1, tensor_size - 1, axis=0
    ).reshape(-1)
    col_count = col_owner.shape[0] // tensor_size
    col_slot = jnp.take(local_columns(col_owner), new_col)
    place = jnp.stack([my_dp // 2, my_dp % 2, my_index]).astype(jnp.int32)
    dp_index = my_dp.reshape(1).astype(jnp.int32)
    tables = (new_row, col_slot, home, came, kind)

    def exchange(packed):
        shaped = packed.reshape((tensor_size, bucket) + packed.shape[1:])
        got = lax.all_to_all(shaped, "tensor", split_axis=0, concat_axis=0, tiled=True)
        return got.reshape((tensor_size * bucket,) + packed.shape[1:])

    core_pairs = [(d, d ^ 1) for d in range(n_dp)]

    def x_pairs(j):
        return [(d, ((d // 2 + j) % nx) * 2 + d % 2) for d in range(n_dp)]

    def far_pairs(bit):
        return [(t, t ^ bit) for t in range(tensor_size)]

    def spread(own):
        parts = []
        for j in range(nx):
            mine = own
            if j:
                mine = lax.ppermute(own, "dp", x_pairs(j))
            parts += [mine, lax.ppermute(mine, "dp", core_pairs)]
        return parts

    up_pack = pack_weight(up_weight_blocks, send_slots, dp_index, rows)
    down_pack = pack_weight(down_weight_blocks, send_slots, dp_index, rows)
    up_in = exchange(up_pack)
    down_in = exchange(down_pack)
    up_parts = spread(up_in)
    down_parts = spread(down_in)

    shard = activations.shape[1]
    stacked = shard % block == 0 and tensor_size & (tensor_size - 1) == 0
    if stacked:
        bits = [1 << k for k in reversed(range(tensor_size.bit_length() - 1))]
        held = {0: jnp.stack([activations, cotangent])}
        for bit in bits:
            for m in list(held):
                held[m ^ bit] = lax.ppermute(held[m], "tensor", far_pairs(bit))
        feats = [held[m] for m in range(tensor_size)]
        feat_shape = (tensor_size,) + activations.shape
    else:
        x = lax.all_gather(activations, "tensor", axis=1, tiled=True)
        back = lax.all_gather(cotangent, "tensor", axis=1, tiled=True)
        feats = [jnp.stack([x, back])[:, None].reshape((2,) + x.shape)]
        feat_shape = (1,) + x.shape
    row_blocks = feat_shape[0] * feat_shape[2] // block

    ups = (up_first_moment, up_second_moment)
    downs = (down_first_moment, down_second_moment)

    def exchange_parts(parts):
        got = []
        for m, part in enumerate(parts, 1):
            pairs = [(t, (t + m) % tensor_size) for t in range(tensor_size)]
            got.append(lax.ppermute(part, "tensor", pairs))
        return got

    ups_pack = pack_moments(ups, by_distance, bucket)
    downs_pack = pack_moments(downs, by_distance, bucket)
    ups_in = exchange_parts(ups_pack)
    downs_in = exchange_parts(downs_pack)

    act, act_t, slopes, x_t, wu = forward_products(
        tables, place, feats, up_weight_blocks, up_parts, col_count, row_blocks, feat_shape
    )
    bpre, wd, *grads = gradient_products(
        tables, place, feats, down_weight_blocks, down_parts, act_t, slopes, x_t, feat_shape
    )
    terms = []
    for j in range(nx):
        there = lax.ppermute(grads[2 * j + 1], "dp", core_pairs)
        if j == 0:
            terms += [grads[0], there]
        else:
            both = (grads[2 * j].astype(F32) + there.astype(F32)).astype(BF16)
            terms.append(lax.ppermute(both, "dp", x_pairs(j)))

    sums = []
    for w, left, turned in ((wd, act, False), (wu, bpre, True)):
        half = tensor_size // 2
        pieces = ((0, half), (half, half)) if stacked else ((0, 1),)
        got = output_products(
            new_row, col_slot, place, w, left, turned, pieces, feat_shape, row_blocks
        )
        if not stacked:
            sums.append(lax.psum_scatter(got[0][0], "tensor", scatter_dimension=1, tiled=True))
            continue
        held, send = got
        held = [held]
        bit = 1
        while True:
            held.append(lax.ppermute(send, "tensor", far_pairs(bit)))
            bit *= 2
            if bit >= tensor_size:
                break
            half = held[-1].shape[0] // 2
            send = sum(s[half : 2 * half].astype(F32) for s in held).astype(BF16)
            held = [s[:half] for s in held]
        sums.append(sum(s[0].astype(F32) for s in held).astype(BF16))
    out_sum, in_sum = sums

    up_step = adam_step((home, came_moment, kind), terms, 0, ups, ups_in)
    down_step = adam_step((home, came_moment, kind), terms, 1, downs, downs_in)
    return (out_sum, in_sum, up_step, down_step)


def solution(mesh):
    placed = (
        P("dp", "tensor"),
        P("dp", "tensor"),
        P("tensor", None, None),
        P("tensor", None, None),
        P("tensor", "dp", None),
        P("tensor", "dp", None),
        P("tensor", "dp", None),
        P("tensor", "dp", None),
        P(),
        P("tensor"),
        P("tensor"),
        P(),
    )
    return jax.shard_map(
        layer,
        mesh=mesh,
        in_specs=placed,
        out_specs=(
            P("dp", "tensor"),
            P("dp", "tensor"),
            P("tensor", "dp", None),
            P("tensor", "dp", None),
        ),
        check_vma=False,
    )
```

```python
import functools
import math

import jax
import jax.numpy as jnp
from jax import lax
from jax.experimental import pallas as pl
from jax.experimental.pallas import tpu as pltpu
from jax.sharding import PartitionSpec as P


gelu_scale = math.sqrt(2.0 / math.pi)
VMEM_LIMIT = 60 * 1024 * 1024
IN_UNROLL = 32
OUT_UNROLL = 56
CHUNK = 28
ADAM_UNROLL = 8
ADAM_PARTS = 4

F32 = jnp.float32
BF16 = jnp.bfloat16
ANY = pl.BlockSpec(memory_space=pl.ANY)


def gelu_pair(pre_act):
    inner = gelu_scale * (pre_act + 0.044715 * pre_act * pre_act * pre_act)
    tangent = jnp.tanh(inner)
    gelu_value = 0.5 * pre_act * (1.0 + tangent)
    gelu_slope = 0.5 * (1.0 + tangent) + 0.5 * pre_act * (1.0 - tangent * tangent) * gelu_scale * (
        1.0 + 3.0 * 0.044715 * pre_act * pre_act
    )
    return (gelu_value, gelu_slope)


def local_columns(col_owner):
    count_all = col_owner.shape[0]
    order = jnp.arange(count_all, dtype=jnp.int32)
    same = (col_owner[None, :] == col_owner[:, None]) & (order[None, :] < order[:, None])
    return jnp.sum(same.astype(jnp.int32), axis=1)


def pack_weight(tiles, send_slots, dp_index, rows):
    slots, _, width = tiles.shape
    count = send_slots.shape[0]

    def kernel(send_ref, dp_ref, in_ref, out_ref):
        def step(i, carry):
            out_ref[i] = in_ref[send_ref[i]]
            return carry

        lax.fori_loop(0, count, step, 0, unroll=8)

    return pl.pallas_call(
        kernel,
        out_shape=jax.ShapeDtypeStruct((count, rows, width), tiles.dtype),
        grid_spec=pltpu.PrefetchScalarGridSpec(
            num_scalar_prefetch=2,
            grid=(1,),
            in_specs=[pl.BlockSpec((slots, rows, width), lambda i, s, d: (0, d[0], 0))],
            out_specs=pl.BlockSpec((count, rows, width), lambda i, s, d: (0, 0, 0)),
        ),
        compiler_params=pltpu.CompilerParams(vmem_limit_bytes=VMEM_LIMIT),
        cost_estimate=pl.CostEstimate(flops=0, transcendentals=0, bytes_accessed=4 * count * rows * width),
        name="pack_weight",
    )(send_slots, dp_index, tiles)


def pack_moments(arrays, send_slots):
    slots, rows, width = arrays[0].shape
    count = send_slots.shape[0]
    kinds = len(arrays)

    def kernel(send_ref, *refs):
        out_ref = refs[-1]

        def step(i, carry):
            s = send_ref[i]
            for k in range(kinds):
                out_ref[i, k] = refs[k][s].astype(BF16)
            return carry

        lax.fori_loop(0, count, step, 0, unroll=4)

    whole = pl.BlockSpec((slots, rows, width), lambda i, s: (0, 0, 0))
    return pl.pallas_call(
        kernel,
        out_shape=jax.ShapeDtypeStruct((count, kinds, rows, width), BF16),
        grid_spec=pltpu.PrefetchScalarGridSpec(
            num_scalar_prefetch=1,
            grid=(1,),
            in_specs=[whole] * kinds,
            out_specs=pl.BlockSpec((count, kinds, rows, width), lambda i, s: (0, 0, 0, 0)),
        ),
        compiler_params=pltpu.CompilerParams(vmem_limit_bytes=VMEM_LIMIT),
        cost_estimate=pl.CostEstimate(
            flops=0, transcendentals=0, bytes_accessed=6 * kinds * count * rows * width
        ),
        name="pack_moments",
    )(send_slots, *arrays)


def columns(ref, r, block):
    per = ref.shape[2] // block
    a = lax.div(r, per)
    off = pl.multiple_of((r - a * per) * block, block)
    return ref[a, :, pl.ds(off, block)]


def weight(own, came, home_ref, came_ref, kind_ref, g):
    kind = kind_ref[g]
    mine = own[home_ref[g]]
    at = came_ref[g]
    theirs = jnp.concatenate([came[q, at] for q in range(came.shape[0])], axis=0)
    picked = lax.select(kind == 1, mine, theirs)
    return lax.select(kind == 0, jnp.zeros_like(picked), picked)


def feature_copies(parts, which, place_ref, buf, sem):
    copies = []
    for m, part in enumerate(parts):
        at = (place_ref[2] ^ m) if len(parts) > 1 else 0
        copies.append(pltpu.make_async_copy(part.at[which], buf.at[at], sem.at[m]))
    return copies


def weight_copies(own, own_v, parts, parts_v, place_ref, sem):
    n_dp = len(parts)
    nx = n_dp // 2
    copies = [pltpu.make_async_copy(own, own_v, sem.at[0])]
    for j in range(nx):
        for other in range(2):
            k = 2 * j + other
            owner = lax.rem(place_ref[0] + nx - j, nx) * 2 + (place_ref[1] + other) % 2
            copies.append(pltpu.make_async_copy(parts[k], parts_v.at[owner], sem.at[1 + k]))
    return copies


def forward_kernel(n_feat, n_dp, row_blocks, *refs):
    row_ref, col_ref, home_ref, came_ref, kind_ref, place_ref = refs[:6]
    feats = refs[6 : 6 + n_feat]
    up_hbm = refs[6 + n_feat]
    parts = refs[7 + n_feat : 7 + n_feat + n_dp]
    act, act_t, slopes, x_t, wu_hbm, x_v, up_v, up_a, wu, pre, feat_sem, in_sem, out_sem = refs[7 + n_feat + n_dp :]
    slots, block, _ = up_v.shape
    copies = feature_copies(feats, 0, place_ref, x_v, feat_sem)
    copies += weight_copies(up_hbm, up_v, parts, up_a, place_ref, in_sem)
    for copy in copies:
        copy.start()
    pre[...] = jnp.zeros(pre.shape, F32)
    for copy in copies:
        copy.wait()
    unroll = math.gcd(slots, IN_UNROLL)

    def step(i, carry):
        got = []
        for u in range(unroll):
            g = i * unroll + u
            w = weight(up_v, up_a, home_ref, came_ref, kind_ref, g)
            wu[g] = w
            got.append(jnp.dot(columns(x_v, row_ref[g], block), w, preferred_element_type=F32))
        for u in range(unroll):
            c = col_ref[i * unroll + u]
            pre[c] = pre[c] + got[u]
        return carry

    lax.fori_loop(0, slots // unroll, step, 0)
    keep = pltpu.make_async_copy(wu, wu_hbm, out_sem)
    keep.start()

    def turn(r, carry):
        x_t[r] = columns(x_v, r, block).T
        return carry

    lax.fori_loop(0, row_blocks, turn, 0)

    def bend(c, carry):
        value, slope = gelu_pair(pre[c])
        narrow = value.astype(BF16)
        act[c] = narrow
        act_t[c] = narrow.T
        slopes[c] = slope
        return carry

    lax.fori_loop(0, pre.shape[0], bend, 0)
    keep.wait()


def gradient_kernel(n_feat, n_dp, *refs):
    row_ref, col_ref, home_ref, came_ref, kind_ref, place_ref = refs[:6]
    feats = refs[6 : 6 + n_feat]
    down_hbm = refs[6 + n_feat]
    parts = refs[7 + n_feat : 7 + n_feat + n_dp]
    act_t, slopes, x_t = refs[7 + n_feat + n_dp : 10 + n_feat + n_dp]
    outs = refs[10 + n_feat + n_dp :]
    bpre, wd_hbm = outs[:2]
    grad_refs = outs[2 : 2 + n_dp]
    back_v, down_v, down_a, wd, back, stage, feat_sem, in_sem, keep_sem, out_sem = outs[2 + n_dp :]
    slots, block, _ = down_v.shape
    rows = block // n_dp
    nx = n_dp // 2
    chunk = stage.shape[2]
    copies = feature_copies(feats, 1, place_ref, back_v, feat_sem)
    copies += weight_copies(down_hbm, down_v, parts, down_a, place_ref, in_sem)
    for copy in copies:
        copy.start()
    back[...] = jnp.zeros(back.shape, F32)
    for copy in copies:
        copy.wait()
    unroll = math.gcd(slots, IN_UNROLL)

    def backward(i, carry):
        got = []
        for u in range(unroll):
            g = i * unroll + u
            w = weight(down_v, down_a, home_ref, came_ref, kind_ref, g)
            wd[g] = w
            got.append(
                lax.dot_general(
                    columns(back_v, row_ref[g], block), w, (((1,), (1,)), ((), ())), preferred_element_type=F32
                )
            )
        for u in range(unroll):
            c = col_ref[i * unroll + u]
            back[c] = back[c] + got[u]
        return carry

    lax.fori_loop(0, slots // unroll, backward, 0)
    keep = pltpu.make_async_copy(wd, wd_hbm, keep_sem)
    keep.start()

    def bend(c, carry):
        bpre[c] = (back[c] * slopes[c]).astype(BF16)
        return carry

    lax.fori_loop(0, slopes.shape[0], bend, 0)

    def ship(i, slot):
        out = []
        for j in range(nx):
            for other in range(2):
                owner = lax.rem(place_ref[0] + j, nx) * 2 + (place_ref[1] + other) % 2
                start = pl.multiple_of(owner * rows, rows)
                for p in range(2):
                    out.append(
                        pltpu.make_async_copy(
                            stage.at[slot, p, :, pl.ds(start, rows), :],
                            grad_refs[2 * j + other].at[p, pl.ds(i * chunk, chunk)],
                            out_sem.at[slot, 2 * (2 * j + other) + p],
                        )
                    )
        return out

    def last(i, carry):
        slot = lax.rem(i, 2)

        @pl.when(i >= 2)
        def _():
            for copy in ship(i - 2, slot):
                copy.wait()

        for u in range(chunk):
            g = i * chunk + u
            r = row_ref[g]
            c = col_ref[g]
            stage[slot, 0, u] = jnp.dot(x_t[r], bpre[c], preferred_element_type=F32).astype(BF16)
            stage[slot, 1, u] = jnp.dot(
                act_t[c], columns(back_v, r, block), preferred_element_type=F32
            ).astype(BF16)
        for copy in ship(i, slot):
            copy.start()
        return carry

    chunks = slots // chunk
    lax.fori_loop(0, chunks, last, 0)
    for i in range(max(chunks - 2, 0), chunks):
        for copy in ship(i, i % 2):
            copy.wait()
    keep.wait()


def output_kernel(pieces, turned, *refs):
    row_ref, col_ref, place_ref = refs[:3]
    w_hbm, left = refs[3:5]
    outs = refs[5 : 5 + len(pieces)]
    w_v, acc, staged, in_sem, out_sem = refs[5 + len(pieces) :]
    slots, block, _ = w_v.shape
    parts = 4
    some = slots // parts
    loads = []
    for k in range(parts):
        at = pl.ds(k * some, some)
        loads.append(pltpu.make_async_copy(w_hbm.at[at], w_v.at[at], in_sem.at[k]))
    for copy in loads:
        copy.start()
    acc[...] = jnp.zeros(acc.shape, F32)
    unroll = math.gcd(some, OUT_UNROLL)
    dims = (((1,), (1 if turned else 0,)), ((), ()))

    def step(i, carry):
        got = []
        for u in range(unroll):
            g = i * unroll + u
            got.append(lax.dot_general(left[col_ref[g]], w_v[g], dims, preferred_element_type=F32))
        for u in range(unroll):
            r = row_ref[i * unroll + u]
            acc[r] = acc[r] + got[u]
        return carry

    for k in range(parts):
        loads[k].wait()
        lax.fori_loop(k * some // unroll, (k + 1) * some // unroll, step, 0)

    count = staged.shape[0]
    per = staged.shape[2] // block
    bits = count.bit_length() - 1
    for a in range(count):
        if count == 1:
            at = 0
        else:
            far = place_ref[2] ^ a
            at = 0
            for b in range(bits):
                at = at + ((far >> b) & 1) * (count >> (b + 1))
        for q in range(per):
            staged[at, :, q * block : (q + 1) * block] = acc[a * per + q].astype(BF16)
    copies = [
        pltpu.make_async_copy(staged.at[pl.ds(start, size)], out, out_sem.at[k])
        for k, ((start, size), out) in enumerate(zip(pieces, outs))
    ]
    for copy in copies:
        copy.start()
    for copy in copies:
        copy.wait()


VMEM = pl.BlockSpec(memory_space=pltpu.VMEM)
SMEM = pl.BlockSpec(memory_space=pltpu.SMEM)


def cost(flops, size):
    return pl.CostEstimate(flops=flops, transcendentals=0, bytes_accessed=size)


def forward_products(tables, place, feats, up, parts, col_count, row_blocks, feat_shape):
    slots, block, _ = up.shape
    n_dp, n_feat = len(parts), len(feats)
    tokens = feat_shape[1]
    return pl.pallas_call(
        functools.partial(forward_kernel, n_feat, n_dp, row_blocks),
        out_shape=[
            jax.ShapeDtypeStruct((col_count, tokens, block), BF16),
            jax.ShapeDtypeStruct((col_count, block, tokens), BF16),
            jax.ShapeDtypeStruct((col_count, tokens, block), F32),
            jax.ShapeDtypeStruct((row_blocks, block, tokens), BF16),
            jax.ShapeDtypeStruct(up.shape, BF16),
        ],
        in_specs=[SMEM] * 6 + [ANY] * (n_feat + 1 + n_dp),
        out_specs=[VMEM] * 4 + [ANY],
        scratch_shapes=[
            pltpu.VMEM(feat_shape, BF16),
            pltpu.VMEM(up.shape, BF16),
            pltpu.VMEM((n_dp,) + parts[0].shape, BF16),
            pltpu.VMEM(up.shape, BF16),
            pltpu.VMEM((col_count, tokens, block), F32),
            pltpu.SemaphoreType.DMA((n_feat,)),
            pltpu.SemaphoreType.DMA((1 + n_dp,)),
            pltpu.SemaphoreType.DMA,
        ],
        compiler_params=pltpu.CompilerParams(vmem_limit_bytes=VMEM_LIMIT),
        cost_estimate=cost(2 * slots * tokens * block * block, 12 * slots * block * block),
        name="forward_products",
    )(*tables, place, *feats, up, *parts)


def gradient_products(tables, place, feats, down, parts, act_t, slopes, x_t, feat_shape):
    slots, block, _ = down.shape
    n_dp, n_feat = len(parts), len(feats)
    rows = block // n_dp
    chunk = math.gcd(slots, CHUNK)
    tokens = slopes.shape[1]
    grad = jax.ShapeDtypeStruct((2, slots, rows, block), BF16)
    return pl.pallas_call(
        functools.partial(gradient_kernel, n_feat, n_dp),
        out_shape=[jax.ShapeDtypeStruct(slopes.shape, BF16)]
        + [jax.ShapeDtypeStruct(down.shape, BF16)]
        + [grad] * n_dp,
        in_specs=[SMEM] * 6 + [ANY] * (n_feat + 1 + n_dp) + [VMEM] * 3,
        out_specs=[VMEM] + [ANY] * (1 + n_dp),
        scratch_shapes=[
            pltpu.VMEM(feat_shape, BF16),
            pltpu.VMEM(down.shape, BF16),
            pltpu.VMEM((n_dp,) + parts[0].shape, BF16),
            pltpu.VMEM(down.shape, BF16),
            pltpu.VMEM(slopes.shape, F32),
            pltpu.VMEM((2, 2, chunk, block, block), BF16),
            pltpu.SemaphoreType.DMA((n_feat,)),
            pltpu.SemaphoreType.DMA((1 + n_dp,)),
            pltpu.SemaphoreType.DMA,
            pltpu.SemaphoreType.DMA((2, 2 * n_dp)),
        ],
        compiler_params=pltpu.CompilerParams(vmem_limit_bytes=VMEM_LIMIT),
        cost_estimate=cost(6 * slots * tokens * block * block, 20 * slots * block * block),
        name="gradient_products",
    )(*tables, place, *feats, down, *parts, act_t, slopes, x_t)


def output_products(row, col, place, w, left, turned, pieces, feat_shape, row_blocks):
    slots, block, _ = w.shape
    count, tokens, shard = feat_shape
    return pl.pallas_call(
        functools.partial(output_kernel, pieces, turned),
        out_shape=[jax.ShapeDtypeStruct((size, tokens, shard), BF16) for _, size in pieces],
        in_specs=[SMEM] * 3 + [ANY, VMEM],
        out_specs=[ANY] * len(pieces),
        scratch_shapes=[
            pltpu.VMEM(w.shape, BF16),
            pltpu.VMEM((row_blocks, tokens, block), F32),
            pltpu.VMEM((count, tokens, shard), BF16),
            pltpu.SemaphoreType.DMA((4,)),
            pltpu.SemaphoreType.DMA((len(pieces),)),
        ],
        compiler_params=pltpu.CompilerParams(vmem_limit_bytes=VMEM_LIMIT),
        cost_estimate=cost(2 * slots * tokens * block * block, 4 * slots * block * block),
        name="output_products",
    )(row, col, place, w, left)


def adam_step(tables, grads, which, moments, arrived):
    slots, rows, block = moments[0].shape
    n_grads = len(grads)
    n_from = len(arrived)
    bucket = arrived[0].shape[0]
    parts = math.gcd(slots, ADAM_PARTS)
    some = slots // parts

    def kernel(home_ref, came_ref, kind_ref, *refs):
        grad_refs = refs[:n_grads]
        moment_refs = refs[n_grads : n_grads + 2]
        arrived_refs = refs[n_grads + 2 : n_grads + 2 + n_from]
        out_hbm, grad_v, moment_v, arrived_v, out_v, grad_sem, moment_sem, arrived_sem, out_sem = refs[
            n_grads + 2 + n_from :
        ]
        first = [
            pltpu.make_async_copy(moment_refs[k], moment_v.at[k], moment_sem.at[k]) for k in range(2)
        ] + [
            pltpu.make_async_copy(arrived_refs[m], arrived_v.at[pl.ds(m * bucket, bucket)], arrived_sem.at[m])
            for m in range(n_from)
        ]
        later = [
            [
                pltpu.make_async_copy(
                    grad_refs[k].at[which, pl.ds(q * some, some)],
                    grad_v.at[k, pl.ds(q * some, some)],
                    grad_sem.at[q, k],
                )
                for k in range(n_grads)
            ]
            for q in range(parts)
        ]
        outs = [
            pltpu.make_async_copy(
                out_v.at[pl.ds(q * some, some)], out_hbm.at[pl.ds(q * some, some)], out_sem.at[q]
            )
            for q in range(parts)
        ]
        for copy in first + sum(later, []):
            copy.start()

        def step(g, carry):
            at = came_ref[g]
            own = home_ref[g]
            kind = kind_ref[g]

            def moved(k):
                picked = lax.select(kind == 1, moment_v[k, own], arrived_v[at, k].astype(F32))
                return lax.select(kind == 0, jnp.zeros_like(picked), picked)

            total = grad_v[0, g].astype(F32)
            for k in range(1, n_grads):
                total = total + grad_v[k, g].astype(F32)
            first_moment = 0.9 * moved(0) + 0.1 * total
            second_moment = 0.95 * moved(1) + 0.05 * total * total
            out_v[g] = first_moment / (jnp.sqrt(second_moment) + 1.0)
            return carry

        for copy in first:
            copy.wait()
        unroll = math.gcd(some, ADAM_UNROLL)
        for q in range(parts):
            for copy in later[q]:
                copy.wait()

            def trip(i, carry, q=q):
                for u in range(unroll):
                    step(q * some + i * unroll + u, carry)
                return carry

            lax.fori_loop(0, some // unroll, trip, 0)
            outs[q].start()
        for copy in outs:
            copy.wait()

    return pl.pallas_call(
        kernel,
        out_shape=jax.ShapeDtypeStruct(moments[0].shape, F32),
        in_specs=[SMEM] * 3 + [ANY] * (n_grads + 2 + n_from),
        out_specs=ANY,
        scratch_shapes=[
            pltpu.VMEM((n_grads, slots, rows, block), BF16),
            pltpu.VMEM((2, slots, rows, block), F32),
            pltpu.VMEM((n_from * bucket, 2, rows, block), BF16),
            pltpu.VMEM((slots, rows, block), F32),
            pltpu.SemaphoreType.DMA((parts, n_grads)),
            pltpu.SemaphoreType.DMA((2,)),
            pltpu.SemaphoreType.DMA((n_from,)),
            pltpu.SemaphoreType.DMA((parts,)),
        ],
        compiler_params=pltpu.CompilerParams(vmem_limit_bytes=VMEM_LIMIT),
        cost_estimate=cost(15 * slots * rows * block, 17 * slots * rows * block),
        name="adam_step",
    )(*tables, *grads, *moments, *arrived)


def layer(
    activations,
    cotangent,
    up_weight_blocks,
    down_weight_blocks,
    up_first_moment,
    up_second_moment,
    down_first_moment,
    down_second_moment,
    source,
    new_row,
    new_col,
    col_owner,
):
    tensor_size = lax.axis_size("tensor")
    n_dp = lax.axis_size("dp")
    nx = n_dp // 2
    my_index = lax.axis_index("tensor")
    my_dp = lax.axis_index("dp")
    slot_count, block, _ = up_weight_blocks.shape
    rows = block // n_dp
    bucket = (slot_count + tensor_size - 2) // tensor_size

    sources = source.reshape(tensor_size, slot_count)
    is_live = sources >= 0
    sender_dev = jnp.where(is_live, sources // slot_count, -1)
    sender_slot = jnp.where(is_live, sources % slot_count, 0)
    targets = jnp.arange(tensor_size, dtype=jnp.int32)[:, None]
    outgoing = is_live & (sender_dev == my_index) & (targets != my_index)
    out_flags = outgoing.astype(jnp.int32)
    out_rank = jnp.cumsum(out_flags, axis=1) - out_flags
    chosen = outgoing[:, :, None] & (
        out_rank[:, :, None] == jnp.arange(bucket, dtype=jnp.int32)[None, None, :]
    )
    send_slots = jnp.sum(jnp.where(chosen, sender_slot[:, :, None], 0), axis=1).reshape(-1)
    mine_dev = lax.dynamic_index_in_dim(sender_dev, my_index, 0, keepdims=False)
    mine_slot = lax.dynamic_index_in_dim(sender_slot, my_index, 0, keepdims=False)
    mine_live = mine_dev >= 0
    stays = mine_live & (mine_dev == my_index)
    positions = jnp.arange(slot_count, dtype=jnp.int32)
    earlier = (
        (mine_dev[:, None] == mine_dev[None, :])
        & mine_live[None, :]
        & (positions[None, :] < positions[:, None])
    )
    recv_rank = jnp.minimum(jnp.sum(earlier.astype(jnp.int32), axis=1), bucket - 1)
    home = jnp.where(stays, mine_slot, 0)
    came = jnp.where(mine_live & ~stays, mine_dev * bucket + recv_rank, 0)
    kind = jnp.where(stays, 1, jnp.where(mine_live, 2, 0)).astype(jnp.int32)
    col_count = col_owner.shape[0] // tensor_size
    col_slot = jnp.take(local_columns(col_owner), new_col)
    place = jnp.stack([my_dp // 2, my_dp % 2, my_index]).astype(jnp.int32)
    dp_index = my_dp.reshape(1).astype(jnp.int32)
    tables = (new_row, col_slot, home, came, kind)

    def exchange(packed):
        shaped = packed.reshape((tensor_size, bucket) + packed.shape[1:])
        got = lax.all_to_all(shaped, "tensor", split_axis=0, concat_axis=0, tiled=True)
        return got.reshape((tensor_size * bucket,) + packed.shape[1:])

    core_pairs = [(d, d ^ 1) for d in range(n_dp)]

    def x_pairs(j):
        return [(d, ((d // 2 + j) % nx) * 2 + d % 2) for d in range(n_dp)]

    def far_pairs(bit):
        return [(t, t ^ bit) for t in range(tensor_size)]

    def spread(own):
        parts = []
        for j in range(nx):
            mine = own
            if j:
                mine = lax.ppermute(own, "dp", x_pairs(j))
            parts += [mine, lax.ppermute(mine, "dp", core_pairs)]
        return parts

    up_pack = pack_weight(up_weight_blocks, send_slots, dp_index, rows)
    down_pack = pack_weight(down_weight_blocks, send_slots, dp_index, rows)
    up_in = exchange(up_pack)
    down_in = exchange(down_pack)
    up_parts = spread(up_in)
    down_parts = spread(down_in)

    shard = activations.shape[1]
    stacked = shard % block == 0 and tensor_size & (tensor_size - 1) == 0
    if stacked:
        bits = [1 << k for k in reversed(range(tensor_size.bit_length() - 1))]
        held = {0: jnp.stack([activations, cotangent])}
        for bit in bits:
            for m in list(held):
                held[m ^ bit] = lax.ppermute(held[m], "tensor", far_pairs(bit))
        feats = [held[m] for m in range(tensor_size)]
        feat_shape = (tensor_size,) + activations.shape
    else:
        x = lax.all_gather(activations, "tensor", axis=1, tiled=True)
        back = lax.all_gather(cotangent, "tensor", axis=1, tiled=True)
        feats = [jnp.stack([x, back])[:, None].reshape((2,) + x.shape)]
        feat_shape = (1,) + x.shape
    row_blocks = feat_shape[0] * feat_shape[2] // block

    ups = (up_first_moment, up_second_moment)
    downs = (down_first_moment, down_second_moment)
    ups_pack = pack_moments(ups, send_slots)
    downs_pack = pack_moments(downs, send_slots)
    ups_in = [exchange(ups_pack)]
    downs_in = [exchange(downs_pack)]

    act, act_t, slopes, x_t, wu = forward_products(
        tables, place, feats, up_weight_blocks, up_parts, col_count, row_blocks, feat_shape
    )
    bpre, wd, *grads = gradient_products(
        tables, place, feats, down_weight_blocks, down_parts, act_t, slopes, x_t, feat_shape
    )
    terms = []
    for j in range(nx):
        there = lax.ppermute(grads[2 * j + 1], "dp", core_pairs)
        if j == 0:
            terms += [grads[0], there]
        else:
            both = (grads[2 * j].astype(F32) + there.astype(F32)).astype(BF16)
            terms.append(lax.ppermute(both, "dp", x_pairs(j)))

    sums = []
    for w, left, turned in ((wd, act, False), (wu, bpre, True)):
        half = tensor_size // 2
        pieces = ((0, half), (half, half)) if stacked else ((0, 1),)
        got = output_products(
            new_row, col_slot, place, w, left, turned, pieces, feat_shape, row_blocks
        )
        if not stacked:
            sums.append(lax.psum_scatter(got[0][0], "tensor", scatter_dimension=1, tiled=True))
            continue
        held, send = got
        held = [held]
        bit = 1
        while True:
            held.append(lax.ppermute(send, "tensor", far_pairs(bit)))
            bit *= 2
            if bit >= tensor_size:
                break
            half = held[-1].shape[0] // 2
            send = sum(s[half : 2 * half].astype(F32) for s in held).astype(BF16)
            held = [s[:half] for s in held]
        sums.append(sum(s[0].astype(F32) for s in held).astype(BF16))
    out_sum, in_sum = sums

    up_step = adam_step((home, came, kind), terms, 0, ups, ups_in)
    down_step = adam_step((home, came, kind), terms, 1, downs, downs_in)
    return (out_sum, in_sum, up_step, down_step)


def solution(mesh):
    placed = (
        P("dp", "tensor"),
        P("dp", "tensor"),
        P("tensor", None, None),
        P("tensor", None, None),
        P("tensor", "dp", None),
        P("tensor", "dp", None),
        P("tensor", "dp", None),
        P("tensor", "dp", None),
        P(),
        P("tensor"),
        P("tensor"),
        P(),
    )
    return jax.shard_map(
        layer,
        mesh=mesh,
        in_specs=placed,
        out_specs=(
            P("dp", "tensor"),
            P("dp", "tensor"),
            P("tensor", "dp", None),
            P("tensor", "dp", None),
        ),
        check_vma=False,
    )
```

```python
import functools
import math

import jax
import jax.numpy as jnp
from jax import lax
from jax.experimental import pallas as pl
from jax.experimental.pallas import tpu as pltpu
from jax.sharding import PartitionSpec as P


gelu_scale = math.sqrt(2.0 / math.pi)
VMEM_LIMIT = 60 * 1024 * 1024
IN_UNROLL = 32
OUT_UNROLL = 56
CHUNK = 28
ADAM_UNROLL = 8
ADAM_PARTS = 4

F32 = jnp.float32
BF16 = jnp.bfloat16
ANY = pl.BlockSpec(memory_space=pl.ANY)


def gelu_pair(pre_act):
    inner = gelu_scale * (pre_act + 0.044715 * pre_act * pre_act * pre_act)
    tangent = jnp.tanh(inner)
    gelu_value = 0.5 * pre_act * (1.0 + tangent)
    gelu_slope = 0.5 * (1.0 + tangent) + 0.5 * pre_act * (1.0 - tangent * tangent) * gelu_scale * (
        1.0 + 3.0 * 0.044715 * pre_act * pre_act
    )
    return (gelu_value, gelu_slope)


def local_columns(col_owner):
    count_all = col_owner.shape[0]
    order = jnp.arange(count_all, dtype=jnp.int32)
    same = (col_owner[None, :] == col_owner[:, None]) & (order[None, :] < order[:, None])
    return jnp.sum(same.astype(jnp.int32), axis=1)


def pack_weight(tiles, send_slots, dp_index, rows):
    slots, _, width = tiles.shape
    count = send_slots.shape[0]

    def kernel(send_ref, dp_ref, in_ref, out_ref):
        def step(i, carry):
            out_ref[i] = in_ref[send_ref[i]]
            return carry

        lax.fori_loop(0, count, step, 0, unroll=8)

    return pl.pallas_call(
        kernel,
        out_shape=jax.ShapeDtypeStruct((count, rows, width), tiles.dtype),
        grid_spec=pltpu.PrefetchScalarGridSpec(
            num_scalar_prefetch=2,
            grid=(1,),
            in_specs=[pl.BlockSpec((slots, rows, width), lambda i, s, d: (0, d[0], 0))],
            out_specs=pl.BlockSpec((count, rows, width), lambda i, s, d: (0, 0, 0)),
        ),
        compiler_params=pltpu.CompilerParams(vmem_limit_bytes=VMEM_LIMIT),
        cost_estimate=pl.CostEstimate(flops=0, transcendentals=0, bytes_accessed=4 * count * rows * width),
        name="pack_weight",
    )(send_slots, dp_index, tiles)


def pack_moments(arrays, send_slots):
    slots, rows, width = arrays[0].shape
    count = send_slots.shape[0]
    kinds = len(arrays)

    def kernel(send_ref, *refs):
        out_ref = refs[-1]

        def step(i, carry):
            s = send_ref[i]
            for k in range(kinds):
                out_ref[i, k] = refs[k][s].astype(BF16)
            return carry

        lax.fori_loop(0, count, step, 0, unroll=4)

    whole = pl.BlockSpec((slots, rows, width), lambda i, s: (0, 0, 0))
    return pl.pallas_call(
        kernel,
        out_shape=jax.ShapeDtypeStruct((count, kinds, rows, width), BF16),
        grid_spec=pltpu.PrefetchScalarGridSpec(
            num_scalar_prefetch=1,
            grid=(1,),
            in_specs=[whole] * kinds,
            out_specs=pl.BlockSpec((count, kinds, rows, width), lambda i, s: (0, 0, 0, 0)),
        ),
        compiler_params=pltpu.CompilerParams(vmem_limit_bytes=VMEM_LIMIT),
        cost_estimate=pl.CostEstimate(
            flops=0, transcendentals=0, bytes_accessed=6 * kinds * count * rows * width
        ),
        name="pack_moments",
    )(send_slots, *arrays)


def columns(ref, r, block):
    per = ref.shape[2] // block
    a = lax.div(r, per)
    off = pl.multiple_of((r - a * per) * block, block)
    return ref[a, :, pl.ds(off, block)]


def weight(own, came, home_ref, came_ref, kind_ref, g):
    kind = kind_ref[g]
    mine = own[home_ref[g]]
    at = came_ref[g]
    theirs = jnp.concatenate([came[q, at] for q in range(came.shape[0])], axis=0)
    picked = lax.select(kind == 1, mine, theirs)
    return lax.select(kind == 0, jnp.zeros_like(picked), picked)


def feature_copies(parts, place_ref, buf, sem):
    copies = []
    for m, part in enumerate(parts):
        at = (place_ref[2] ^ m) if len(parts) > 1 else 0
        copies.append(pltpu.make_async_copy(part, buf.at[at], sem.at[m]))
    return copies


def weight_copies(own, own_v, parts, parts_v, place_ref, sem):
    n_dp = len(parts)
    nx = n_dp // 2
    copies = [pltpu.make_async_copy(own, own_v, sem.at[0])]
    for j in range(nx):
        for other in range(2):
            k = 2 * j + other
            owner = lax.rem(place_ref[0] + nx - j, nx) * 2 + (place_ref[1] + other) % 2
            copies.append(pltpu.make_async_copy(parts[k], parts_v.at[owner], sem.at[1 + k]))
    return copies


def forward_kernel(n_feat, n_dp, row_blocks, *refs):
    row_ref, col_ref, home_ref, came_ref, kind_ref, place_ref = refs[:6]
    feats = refs[6 : 6 + n_feat]
    up_hbm = refs[6 + n_feat]
    parts = refs[7 + n_feat : 7 + n_feat + n_dp]
    act, act_t, slopes, x_t, wu_hbm, x_v, up_v, up_a, wu, pre, feat_sem, in_sem, out_sem = refs[7 + n_feat + n_dp :]
    slots, block, _ = up_v.shape
    copies = feature_copies(feats, place_ref, x_v, feat_sem)
    copies += weight_copies(up_hbm, up_v, parts, up_a, place_ref, in_sem)
    for copy in copies:
        copy.start()
    pre[...] = jnp.zeros(pre.shape, F32)
    for copy in copies:
        copy.wait()
    unroll = math.gcd(slots, IN_UNROLL)

    def step(i, carry):
        got = []
        for u in range(unroll):
            g = i * unroll + u
            w = weight(up_v, up_a, home_ref, came_ref, kind_ref, g)
            wu[g] = w
            got.append(jnp.dot(columns(x_v, row_ref[g], block), w, preferred_element_type=F32))
        for u in range(unroll):
            c = col_ref[i * unroll + u]
            pre[c] = pre[c] + got[u]
        return carry

    lax.fori_loop(0, slots // unroll, step, 0)
    keep = pltpu.make_async_copy(wu, wu_hbm, out_sem)
    keep.start()

    def turn(r, carry):
        x_t[r] = columns(x_v, r, block).T
        return carry

    lax.fori_loop(0, row_blocks, turn, 0)

    def bend(c, carry):
        value, slope = gelu_pair(pre[c])
        narrow = value.astype(BF16)
        act[c] = narrow
        act_t[c] = narrow.T
        slopes[c] = slope
        return carry

    lax.fori_loop(0, pre.shape[0], bend, 0)
    keep.wait()


def gradient_kernel(n_feat, n_dp, *refs):
    row_ref, col_ref, home_ref, came_ref, kind_ref, place_ref = refs[:6]
    feats = refs[6 : 6 + n_feat]
    down_hbm = refs[6 + n_feat]
    parts = refs[7 + n_feat : 7 + n_feat + n_dp]
    act_t, slopes, x_t = refs[7 + n_feat + n_dp : 10 + n_feat + n_dp]
    outs = refs[10 + n_feat + n_dp :]
    bpre, wd_hbm = outs[:2]
    grad_refs = outs[2 : 2 + n_dp]
    back_v, down_v, down_a, wd, back, stage, feat_sem, in_sem, keep_sem, out_sem = outs[2 + n_dp :]
    slots, block, _ = down_v.shape
    rows = block // n_dp
    nx = n_dp // 2
    chunk = stage.shape[2]
    copies = feature_copies(feats, place_ref, back_v, feat_sem)
    copies += weight_copies(down_hbm, down_v, parts, down_a, place_ref, in_sem)
    for copy in copies:
        copy.start()
    back[...] = jnp.zeros(back.shape, F32)
    for copy in copies:
        copy.wait()
    unroll = math.gcd(slots, IN_UNROLL)

    def backward(i, carry):
        got = []
        for u in range(unroll):
            g = i * unroll + u
            w = weight(down_v, down_a, home_ref, came_ref, kind_ref, g)
            wd[g] = w
            got.append(
                lax.dot_general(
                    columns(back_v, row_ref[g], block), w, (((1,), (1,)), ((), ())), preferred_element_type=F32
                )
            )
        for u in range(unroll):
            c = col_ref[i * unroll + u]
            back[c] = back[c] + got[u]
        return carry

    lax.fori_loop(0, slots // unroll, backward, 0)
    keep = pltpu.make_async_copy(wd, wd_hbm, keep_sem)
    keep.start()

    def bend(c, carry):
        bpre[c] = (back[c] * slopes[c]).astype(BF16)
        return carry

    lax.fori_loop(0, slopes.shape[0], bend, 0)

    def ship(i, slot):
        out = []
        for j in range(nx):
            for other in range(2):
                owner = lax.rem(place_ref[0] + j, nx) * 2 + (place_ref[1] + other) % 2
                start = pl.multiple_of(owner * rows, rows)
                for p in range(2):
                    out.append(
                        pltpu.make_async_copy(
                            stage.at[slot, p, :, pl.ds(start, rows), :],
                            grad_refs[2 * j + other].at[p, pl.ds(i * chunk, chunk)],
                            out_sem.at[slot, 2 * (2 * j + other) + p],
                        )
                    )
        return out

    def last(i, carry):
        slot = lax.rem(i, 2)

        @pl.when(i >= 2)
        def _():
            for copy in ship(i - 2, slot):
                copy.wait()

        for u in range(chunk):
            g = i * chunk + u
            r = row_ref[g]
            c = col_ref[g]
            stage[slot, 0, u] = jnp.dot(x_t[r], bpre[c], preferred_element_type=F32).astype(BF16)
            stage[slot, 1, u] = jnp.dot(
                act_t[c], columns(back_v, r, block), preferred_element_type=F32
            ).astype(BF16)
        for copy in ship(i, slot):
            copy.start()
        return carry

    chunks = slots // chunk
    lax.fori_loop(0, chunks, last, 0)
    for i in range(max(chunks - 2, 0), chunks):
        for copy in ship(i, i % 2):
            copy.wait()
    keep.wait()


def output_kernel(pieces, turned, bits, *refs):
    row_ref, col_ref, place_ref = refs[:3]
    w_hbm, left = refs[3:5]
    outs = refs[5 : 5 + len(pieces)]
    w_v, acc, staged, in_sem, out_sem = refs[5 + len(pieces) :]
    slots, block, _ = w_v.shape
    parts = 4
    some = slots // parts
    loads = []
    for k in range(parts):
        at = pl.ds(k * some, some)
        loads.append(pltpu.make_async_copy(w_hbm.at[at], w_v.at[at], in_sem.at[k]))
    for copy in loads:
        copy.start()
    acc[...] = jnp.zeros(acc.shape, F32)
    unroll = math.gcd(some, OUT_UNROLL)
    dims = (((1,), (1 if turned else 0,)), ((), ()))

    def step(i, carry):
        got = []
        for u in range(unroll):
            g = i * unroll + u
            got.append(lax.dot_general(left[col_ref[g]], w_v[g], dims, preferred_element_type=F32))
        for u in range(unroll):
            r = row_ref[i * unroll + u]
            acc[r] = acc[r] + got[u]
        return carry

    for k in range(parts):
        loads[k].wait()
        lax.fori_loop(k * some // unroll, (k + 1) * some // unroll, step, 0)

    count = staged.shape[0]
    per = staged.shape[2] // block
    for a in range(count):
        if count == 1:
            at = 0
        else:
            far = place_ref[2] ^ a
            at = 0
            for b, bit in enumerate(bits):
                at = at + lax.div(far, bit) % 2 * (count >> (b + 1))
        for q in range(per):
            staged[at, :, q * block : (q + 1) * block] = acc[a * per + q].astype(BF16)
    copies = [
        pltpu.make_async_copy(staged.at[pl.ds(start, size)], out, out_sem.at[k])
        for k, ((start, size), out) in enumerate(zip(pieces, outs))
    ]
    for copy in copies:
        copy.start()
    for copy in copies:
        copy.wait()


VMEM = pl.BlockSpec(memory_space=pltpu.VMEM)
SMEM = pl.BlockSpec(memory_space=pltpu.SMEM)


def cost(flops, size):
    return pl.CostEstimate(flops=flops, transcendentals=0, bytes_accessed=size)


def forward_products(tables, place, feats, up, parts, col_count, row_blocks, feat_shape):
    slots, block, _ = up.shape
    n_dp, n_feat = len(parts), len(feats)
    tokens = feat_shape[1]
    return pl.pallas_call(
        functools.partial(forward_kernel, n_feat, n_dp, row_blocks),
        out_shape=[
            jax.ShapeDtypeStruct((col_count, tokens, block), BF16),
            jax.ShapeDtypeStruct((col_count, block, tokens), BF16),
            jax.ShapeDtypeStruct((col_count, tokens, block), F32),
            jax.ShapeDtypeStruct((row_blocks, block, tokens), BF16),
            jax.ShapeDtypeStruct(up.shape, BF16),
        ],
        in_specs=[SMEM] * 6 + [ANY] * (n_feat + 1 + n_dp),
        out_specs=[VMEM] * 4 + [ANY],
        scratch_shapes=[
            pltpu.VMEM(feat_shape, BF16),
            pltpu.VMEM(up.shape, BF16),
            pltpu.VMEM((n_dp,) + parts[0].shape, BF16),
            pltpu.VMEM(up.shape, BF16),
            pltpu.VMEM((col_count, tokens, block), F32),
            pltpu.SemaphoreType.DMA((n_feat,)),
            pltpu.SemaphoreType.DMA((1 + n_dp,)),
            pltpu.SemaphoreType.DMA,
        ],
        compiler_params=pltpu.CompilerParams(vmem_limit_bytes=VMEM_LIMIT),
        cost_estimate=cost(2 * slots * tokens * block * block, 12 * slots * block * block),
        name="forward_products",
    )(*tables, place, *feats, up, *parts)


def gradient_products(tables, place, feats, down, parts, act_t, slopes, x_t, feat_shape):
    slots, block, _ = down.shape
    n_dp, n_feat = len(parts), len(feats)
    rows = block // n_dp
    chunk = math.gcd(slots, CHUNK)
    tokens = slopes.shape[1]
    grad = jax.ShapeDtypeStruct((2, slots, rows, block), BF16)
    return pl.pallas_call(
        functools.partial(gradient_kernel, n_feat, n_dp),
        out_shape=[jax.ShapeDtypeStruct(slopes.shape, BF16)]
        + [jax.ShapeDtypeStruct(down.shape, BF16)]
        + [grad] * n_dp,
        in_specs=[SMEM] * 6 + [ANY] * (n_feat + 1 + n_dp) + [VMEM] * 3,
        out_specs=[VMEM] + [ANY] * (1 + n_dp),
        scratch_shapes=[
            pltpu.VMEM(feat_shape, BF16),
            pltpu.VMEM(down.shape, BF16),
            pltpu.VMEM((n_dp,) + parts[0].shape, BF16),
            pltpu.VMEM(down.shape, BF16),
            pltpu.VMEM(slopes.shape, F32),
            pltpu.VMEM((2, 2, chunk, block, block), BF16),
            pltpu.SemaphoreType.DMA((n_feat,)),
            pltpu.SemaphoreType.DMA((1 + n_dp,)),
            pltpu.SemaphoreType.DMA,
            pltpu.SemaphoreType.DMA((2, 2 * n_dp)),
        ],
        compiler_params=pltpu.CompilerParams(vmem_limit_bytes=VMEM_LIMIT),
        cost_estimate=cost(6 * slots * tokens * block * block, 20 * slots * block * block),
        name="gradient_products",
    )(*tables, place, *feats, down, *parts, act_t, slopes, x_t)


def output_products(row, col, place, w, left, turned, bits, pieces, feat_shape, row_blocks):
    slots, block, _ = w.shape
    count, tokens, shard = feat_shape
    return pl.pallas_call(
        functools.partial(output_kernel, pieces, turned, bits),
        out_shape=[jax.ShapeDtypeStruct((size, tokens, shard), BF16) for _, size in pieces],
        in_specs=[SMEM] * 3 + [ANY, VMEM],
        out_specs=[ANY] * len(pieces),
        scratch_shapes=[
            pltpu.VMEM(w.shape, BF16),
            pltpu.VMEM((row_blocks, tokens, block), F32),
            pltpu.VMEM((count, tokens, shard), BF16),
            pltpu.SemaphoreType.DMA((4,)),
            pltpu.SemaphoreType.DMA((len(pieces),)),
        ],
        compiler_params=pltpu.CompilerParams(vmem_limit_bytes=VMEM_LIMIT),
        cost_estimate=cost(2 * slots * tokens * block * block, 4 * slots * block * block),
        name="output_products",
    )(row, col, place, w, left)


def adam_step(tables, grads, which, moments, arrived):
    slots, rows, block = moments[0].shape
    n_grads = len(grads)
    n_from = len(arrived)
    bucket = arrived[0].shape[0]
    parts = math.gcd(slots, ADAM_PARTS)
    some = slots // parts

    def kernel(home_ref, came_ref, kind_ref, *refs):
        grad_refs = refs[:n_grads]
        moment_refs = refs[n_grads : n_grads + 2]
        arrived_refs = refs[n_grads + 2 : n_grads + 2 + n_from]
        out_hbm, grad_v, moment_v, arrived_v, out_v, grad_sem, moment_sem, arrived_sem, out_sem = refs[
            n_grads + 2 + n_from :
        ]
        first = [
            pltpu.make_async_copy(moment_refs[k], moment_v.at[k], moment_sem.at[k]) for k in range(2)
        ] + [
            pltpu.make_async_copy(arrived_refs[m], arrived_v.at[pl.ds(m * bucket, bucket)], arrived_sem.at[m])
            for m in range(n_from)
        ]
        later = [
            [
                pltpu.make_async_copy(
                    grad_refs[k].at[which, pl.ds(q * some, some)],
                    grad_v.at[k, pl.ds(q * some, some)],
                    grad_sem.at[q, k],
                )
                for k in range(n_grads)
            ]
            for q in range(parts)
        ]
        outs = [
            pltpu.make_async_copy(
                out_v.at[pl.ds(q * some, some)], out_hbm.at[pl.ds(q * some, some)], out_sem.at[q]
            )
            for q in range(parts)
        ]
        for copy in first + sum(later, []):
            copy.start()

        def step(g, carry):
            at = came_ref[g]
            own = home_ref[g]
            kind = kind_ref[g]

            def moved(k):
                picked = lax.select(kind == 1, moment_v[k, own], arrived_v[at, k].astype(F32))
                return lax.select(kind == 0, jnp.zeros_like(picked), picked)

            total = grad_v[0, g].astype(F32)
            for k in range(1, n_grads):
                total = total + grad_v[k, g].astype(F32)
            first_moment = 0.9 * moved(0) + 0.1 * total
            second_moment = 0.95 * moved(1) + 0.05 * total * total
            out_v[g] = first_moment / (jnp.sqrt(second_moment) + 1.0)
            return carry

        for copy in first:
            copy.wait()
        unroll = math.gcd(some, ADAM_UNROLL)
        for q in range(parts):
            for copy in later[q]:
                copy.wait()

            def trip(i, carry, q=q):
                for u in range(unroll):
                    step(q * some + i * unroll + u, carry)
                return carry

            lax.fori_loop(0, some // unroll, trip, 0)
            outs[q].start()
        for copy in outs:
            copy.wait()

    return pl.pallas_call(
        kernel,
        out_shape=jax.ShapeDtypeStruct(moments[0].shape, F32),
        in_specs=[SMEM] * 3 + [ANY] * (n_grads + 2 + n_from),
        out_specs=ANY,
        scratch_shapes=[
            pltpu.VMEM((n_grads, slots, rows, block), BF16),
            pltpu.VMEM((2, slots, rows, block), F32),
            pltpu.VMEM((n_from * bucket, 2, rows, block), BF16),
            pltpu.VMEM((slots, rows, block), F32),
            pltpu.SemaphoreType.DMA((parts, n_grads)),
            pltpu.SemaphoreType.DMA((2,)),
            pltpu.SemaphoreType.DMA((n_from,)),
            pltpu.SemaphoreType.DMA((parts,)),
        ],
        compiler_params=pltpu.CompilerParams(vmem_limit_bytes=VMEM_LIMIT),
        cost_estimate=cost(15 * slots * rows * block, 17 * slots * rows * block),
        name="adam_step",
    )(*tables, *grads, *moments, *arrived)


def layer(
    activations,
    cotangent,
    up_weight_blocks,
    down_weight_blocks,
    up_first_moment,
    up_second_moment,
    down_first_moment,
    down_second_moment,
    source,
    new_row,
    new_col,
    col_owner,
):
    tensor_size = lax.axis_size("tensor")
    n_dp = lax.axis_size("dp")
    nx = n_dp // 2
    my_index = lax.axis_index("tensor")
    my_dp = lax.axis_index("dp")
    slot_count, block, _ = up_weight_blocks.shape
    rows = block // n_dp
    bucket = (slot_count + tensor_size - 2) // tensor_size

    sources = source.reshape(tensor_size, slot_count)
    is_live = sources >= 0
    sender_dev = jnp.where(is_live, sources // slot_count, -1)
    sender_slot = jnp.where(is_live, sources % slot_count, 0)
    targets = jnp.arange(tensor_size, dtype=jnp.int32)[:, None]
    outgoing = is_live & (sender_dev == my_index) & (targets != my_index)
    out_flags = outgoing.astype(jnp.int32)
    out_rank = jnp.cumsum(out_flags, axis=1) - out_flags
    chosen = outgoing[:, :, None] & (
        out_rank[:, :, None] == jnp.arange(bucket, dtype=jnp.int32)[None, None, :]
    )
    send_slots = jnp.sum(jnp.where(chosen, sender_slot[:, :, None], 0), axis=1).reshape(-1)
    mine_dev = lax.dynamic_index_in_dim(sender_dev, my_index, 0, keepdims=False)
    mine_slot = lax.dynamic_index_in_dim(sender_slot, my_index, 0, keepdims=False)
    mine_live = mine_dev >= 0
    stays = mine_live & (mine_dev == my_index)
    positions = jnp.arange(slot_count, dtype=jnp.int32)
    earlier = (
        (mine_dev[:, None] == mine_dev[None, :])
        & mine_live[None, :]
        & (positions[None, :] < positions[:, None])
    )
    recv_rank = jnp.minimum(jnp.sum(earlier.astype(jnp.int32), axis=1), bucket - 1)
    home = jnp.where(stays, mine_slot, 0)
    came = jnp.where(mine_live & ~stays, mine_dev * bucket + recv_rank, 0)
    kind = jnp.where(stays, 1, jnp.where(mine_live, 2, 0)).astype(jnp.int32)
    col_count = col_owner.shape[0] // tensor_size
    col_slot = jnp.take(local_columns(col_owner), new_col)
    place = jnp.stack([my_dp // 2, my_dp % 2, my_index]).astype(jnp.int32)
    dp_index = my_dp.reshape(1).astype(jnp.int32)
    tables = (new_row, col_slot, home, came, kind)

    def exchange(packed):
        shaped = packed.reshape((tensor_size, bucket) + packed.shape[1:])
        got = lax.all_to_all(shaped, "tensor", split_axis=0, concat_axis=0, tiled=True)
        return got.reshape((tensor_size * bucket,) + packed.shape[1:])

    core_pairs = [(d, d ^ 1) for d in range(n_dp)]

    def x_pairs(j):
        return [(d, ((d // 2 + j) % nx) * 2 + d % 2) for d in range(n_dp)]

    def far_pairs(bit):
        return [(t, t ^ bit) for t in range(tensor_size)]

    def spread(own):
        parts = []
        for j in range(nx):
            mine = own
            if j:
                mine = lax.ppermute(own, "dp", x_pairs(j))
            parts += [mine, lax.ppermute(mine, "dp", core_pairs)]
        return parts

    up_pack = pack_weight(up_weight_blocks, send_slots, dp_index, rows)
    later_slots, tables, place = lax.optimization_barrier((send_slots, tables, place))
    new_row, col_slot, home, came, kind = tables
    down_pack = pack_weight(down_weight_blocks, later_slots, dp_index, rows)
    up_in = exchange(up_pack)
    down_in = exchange(down_pack)
    up_parts = spread(up_in)
    down_parts = spread(down_in)

    shard = activations.shape[1]
    stacked = shard % block == 0 and tensor_size & (tensor_size - 1) == 0
    if stacked:
        bits = [1 << k for k in reversed(range(tensor_size.bit_length() - 1))]

        def gather(own):
            held = {0: own}
            for bit in bits:
                for m in list(held):
                    held[m ^ bit] = lax.ppermute(held[m], "tensor", far_pairs(bit))
            return [held[m] for m in range(tensor_size)]

        feats = gather(activations)
        backs = gather(cotangent)
        feat_shape = (tensor_size,) + activations.shape
    else:
        feats = [lax.all_gather(activations, "tensor", axis=1, tiled=True)]
        backs = [lax.all_gather(cotangent, "tensor", axis=1, tiled=True)]
        feat_shape = (1,) + feats[0].shape
    row_blocks = feat_shape[0] * feat_shape[2] // block

    ups = (up_first_moment, up_second_moment)
    downs = (down_first_moment, down_second_moment)
    ups_pack = pack_moments(ups, send_slots)
    downs_pack = pack_moments(downs, send_slots)
    ups_in = [exchange(ups_pack)]
    downs_in = [exchange(downs_pack)]

    act, act_t, slopes, x_t, wu = forward_products(
        tables, place, feats, up_weight_blocks, up_parts, col_count, row_blocks, feat_shape
    )
    bpre, wd, *grads = gradient_products(
        tables, place, backs, down_weight_blocks, down_parts, act_t, slopes, x_t, feat_shape
    )
    terms = []
    for j in range(nx):
        there = lax.ppermute(grads[2 * j + 1], "dp", core_pairs)
        if j == 0:
            terms += [grads[0], there]
        else:
            both = (grads[2 * j].astype(F32) + there.astype(F32)).astype(BF16)
            terms.append(lax.ppermute(both, "dp", x_pairs(j)))

    sums = []
    near = [1 << k for k in range(tensor_size.bit_length() - 1)] if stacked else []
    swapped = near[1::-1] + near[2:]
    for w, left, turned, order in ((wd, act, False, near), (wu, bpre, True, swapped)):
        half = tensor_size // 2
        pieces = ((0, half), (half, half)) if stacked else ((0, 1),)
        got = output_products(
            new_row, col_slot, place, w, left, turned, order, pieces, feat_shape, row_blocks
        )
        if not stacked:
            sums.append(lax.psum_scatter(got[0][0], "tensor", scatter_dimension=1, tiled=True))
            continue
        held, send = got
        held = [held]
        for step, bit in enumerate(order):
            if step:
                half = held[-1].shape[0] // 2
                send = sum(s[half : 2 * half].astype(F32) for s in held).astype(BF16)
                held = [s[:half] for s in held]
            held.append(lax.ppermute(send, "tensor", far_pairs(bit)))
        sums.append(sum(s[0].astype(F32) for s in held).astype(BF16))
    out_sum, in_sum = sums

    up_step = adam_step((home, came, kind), terms, 0, ups, ups_in)
    down_step = adam_step((home, came, kind), terms, 1, downs, downs_in)
    return (out_sum, in_sum, up_step, down_step)


def solution(mesh):
    placed = (
        P("dp", "tensor"),
        P("dp", "tensor"),
        P("tensor", None, None),
        P("tensor", None, None),
        P("tensor", "dp", None),
        P("tensor", "dp", None),
        P("tensor", "dp", None),
        P("tensor", "dp", None),
        P(),
        P("tensor"),
        P("tensor"),
        P(),
    )
    return jax.shard_map(
        layer,
        mesh=mesh,
        in_specs=placed,
        out_specs=(
            P("dp", "tensor"),
            P("dp", "tensor"),
            P("tensor", "dp", None),
            P("tensor", "dp", None),
        ),
        check_vma=False,
    )
```

```python
import functools
import math

import jax
import jax.numpy as jnp
from jax import lax
from jax.experimental import pallas as pl
from jax.experimental.pallas import tpu as pltpu
from jax.sharding import PartitionSpec as P


gelu_scale = math.sqrt(2.0 / math.pi)
VMEM_LIMIT = 60 * 1024 * 1024
IN_UNROLL = 32
OUT_UNROLL = 56
CHUNK = 28
ADAM_UNROLL = 8
ADAM_PARTS = 4

F32 = jnp.float32
BF16 = jnp.bfloat16
ANY = pl.BlockSpec(memory_space=pl.ANY)


def gelu_pair(pre_act):
    inner = gelu_scale * (pre_act + 0.044715 * pre_act * pre_act * pre_act)
    tangent = jnp.tanh(inner)
    gelu_value = 0.5 * pre_act * (1.0 + tangent)
    gelu_slope = 0.5 * (1.0 + tangent) + 0.5 * pre_act * (1.0 - tangent * tangent) * gelu_scale * (
        1.0 + 3.0 * 0.044715 * pre_act * pre_act
    )
    return (gelu_value, gelu_slope)


def local_columns(col_owner):
    count_all = col_owner.shape[0]
    order = jnp.arange(count_all, dtype=jnp.int32)
    same = (col_owner[None, :] == col_owner[:, None]) & (order[None, :] < order[:, None])
    return jnp.sum(same.astype(jnp.int32), axis=1)


def pack_weight(tiles, send_slots, dp_index, rows):
    slots, _, width = tiles.shape
    count = send_slots.shape[0]

    def kernel(send_ref, dp_ref, in_ref, out_ref):
        def step(i, carry):
            out_ref[i] = in_ref[send_ref[i]]
            return carry

        lax.fori_loop(0, count, step, 0, unroll=8)

    return pl.pallas_call(
        kernel,
        out_shape=jax.ShapeDtypeStruct((count, rows, width), tiles.dtype),
        grid_spec=pltpu.PrefetchScalarGridSpec(
            num_scalar_prefetch=2,
            grid=(1,),
            in_specs=[pl.BlockSpec((slots, rows, width), lambda i, s, d: (0, d[0], 0))],
            out_specs=pl.BlockSpec((count, rows, width), lambda i, s, d: (0, 0, 0)),
        ),
        compiler_params=pltpu.CompilerParams(vmem_limit_bytes=VMEM_LIMIT),
        cost_estimate=pl.CostEstimate(flops=0, transcendentals=0, bytes_accessed=4 * count * rows * width),
        name="pack_weight",
    )(send_slots, dp_index, tiles)


def pack_moments(arrays, send_slots):
    slots, rows, width = arrays[0].shape
    count = send_slots.shape[0]
    kinds = len(arrays)

    def kernel(send_ref, *refs):
        out_ref = refs[-1]

        def step(i, carry):
            s = send_ref[i]
            for k in range(kinds):
                out_ref[i, k] = refs[k][s].astype(BF16)
            return carry

        lax.fori_loop(0, count, step, 0, unroll=4)

    whole = pl.BlockSpec((slots, rows, width), lambda i, s: (0, 0, 0))
    return pl.pallas_call(
        kernel,
        out_shape=jax.ShapeDtypeStruct((count, kinds, rows, width), BF16),
        grid_spec=pltpu.PrefetchScalarGridSpec(
            num_scalar_prefetch=1,
            grid=(1,),
            in_specs=[whole] * kinds,
            out_specs=pl.BlockSpec((count, kinds, rows, width), lambda i, s: (0, 0, 0, 0)),
        ),
        compiler_params=pltpu.CompilerParams(vmem_limit_bytes=VMEM_LIMIT),
        cost_estimate=pl.CostEstimate(
            flops=0, transcendentals=0, bytes_accessed=6 * kinds * count * rows * width
        ),
        name="pack_moments",
    )(send_slots, *arrays)


def columns(ref, r, block):
    per = ref.shape[2] // block
    a = lax.div(r, per)
    off = pl.multiple_of((r - a * per) * block, block)
    return ref[a, :, pl.ds(off, block)]


def weight(own, came, home_ref, came_ref, kind_ref, g):
    kind = kind_ref[g]
    mine = own[home_ref[g]]
    at = came_ref[g]
    theirs = jnp.concatenate([came[q, at] for q in range(came.shape[0])], axis=0)
    picked = lax.select(kind == 1, mine, theirs)
    return lax.select(kind == 0, jnp.zeros_like(picked), picked)


def feature_copies(parts, place_ref, buf, sem):
    copies = []
    for m, part in enumerate(parts):
        at = (place_ref[2] ^ m) if len(parts) > 1 else 0
        copies.append(pltpu.make_async_copy(part, buf.at[at], sem.at[m]))
    return copies


def weight_copies(own, own_v, parts, parts_v, place_ref, sem):
    n_dp = len(parts)
    nx = n_dp // 2
    copies = [pltpu.make_async_copy(own, own_v, sem.at[0])]
    for j in range(nx):
        for other in range(2):
            k = 2 * j + other
            owner = lax.rem(place_ref[0] + nx - j, nx) * 2 + (place_ref[1] + other) % 2
            copies.append(pltpu.make_async_copy(parts[k], parts_v.at[owner], sem.at[1 + k]))
    return copies


def forward_kernel(n_feat, n_dp, row_blocks, *refs):
    row_ref, col_ref, home_ref, came_ref, kind_ref, place_ref = refs[:6]
    feats = refs[6 : 6 + n_feat]
    up_hbm = refs[6 + n_feat]
    parts = refs[7 + n_feat : 7 + n_feat + n_dp]
    act, act_t, slopes, x_t, wu_hbm, x_v, up_v, up_a, wu, pre, feat_sem, in_sem, out_sem = refs[7 + n_feat + n_dp :]
    slots, block, _ = up_v.shape
    copies = feature_copies(feats, place_ref, x_v, feat_sem)
    copies += weight_copies(up_hbm, up_v, parts, up_a, place_ref, in_sem)
    for copy in copies:
        copy.start()
    pre[...] = jnp.zeros(pre.shape, F32)
    for copy in copies:
        copy.wait()
    unroll = math.gcd(slots, IN_UNROLL)

    def step(i, carry):
        got = []
        for u in range(unroll):
            g = i * unroll + u
            w = weight(up_v, up_a, home_ref, came_ref, kind_ref, g)
            wu[g] = w
            got.append(jnp.dot(columns(x_v, row_ref[g], block), w, preferred_element_type=F32))
        for u in range(unroll):
            c = col_ref[i * unroll + u]
            pre[c] = pre[c] + got[u]
        return carry

    lax.fori_loop(0, slots // unroll, step, 0)
    keep = pltpu.make_async_copy(wu, wu_hbm, out_sem)
    keep.start()

    def turn(r, carry):
        x_t[r] = columns(x_v, r, block).T
        return carry

    lax.fori_loop(0, row_blocks, turn, 0)

    def bend(c, carry):
        value, slope = gelu_pair(pre[c])
        narrow = value.astype(BF16)
        act[c] = narrow
        act_t[c] = narrow.T
        slopes[c] = slope
        return carry

    lax.fori_loop(0, pre.shape[0], bend, 0)
    keep.wait()


def back_kernel(n_feat, n_dp, *refs):
    row_ref, col_ref, home_ref, came_ref, kind_ref, place_ref = refs[:6]
    feats = refs[6 : 6 + n_feat]
    down_hbm = refs[6 + n_feat]
    parts = refs[7 + n_feat : 7 + n_feat + n_dp]
    slopes, bpre, wd_hbm, back_v, down_v, down_a, wd, back, feat_sem, in_sem, keep_sem = refs[7 + n_feat + n_dp :]
    slots, block, _ = down_v.shape
    copies = feature_copies(feats, place_ref, back_v, feat_sem)
    copies += weight_copies(down_hbm, down_v, parts, down_a, place_ref, in_sem)
    for copy in copies:
        copy.start()
    back[...] = jnp.zeros(back.shape, F32)
    for copy in copies:
        copy.wait()
    unroll = math.gcd(slots, IN_UNROLL)

    def backward(i, carry):
        got = []
        for u in range(unroll):
            g = i * unroll + u
            w = weight(down_v, down_a, home_ref, came_ref, kind_ref, g)
            wd[g] = w
            got.append(
                lax.dot_general(
                    columns(back_v, row_ref[g], block), w, (((1,), (1,)), ((), ())), preferred_element_type=F32
                )
            )
        for u in range(unroll):
            c = col_ref[i * unroll + u]
            back[c] = back[c] + got[u]
        return carry

    lax.fori_loop(0, slots // unroll, backward, 0)
    keep = pltpu.make_async_copy(wd, wd_hbm, keep_sem)
    keep.start()

    def bend(c, carry):
        bpre[c] = (back[c] * slopes[c]).astype(BF16)
        return carry

    lax.fori_loop(0, slopes.shape[0], bend, 0)
    keep.wait()


def gradient_kernel(n_feat, n_dp, *refs):
    row_ref, col_ref, place_ref = refs[:3]
    feats = refs[3 : 3 + n_feat]
    left = refs[3 + n_feat]
    right = None if n_feat else refs[4]
    start = 4 + n_feat if n_feat else 5
    grad_refs = refs[start : start + n_dp]
    stage, out_sem = refs[start + n_dp : start + n_dp + 2]
    slots = row_ref.shape[0]
    chunk, block = stage.shape[1:3]
    rows = block // n_dp
    nx = n_dp // 2
    if n_feat:
        back_v, feat_sem = refs[start + n_dp + 2 :]
        copies = feature_copies(feats, place_ref, back_v, feat_sem)
        for copy in copies:
            copy.start()
        for copy in copies:
            copy.wait()

    def ship(i, slot):
        out = []
        for j in range(nx):
            for other in range(2):
                owner = lax.rem(place_ref[0] + j, nx) * 2 + (place_ref[1] + other) % 2
                at = pl.multiple_of(owner * rows, rows)
                out.append(
                    pltpu.make_async_copy(
                        stage.at[slot, :, pl.ds(at, rows), :],
                        grad_refs[2 * j + other].at[pl.ds(i * chunk, chunk)],
                        out_sem.at[slot, 2 * j + other],
                    )
                )
        return out

    def step(i, carry):
        slot = lax.rem(i, 2)

        @pl.when(i >= 2)
        def _():
            for copy in ship(i - 2, slot):
                copy.wait()

        for u in range(chunk):
            g = i * chunk + u
            r = row_ref[g]
            c = col_ref[g]
            if n_feat:
                product = jnp.dot(left[c], columns(back_v, r, block), preferred_element_type=F32)
            else:
                product = jnp.dot(left[r], right[c], preferred_element_type=F32)
            stage[slot, u] = product.astype(BF16)
        for copy in ship(i, slot):
            copy.start()
        return carry

    chunks = slots // chunk
    lax.fori_loop(0, chunks, step, 0)
    for i in range(max(chunks - 2, 0), chunks):
        for copy in ship(i, i % 2):
            copy.wait()


def output_kernel(pieces, turned, bits, *refs):
    row_ref, col_ref, place_ref = refs[:3]
    w_hbm, left = refs[3:5]
    outs = refs[5 : 5 + len(pieces)]
    w_v, acc, staged, in_sem, out_sem = refs[5 + len(pieces) :]
    slots, block, _ = w_v.shape
    parts = 4
    some = slots // parts
    loads = []
    for k in range(parts):
        at = pl.ds(k * some, some)
        loads.append(pltpu.make_async_copy(w_hbm.at[at], w_v.at[at], in_sem.at[k]))
    for copy in loads:
        copy.start()
    acc[...] = jnp.zeros(acc.shape, F32)
    unroll = math.gcd(some, OUT_UNROLL)
    dims = (((1,), (1 if turned else 0,)), ((), ()))

    def step(i, carry):
        got = []
        for u in range(unroll):
            g = i * unroll + u
            got.append(lax.dot_general(left[col_ref[g]], w_v[g], dims, preferred_element_type=F32))
        for u in range(unroll):
            r = row_ref[i * unroll + u]
            acc[r] = acc[r] + got[u]
        return carry

    for k in range(parts):
        loads[k].wait()
        lax.fori_loop(k * some // unroll, (k + 1) * some // unroll, step, 0)

    count = staged.shape[0]
    per = staged.shape[2] // block
    for a in range(count):
        if count == 1:
            at = 0
        else:
            far = place_ref[2] ^ a
            at = 0
            for b, bit in enumerate(bits):
                at = at + lax.div(far, bit) % 2 * (count >> (b + 1))
        for q in range(per):
            staged[at, :, q * block : (q + 1) * block] = acc[a * per + q].astype(BF16)
    copies = [
        pltpu.make_async_copy(staged.at[pl.ds(start, size)], out, out_sem.at[k])
        for k, ((start, size), out) in enumerate(zip(pieces, outs))
    ]
    for copy in copies:
        copy.start()
    for copy in copies:
        copy.wait()


VMEM = pl.BlockSpec(memory_space=pltpu.VMEM)
SMEM = pl.BlockSpec(memory_space=pltpu.SMEM)


def cost(flops, size):
    return pl.CostEstimate(flops=flops, transcendentals=0, bytes_accessed=size)


def forward_products(tables, place, feats, up, parts, col_count, row_blocks, feat_shape):
    slots, block, _ = up.shape
    n_dp, n_feat = len(parts), len(feats)
    tokens = feat_shape[1]
    return pl.pallas_call(
        functools.partial(forward_kernel, n_feat, n_dp, row_blocks),
        out_shape=[
            jax.ShapeDtypeStruct((col_count, tokens, block), BF16),
            jax.ShapeDtypeStruct((col_count, block, tokens), BF16),
            jax.ShapeDtypeStruct((col_count, tokens, block), F32),
            jax.ShapeDtypeStruct((row_blocks, block, tokens), BF16),
            jax.ShapeDtypeStruct(up.shape, BF16),
        ],
        in_specs=[SMEM] * 6 + [ANY] * (n_feat + 1 + n_dp),
        out_specs=[VMEM] * 4 + [ANY],
        scratch_shapes=[
            pltpu.VMEM(feat_shape, BF16),
            pltpu.VMEM(up.shape, BF16),
            pltpu.VMEM((n_dp,) + parts[0].shape, BF16),
            pltpu.VMEM(up.shape, BF16),
            pltpu.VMEM((col_count, tokens, block), F32),
            pltpu.SemaphoreType.DMA((n_feat,)),
            pltpu.SemaphoreType.DMA((1 + n_dp,)),
            pltpu.SemaphoreType.DMA,
        ],
        compiler_params=pltpu.CompilerParams(vmem_limit_bytes=VMEM_LIMIT),
        cost_estimate=cost(2 * slots * tokens * block * block, 12 * slots * block * block),
        name="forward_products",
    )(*tables, place, *feats, up, *parts)


def back_products(tables, place, feats, down, parts, slopes, feat_shape):
    slots, block, _ = down.shape
    n_dp, n_feat = len(parts), len(feats)
    tokens = slopes.shape[1]
    return pl.pallas_call(
        functools.partial(back_kernel, n_feat, n_dp),
        out_shape=[jax.ShapeDtypeStruct(slopes.shape, BF16), jax.ShapeDtypeStruct(down.shape, BF16)],
        in_specs=[SMEM] * 6 + [ANY] * (n_feat + 1 + n_dp) + [VMEM],
        out_specs=[VMEM, ANY],
        scratch_shapes=[
            pltpu.VMEM(feat_shape, BF16),
            pltpu.VMEM(down.shape, BF16),
            pltpu.VMEM((n_dp,) + parts[0].shape, BF16),
            pltpu.VMEM(down.shape, BF16),
            pltpu.VMEM(slopes.shape, F32),
            pltpu.SemaphoreType.DMA((n_feat,)),
            pltpu.SemaphoreType.DMA((1 + n_dp,)),
            pltpu.SemaphoreType.DMA,
        ],
        compiler_params=pltpu.CompilerParams(vmem_limit_bytes=VMEM_LIMIT),
        cost_estimate=cost(2 * slots * tokens * block * block, 12 * slots * block * block),
        name="back_products",
    )(*tables, place, *feats, down, *parts, slopes)


def gradient_products(row, col, place, feats, blocks, n_dp, block, feat_shape):
    slots = row.shape[0]
    n_feat = len(feats)
    chunk = math.gcd(slots, CHUNK)
    tokens = feat_shape[1]
    extra = [pltpu.VMEM(feat_shape, BF16), pltpu.SemaphoreType.DMA((n_feat,))] if n_feat else []
    return pl.pallas_call(
        functools.partial(gradient_kernel, n_feat, n_dp),
        out_shape=[jax.ShapeDtypeStruct((slots, block // n_dp, block), BF16)] * n_dp,
        in_specs=[SMEM] * 3 + [ANY] * n_feat + [VMEM] * len(blocks),
        out_specs=[ANY] * n_dp,
        scratch_shapes=[
            pltpu.VMEM((2, chunk, block, block), BF16),
            pltpu.SemaphoreType.DMA((2, n_dp)),
        ]
        + extra,
        compiler_params=pltpu.CompilerParams(vmem_limit_bytes=VMEM_LIMIT),
        cost_estimate=cost(2 * slots * tokens * block * block, 3 * slots * block * block),
        name="gradient_products",
    )(row, col, place, *feats, *blocks)


def output_products(row, col, place, w, left, turned, bits, pieces, feat_shape, row_blocks):
    slots, block, _ = w.shape
    count, tokens, shard = feat_shape
    return pl.pallas_call(
        functools.partial(output_kernel, pieces, turned, bits),
        out_shape=[jax.ShapeDtypeStruct((size, tokens, shard), BF16) for _, size in pieces],
        in_specs=[SMEM] * 3 + [ANY, VMEM],
        out_specs=[ANY] * len(pieces),
        scratch_shapes=[
            pltpu.VMEM(w.shape, BF16),
            pltpu.VMEM((row_blocks, tokens, block), F32),
            pltpu.VMEM((count, tokens, shard), BF16),
            pltpu.SemaphoreType.DMA((4,)),
            pltpu.SemaphoreType.DMA((len(pieces),)),
        ],
        compiler_params=pltpu.CompilerParams(vmem_limit_bytes=VMEM_LIMIT),
        cost_estimate=cost(2 * slots * tokens * block * block, 4 * slots * block * block),
        name="output_products",
    )(row, col, place, w, left)


def adam_step(tables, grads, moments, arrived):
    slots, rows, block = moments[0].shape
    n_grads = len(grads)
    n_from = len(arrived)
    bucket = arrived[0].shape[0]
    parts = math.gcd(slots, ADAM_PARTS)
    some = slots // parts

    def kernel(home_ref, came_ref, kind_ref, *refs):
        grad_refs = refs[:n_grads]
        moment_refs = refs[n_grads : n_grads + 2]
        arrived_refs = refs[n_grads + 2 : n_grads + 2 + n_from]
        out_hbm, grad_v, moment_v, arrived_v, out_v, grad_sem, moment_sem, arrived_sem, out_sem = refs[
            n_grads + 2 + n_from :
        ]
        first = [
            pltpu.make_async_copy(moment_refs[k], moment_v.at[k], moment_sem.at[k]) for k in range(2)
        ] + [
            pltpu.make_async_copy(arrived_refs[m], arrived_v.at[pl.ds(m * bucket, bucket)], arrived_sem.at[m])
            for m in range(n_from)
        ]
        later = [
            [
                pltpu.make_async_copy(
                    grad_refs[k].at[pl.ds(q * some, some)],
                    grad_v.at[k, pl.ds(q * some, some)],
                    grad_sem.at[q, k],
                )
                for k in range(n_grads)
            ]
            for q in range(parts)
        ]
        outs = [
            pltpu.make_async_copy(
                out_v.at[pl.ds(q * some, some)], out_hbm.at[pl.ds(q * some, some)], out_sem.at[q]
            )
            for q in range(parts)
        ]
        for copy in first + sum(later, []):
            copy.start()

        def step(g, carry):
            at = came_ref[g]
            own = home_ref[g]
            kind = kind_ref[g]

            def moved(k):
                picked = lax.select(kind == 1, moment_v[k, own], arrived_v[at, k].astype(F32))
                return lax.select(kind == 0, jnp.zeros_like(picked), picked)

            total = grad_v[0, g].astype(F32)
            for k in range(1, n_grads):
                total = total + grad_v[k, g].astype(F32)
            first_moment = 0.9 * moved(0) + 0.1 * total
            second_moment = 0.95 * moved(1) + 0.05 * total * total
            out_v[g] = first_moment / (jnp.sqrt(second_moment) + 1.0)
            return carry

        for copy in first:
            copy.wait()
        unroll = math.gcd(some, ADAM_UNROLL)
        for q in range(parts):
            for copy in later[q]:
                copy.wait()

            def trip(i, carry, q=q):
                for u in range(unroll):
                    step(q * some + i * unroll + u, carry)
                return carry

            lax.fori_loop(0, some // unroll, trip, 0)
            outs[q].start()
        for copy in outs:
            copy.wait()

    return pl.pallas_call(
        kernel,
        out_shape=jax.ShapeDtypeStruct(moments[0].shape, F32),
        in_specs=[SMEM] * 3 + [ANY] * (n_grads + 2 + n_from),
        out_specs=ANY,
        scratch_shapes=[
            pltpu.VMEM((n_grads, slots, rows, block), BF16),
            pltpu.VMEM((2, slots, rows, block), F32),
            pltpu.VMEM((n_from * bucket, 2, rows, block), BF16),
            pltpu.VMEM((slots, rows, block), F32),
            pltpu.SemaphoreType.DMA((parts, n_grads)),
            pltpu.SemaphoreType.DMA((2,)),
            pltpu.SemaphoreType.DMA((n_from,)),
            pltpu.SemaphoreType.DMA((parts,)),
        ],
        compiler_params=pltpu.CompilerParams(vmem_limit_bytes=VMEM_LIMIT),
        cost_estimate=cost(15 * slots * rows * block, 17 * slots * rows * block),
        name="adam_step",
    )(*tables, *grads, *moments, *arrived)


def layer(
    activations,
    cotangent,
    up_weight_blocks,
    down_weight_blocks,
    up_first_moment,
    up_second_moment,
    down_first_moment,
    down_second_moment,
    source,
    new_row,
    new_col,
    col_owner,
):
    tensor_size = lax.axis_size("tensor")
    n_dp = lax.axis_size("dp")
    nx = n_dp // 2
    my_index = lax.axis_index("tensor")
    my_dp = lax.axis_index("dp")
    slot_count, block, _ = up_weight_blocks.shape
    rows = block // n_dp
    bucket = (slot_count + tensor_size - 2) // tensor_size

    sources = source.reshape(tensor_size, slot_count)
    is_live = sources >= 0
    sender_dev = jnp.where(is_live, sources // slot_count, -1)
    sender_slot = jnp.where(is_live, sources % slot_count, 0)
    targets = jnp.arange(tensor_size, dtype=jnp.int32)[:, None]
    outgoing = is_live & (sender_dev == my_index) & (targets != my_index)
    out_flags = outgoing.astype(jnp.int32)
    out_rank = jnp.cumsum(out_flags, axis=1) - out_flags
    chosen = outgoing[:, :, None] & (
        out_rank[:, :, None] == jnp.arange(bucket, dtype=jnp.int32)[None, None, :]
    )
    send_slots = jnp.sum(jnp.where(chosen, sender_slot[:, :, None], 0), axis=1).reshape(-1)
    mine_dev = lax.dynamic_index_in_dim(sender_dev, my_index, 0, keepdims=False)
    mine_slot = lax.dynamic_index_in_dim(sender_slot, my_index, 0, keepdims=False)
    mine_live = mine_dev >= 0
    stays = mine_live & (mine_dev == my_index)
    positions = jnp.arange(slot_count, dtype=jnp.int32)
    earlier = (
        (mine_dev[:, None] == mine_dev[None, :])
        & mine_live[None, :]
        & (positions[None, :] < positions[:, None])
    )
    recv_rank = jnp.minimum(jnp.sum(earlier.astype(jnp.int32), axis=1), bucket - 1)
    home = jnp.where(stays, mine_slot, 0)
    came = jnp.where(mine_live & ~stays, mine_dev * bucket + recv_rank, 0)
    kind = jnp.where(stays, 1, jnp.where(mine_live, 2, 0)).astype(jnp.int32)
    col_count = col_owner.shape[0] // tensor_size
    col_slot = jnp.take(local_columns(col_owner), new_col)
    place = jnp.stack([my_dp // 2, my_dp % 2, my_index]).astype(jnp.int32)
    dp_index = my_dp.reshape(1).astype(jnp.int32)
    tables = (new_row, col_slot, home, came, kind)

    def exchange(packed):
        shaped = packed.reshape((tensor_size, bucket) + packed.shape[1:])
        got = lax.all_to_all(shaped, "tensor", split_axis=0, concat_axis=0, tiled=True)
        return got.reshape((tensor_size * bucket,) + packed.shape[1:])

    core_pairs = [(d, d ^ 1) for d in range(n_dp)]

    def x_pairs(j):
        return [(d, ((d // 2 + j) % nx) * 2 + d % 2) for d in range(n_dp)]

    def far_pairs(bit):
        return [(t, t ^ bit) for t in range(tensor_size)]

    def spread(own):
        parts = []
        for j in range(nx):
            mine = own
            if j:
                mine = lax.ppermute(own, "dp", x_pairs(j))
            parts += [mine, lax.ppermute(mine, "dp", core_pairs)]
        return parts

    up_pack = pack_weight(up_weight_blocks, send_slots, dp_index, rows)
    later_slots, tables, place = lax.optimization_barrier((send_slots, tables, place))
    new_row, col_slot, home, came, kind = tables
    down_pack = pack_weight(down_weight_blocks, later_slots, dp_index, rows)
    up_in = exchange(up_pack)
    down_in = exchange(down_pack)
    up_parts = spread(up_in)
    down_parts = spread(down_in)

    shard = activations.shape[1]
    stacked = shard % block == 0 and tensor_size & (tensor_size - 1) == 0
    if stacked:
        bits = [1 << k for k in reversed(range(tensor_size.bit_length() - 1))]

        def gather(own):
            held = {0: own}
            for bit in bits:
                for m in list(held):
                    held[m ^ bit] = lax.ppermute(held[m], "tensor", far_pairs(bit))
            return [held[m] for m in range(tensor_size)]

        feats = gather(activations)
        backs = gather(cotangent)
        feat_shape = (tensor_size,) + activations.shape
    else:
        feats = [lax.all_gather(activations, "tensor", axis=1, tiled=True)]
        backs = [lax.all_gather(cotangent, "tensor", axis=1, tiled=True)]
        feat_shape = (1,) + feats[0].shape
    row_blocks = feat_shape[0] * feat_shape[2] // block

    ups = (up_first_moment, up_second_moment)
    downs = (down_first_moment, down_second_moment)
    ups_pack = pack_moments(ups, send_slots)
    downs_pack = pack_moments(downs, send_slots)
    ups_in = [exchange(ups_pack)]
    downs_in = [exchange(downs_pack)]

    act, act_t, slopes, x_t, wu = forward_products(
        tables, place, feats, up_weight_blocks, up_parts, col_count, row_blocks, feat_shape
    )

    def share(grads):
        terms = []
        for j in range(nx):
            there = lax.ppermute(grads[2 * j + 1], "dp", core_pairs)
            if j == 0:
                terms += [grads[0], there]
            else:
                both = (grads[2 * j].astype(F32) + there.astype(F32)).astype(BF16)
                terms.append(lax.ppermute(both, "dp", x_pairs(j)))
        return terms

    down_grads = gradient_products(new_row, col_slot, place, backs, (act_t,), n_dp, block, feat_shape)
    down_terms = share(down_grads)
    bpre, wd = back_products(
        tables, place, backs, down_weight_blocks, down_parts, slopes, feat_shape
    )
    up_grads = gradient_products(new_row, col_slot, place, (), (x_t, bpre), n_dp, block, feat_shape)
    up_terms = share(up_grads)
    sums = []
    near = [1 << k for k in range(tensor_size.bit_length() - 1)] if stacked else []
    order = near
    for w, left, turned in ((wd, act, False), (wu, bpre, True)):
        half = tensor_size // 2
        pieces = ((0, half), (half, half)) if stacked else ((0, 1),)
        got = output_products(
            new_row, col_slot, place, w, left, turned, order, pieces, feat_shape, row_blocks
        )
        if not stacked:
            sums.append(lax.psum_scatter(got[0][0], "tensor", scatter_dimension=1, tiled=True))
            continue
        held, send = got
        held = [held]
        for step, bit in enumerate(order):
            if step:
                half = held[-1].shape[0] // 2
                send = sum(s[half : 2 * half].astype(F32) for s in held).astype(BF16)
                held = [s[:half] for s in held]
            held.append(lax.ppermute(send, "tensor", far_pairs(bit)))
        sums.append(sum(s[0].astype(F32) for s in held).astype(BF16))
    out_sum, in_sum = sums

    up_step = adam_step((home, came, kind), up_terms, ups, ups_in)
    down_step = adam_step((home, came, kind), down_terms, downs, downs_in)
    return (out_sum, in_sum, up_step, down_step)


def solution(mesh):
    placed = (
        P("dp", "tensor"),
        P("dp", "tensor"),
        P("tensor", None, None),
        P("tensor", None, None),
        P("tensor", "dp", None),
        P("tensor", "dp", None),
        P("tensor", "dp", None),
        P("tensor", "dp", None),
        P(),
        P("tensor"),
        P("tensor"),
        P(),
    )
    return jax.shard_map(
        layer,
        mesh=mesh,
        in_specs=placed,
        out_specs=(
            P("dp", "tensor"),
            P("dp", "tensor"),
            P("tensor", "dp", None),
            P("tensor", "dp", None),
        ),
        check_vma=False,
    )
```

```python
import functools
import math

import jax
import jax.numpy as jnp
from jax import lax
from jax.experimental import pallas as pl
from jax.experimental.pallas import tpu as pltpu
from jax.sharding import PartitionSpec as P


gelu_scale = math.sqrt(2.0 / math.pi)
VMEM_LIMIT = 60 * 1024 * 1024
IN_UNROLL = 32
OUT_UNROLL = 56
CHUNK = 28
ADAM_UNROLL = 8
ADAM_PARTS = 4
FINISH_PARTS = 2

F32 = jnp.float32
BF16 = jnp.bfloat16
ANY = pl.BlockSpec(memory_space=pl.ANY)


def gelu_pair(pre_act):
    inner = gelu_scale * (pre_act + 0.044715 * pre_act * pre_act * pre_act)
    tangent = jnp.tanh(inner)
    gelu_value = 0.5 * pre_act * (1.0 + tangent)
    gelu_slope = 0.5 * (1.0 + tangent) + 0.5 * pre_act * (1.0 - tangent * tangent) * gelu_scale * (
        1.0 + 3.0 * 0.044715 * pre_act * pre_act
    )
    return (gelu_value, gelu_slope)


def local_columns(col_owner):
    count_all = col_owner.shape[0]
    order = jnp.arange(count_all, dtype=jnp.int32)
    same = (col_owner[None, :] == col_owner[:, None]) & (order[None, :] < order[:, None])
    return jnp.sum(same.astype(jnp.int32), axis=1)


def pack_weight(tiles, send_slots, dp_index, rows):
    slots, _, width = tiles.shape
    count = send_slots.shape[0]

    def kernel(send_ref, dp_ref, in_ref, out_ref):
        def step(i, carry):
            out_ref[i] = in_ref[send_ref[i]]
            return carry

        lax.fori_loop(0, count, step, 0, unroll=8)

    return pl.pallas_call(
        kernel,
        out_shape=jax.ShapeDtypeStruct((count, rows, width), tiles.dtype),
        grid_spec=pltpu.PrefetchScalarGridSpec(
            num_scalar_prefetch=2,
            grid=(1,),
            in_specs=[pl.BlockSpec((slots, rows, width), lambda i, s, d: (0, d[0], 0))],
            out_specs=pl.BlockSpec((count, rows, width), lambda i, s, d: (0, 0, 0)),
        ),
        compiler_params=pltpu.CompilerParams(vmem_limit_bytes=VMEM_LIMIT),
        cost_estimate=pl.CostEstimate(flops=0, transcendentals=0, bytes_accessed=4 * count * rows * width),
        name="pack_weight",
    )(send_slots, dp_index, tiles)


def pack_moments(arrays, send_slots):
    slots, rows, width = arrays[0].shape
    count = send_slots.shape[0]
    kinds = len(arrays)

    def kernel(send_ref, *refs):
        out_ref = refs[-1]

        def step(i, carry):
            s = send_ref[i]
            for k in range(kinds):
                out_ref[i, k] = refs[k][s].astype(BF16)
            return carry

        lax.fori_loop(0, count, step, 0, unroll=4)

    whole = pl.BlockSpec((slots, rows, width), lambda i, s: (0, 0, 0))
    return pl.pallas_call(
        kernel,
        out_shape=jax.ShapeDtypeStruct((count, kinds, rows, width), BF16),
        grid_spec=pltpu.PrefetchScalarGridSpec(
            num_scalar_prefetch=1,
            grid=(1,),
            in_specs=[whole] * kinds,
            out_specs=pl.BlockSpec((count, kinds, rows, width), lambda i, s: (0, 0, 0, 0)),
        ),
        compiler_params=pltpu.CompilerParams(vmem_limit_bytes=VMEM_LIMIT),
        cost_estimate=pl.CostEstimate(
            flops=0, transcendentals=0, bytes_accessed=6 * kinds * count * rows * width
        ),
        name="pack_moments",
    )(send_slots, *arrays)


def columns(ref, r, block):
    per = ref.shape[2] // block
    a = lax.div(r, per)
    off = pl.multiple_of((r - a * per) * block, block)
    return ref[a, :, pl.ds(off, block)]


def weight(own, came, home_ref, came_ref, kind_ref, g):
    kind = kind_ref[g]
    mine = own[home_ref[g]]
    at = came_ref[g]
    theirs = jnp.concatenate([came[q, at] for q in range(came.shape[0])], axis=0)
    picked = lax.select(kind == 1, mine, theirs)
    return lax.select(kind == 0, jnp.zeros_like(picked), picked)


def feature_copies(parts, place_ref, buf, sem):
    copies = []
    for m, part in enumerate(parts):
        at = (place_ref[2] ^ m) if len(parts) > 1 else 0
        copies.append(pltpu.make_async_copy(part, buf.at[at], sem.at[m]))
    return copies


def weight_copies(own, own_v, parts, parts_v, place_ref, sem):
    n_dp = len(parts)
    nx = n_dp // 2
    copies = [pltpu.make_async_copy(own, own_v, sem.at[0])]
    for j in range(nx):
        for other in range(2):
            k = 2 * j + other
            owner = lax.rem(place_ref[0] + nx - j, nx) * 2 + (place_ref[1] + other) % 2
            copies.append(pltpu.make_async_copy(parts[k], parts_v.at[owner], sem.at[1 + k]))
    return copies


def forward_kernel(n_feat, n_dp, row_blocks, *refs):
    row_ref, col_ref, home_ref, came_ref, kind_ref, place_ref = refs[:6]
    feats = refs[6 : 6 + n_feat]
    up_hbm = refs[6 + n_feat]
    parts = refs[7 + n_feat : 7 + n_feat + n_dp]
    act, act_t, slopes, x_t, wu_hbm, x_v, up_v, up_a, wu, pre, feat_sem, in_sem, out_sem = refs[7 + n_feat + n_dp :]
    slots, block, _ = up_v.shape
    copies = feature_copies(feats, place_ref, x_v, feat_sem)
    copies += weight_copies(up_hbm, up_v, parts, up_a, place_ref, in_sem)
    for copy in copies:
        copy.start()
    pre[...] = jnp.zeros(pre.shape, F32)
    for copy in copies:
        copy.wait()
    unroll = math.gcd(slots, IN_UNROLL)

    def step(i, carry):
        got = []
        for u in range(unroll):
            g = i * unroll + u
            w = weight(up_v, up_a, home_ref, came_ref, kind_ref, g)
            wu[g] = w
            got.append(jnp.dot(columns(x_v, row_ref[g], block), w, preferred_element_type=F32))
        for u in range(unroll):
            c = col_ref[i * unroll + u]
            pre[c] = pre[c] + got[u]
        return carry

    lax.fori_loop(0, slots // unroll, step, 0)
    keep = pltpu.make_async_copy(wu, wu_hbm, out_sem)
    keep.start()

    def turn(r, carry):
        x_t[r] = columns(x_v, r, block).T
        return carry

    lax.fori_loop(0, row_blocks, turn, 0)

    def bend(c, carry):
        value, slope = gelu_pair(pre[c])
        narrow = value.astype(BF16)
        act[c] = narrow
        act_t[c] = narrow.T
        slopes[c] = slope
        return carry

    lax.fori_loop(0, pre.shape[0], bend, 0)
    keep.wait()


def back_kernel(n_feat, n_dp, *refs):
    row_ref, col_ref, home_ref, came_ref, kind_ref, place_ref = refs[:6]
    feats = refs[6 : 6 + n_feat]
    down_hbm = refs[6 + n_feat]
    parts = refs[7 + n_feat : 7 + n_feat + n_dp]
    slopes, bpre, wd_hbm, back_v, down_v, down_a, wd, back, feat_sem, in_sem, keep_sem = refs[7 + n_feat + n_dp :]
    slots, block, _ = down_v.shape
    copies = feature_copies(feats, place_ref, back_v, feat_sem)
    copies += weight_copies(down_hbm, down_v, parts, down_a, place_ref, in_sem)
    for copy in copies:
        copy.start()
    back[...] = jnp.zeros(back.shape, F32)
    for copy in copies:
        copy.wait()
    unroll = math.gcd(slots, IN_UNROLL)

    def backward(i, carry):
        got = []
        for u in range(unroll):
            g = i * unroll + u
            w = weight(down_v, down_a, home_ref, came_ref, kind_ref, g)
            wd[g] = w
            got.append(
                lax.dot_general(
                    columns(back_v, row_ref[g], block), w, (((1,), (1,)), ((), ())), preferred_element_type=F32
                )
            )
        for u in range(unroll):
            c = col_ref[i * unroll + u]
            back[c] = back[c] + got[u]
        return carry

    lax.fori_loop(0, slots // unroll, backward, 0)
    keep = pltpu.make_async_copy(wd, wd_hbm, keep_sem)
    keep.start()

    def bend(c, carry):
        bpre[c] = (back[c] * slopes[c]).astype(BF16)
        return carry

    lax.fori_loop(0, slopes.shape[0], bend, 0)
    keep.wait()


def gradient_kernel(n_feat, n_dp, *refs):
    row_ref, col_ref, place_ref = refs[:3]
    feats = refs[3 : 3 + n_feat]
    left = refs[3 + n_feat]
    right = None if n_feat else refs[4]
    start = 4 + n_feat if n_feat else 5
    grad_refs = refs[start : start + n_dp]
    stage, out_sem = refs[start + n_dp : start + n_dp + 2]
    slots = row_ref.shape[0]
    chunk, block = stage.shape[1:3]
    rows = block // n_dp
    nx = n_dp // 2
    if n_feat:
        back_v, feat_sem = refs[start + n_dp + 2 :]
        copies = feature_copies(feats, place_ref, back_v, feat_sem)
        for copy in copies:
            copy.start()
        for copy in copies:
            copy.wait()

    def ship(i, slot):
        out = []
        for j in range(nx):
            for other in range(2):
                owner = lax.rem(place_ref[0] + j, nx) * 2 + (place_ref[1] + other) % 2
                at = pl.multiple_of(owner * rows, rows)
                out.append(
                    pltpu.make_async_copy(
                        stage.at[slot, :, pl.ds(at, rows), :],
                        grad_refs[2 * j + other].at[pl.ds(i * chunk, chunk)],
                        out_sem.at[slot, 2 * j + other],
                    )
                )
        return out

    def step(i, carry):
        slot = lax.rem(i, 2)

        @pl.when(i >= 2)
        def _():
            for copy in ship(i - 2, slot):
                copy.wait()

        for u in range(chunk):
            g = i * chunk + u
            r = row_ref[g]
            c = col_ref[g]
            if n_feat:
                product = jnp.dot(left[c], columns(back_v, r, block), preferred_element_type=F32)
            else:
                product = jnp.dot(left[r], right[c], preferred_element_type=F32)
            stage[slot, u] = product.astype(BF16)
        for copy in ship(i, slot):
            copy.start()
        return carry

    chunks = slots // chunk
    lax.fori_loop(0, chunks, step, 0)
    for i in range(max(chunks - 2, 0), chunks):
        for copy in ship(i, i % 2):
            copy.wait()


def output_kernel(pieces, turned, bits, *refs):
    row_ref, col_ref, place_ref = refs[:3]
    w_hbm, left = refs[3:5]
    outs = refs[5 : 5 + len(pieces)]
    w_v, acc, staged, in_sem, out_sem = refs[5 + len(pieces) :]
    slots, block, _ = w_v.shape
    parts = 4
    some = slots // parts
    loads = []
    for k in range(parts):
        at = pl.ds(k * some, some)
        loads.append(pltpu.make_async_copy(w_hbm.at[at], w_v.at[at], in_sem.at[k]))
    for copy in loads:
        copy.start()
    acc[...] = jnp.zeros(acc.shape, F32)
    unroll = math.gcd(some, OUT_UNROLL)
    dims = (((1,), (1 if turned else 0,)), ((), ()))

    def step(i, carry):
        got = []
        for u in range(unroll):
            g = i * unroll + u
            got.append(lax.dot_general(left[col_ref[g]], w_v[g], dims, preferred_element_type=F32))
        for u in range(unroll):
            r = row_ref[i * unroll + u]
            acc[r] = acc[r] + got[u]
        return carry

    for k in range(parts):
        loads[k].wait()
        lax.fori_loop(k * some // unroll, (k + 1) * some // unroll, step, 0)

    count = staged.shape[0]
    per = staged.shape[2] // block
    for a in range(count):
        if count == 1:
            at = 0
        else:
            far = place_ref[2] ^ a
            at = 0
            for b, bit in enumerate(bits):
                at = at + lax.div(far, bit) % 2 * (count >> (b + 1))
        for q in range(per):
            staged[at, :, q * block : (q + 1) * block] = acc[a * per + q].astype(BF16)
    copies = [
        pltpu.make_async_copy(staged.at[pl.ds(start, size)], out, out_sem.at[k])
        for k, ((start, size), out) in enumerate(zip(pieces, outs))
    ]
    for copy in copies:
        copy.start()
    for copy in copies:
        copy.wait()


VMEM = pl.BlockSpec(memory_space=pltpu.VMEM)
SMEM = pl.BlockSpec(memory_space=pltpu.SMEM)


def cost(flops, size):
    return pl.CostEstimate(flops=flops, transcendentals=0, bytes_accessed=size)


def forward_products(tables, place, feats, up, parts, col_count, row_blocks, feat_shape):
    slots, block, _ = up.shape
    n_dp, n_feat = len(parts), len(feats)
    tokens = feat_shape[1]
    return pl.pallas_call(
        functools.partial(forward_kernel, n_feat, n_dp, row_blocks),
        out_shape=[
            jax.ShapeDtypeStruct((col_count, tokens, block), BF16),
            jax.ShapeDtypeStruct((col_count, block, tokens), BF16),
            jax.ShapeDtypeStruct((col_count, tokens, block), F32),
            jax.ShapeDtypeStruct((row_blocks, block, tokens), BF16),
            jax.ShapeDtypeStruct(up.shape, BF16),
        ],
        in_specs=[SMEM] * 6 + [ANY] * (n_feat + 1 + n_dp),
        out_specs=[VMEM] * 4 + [ANY],
        scratch_shapes=[
            pltpu.VMEM(feat_shape, BF16),
            pltpu.VMEM(up.shape, BF16),
            pltpu.VMEM((n_dp,) + parts[0].shape, BF16),
            pltpu.VMEM(up.shape, BF16),
            pltpu.VMEM((col_count, tokens, block), F32),
            pltpu.SemaphoreType.DMA((n_feat,)),
            pltpu.SemaphoreType.DMA((1 + n_dp,)),
            pltpu.SemaphoreType.DMA,
        ],
        compiler_params=pltpu.CompilerParams(vmem_limit_bytes=VMEM_LIMIT),
        cost_estimate=cost(2 * slots * tokens * block * block, 12 * slots * block * block),
        name="forward_products",
    )(*tables, place, *feats, up, *parts)


def back_products(tables, place, feats, down, parts, slopes, feat_shape):
    slots, block, _ = down.shape
    n_dp, n_feat = len(parts), len(feats)
    tokens = slopes.shape[1]
    return pl.pallas_call(
        functools.partial(back_kernel, n_feat, n_dp),
        out_shape=[jax.ShapeDtypeStruct(slopes.shape, BF16), jax.ShapeDtypeStruct(down.shape, BF16)],
        in_specs=[SMEM] * 6 + [ANY] * (n_feat + 1 + n_dp) + [VMEM],
        out_specs=[VMEM, ANY],
        scratch_shapes=[
            pltpu.VMEM(feat_shape, BF16),
            pltpu.VMEM(down.shape, BF16),
            pltpu.VMEM((n_dp,) + parts[0].shape, BF16),
            pltpu.VMEM(down.shape, BF16),
            pltpu.VMEM(slopes.shape, F32),
            pltpu.SemaphoreType.DMA((n_feat,)),
            pltpu.SemaphoreType.DMA((1 + n_dp,)),
            pltpu.SemaphoreType.DMA,
        ],
        compiler_params=pltpu.CompilerParams(vmem_limit_bytes=VMEM_LIMIT),
        cost_estimate=cost(2 * slots * tokens * block * block, 12 * slots * block * block),
        name="back_products",
    )(*tables, place, *feats, down, *parts, slopes)


def gradient_products(row, col, place, feats, blocks, n_dp, block, feat_shape):
    slots = row.shape[0]
    n_feat = len(feats)
    chunk = math.gcd(slots, CHUNK)
    tokens = feat_shape[1]
    extra = [pltpu.VMEM(feat_shape, BF16), pltpu.SemaphoreType.DMA((n_feat,))] if n_feat else []
    return pl.pallas_call(
        functools.partial(gradient_kernel, n_feat, n_dp),
        out_shape=[jax.ShapeDtypeStruct((slots, block // n_dp, block), BF16)] * n_dp,
        in_specs=[SMEM] * 3 + [ANY] * n_feat + [VMEM] * len(blocks),
        out_specs=[ANY] * n_dp,
        scratch_shapes=[
            pltpu.VMEM((2, chunk, block, block), BF16),
            pltpu.SemaphoreType.DMA((2, n_dp)),
        ]
        + extra,
        compiler_params=pltpu.CompilerParams(vmem_limit_bytes=VMEM_LIMIT),
        cost_estimate=cost(2 * slots * tokens * block * block, 3 * slots * block * block),
        name="gradient_products",
    )(row, col, place, *feats, *blocks)


def output_products(row, col, place, w, left, turned, bits, pieces, feat_shape, row_blocks):
    slots, block, _ = w.shape
    count, tokens, shard = feat_shape
    return pl.pallas_call(
        functools.partial(output_kernel, pieces, turned, bits),
        out_shape=[jax.ShapeDtypeStruct((size, tokens, shard), BF16) for _, size in pieces],
        in_specs=[SMEM] * 3 + [ANY, VMEM],
        out_specs=[ANY] * len(pieces),
        scratch_shapes=[
            pltpu.VMEM(w.shape, BF16),
            pltpu.VMEM((row_blocks, tokens, block), F32),
            pltpu.VMEM((count, tokens, shard), BF16),
            pltpu.SemaphoreType.DMA((4,)),
            pltpu.SemaphoreType.DMA((len(pieces),)),
        ],
        compiler_params=pltpu.CompilerParams(vmem_limit_bytes=VMEM_LIMIT),
        cost_estimate=cost(2 * slots * tokens * block * block, 4 * slots * block * block),
        name="output_products",
    )(row, col, place, w, left)


def adam_step(tables, grads, moments, arrived):
    slots, rows, block = moments[0].shape
    n_grads = len(grads)
    n_from = len(arrived)
    bucket = arrived[0].shape[0]
    parts = math.gcd(slots, ADAM_PARTS)
    some = slots // parts

    def kernel(home_ref, came_ref, kind_ref, *refs):
        grad_refs = refs[:n_grads]
        moment_refs = refs[n_grads : n_grads + 2]
        arrived_refs = refs[n_grads + 2 : n_grads + 2 + n_from]
        out_hbm, grad_v, moment_v, arrived_v, out_v, grad_sem, moment_sem, arrived_sem, out_sem = refs[
            n_grads + 2 + n_from :
        ]
        first = [
            pltpu.make_async_copy(moment_refs[k], moment_v.at[k], moment_sem.at[k]) for k in range(2)
        ] + [
            pltpu.make_async_copy(arrived_refs[m], arrived_v.at[pl.ds(m * bucket, bucket)], arrived_sem.at[m])
            for m in range(n_from)
        ]
        later = [
            [
                pltpu.make_async_copy(
                    grad_refs[k].at[pl.ds(q * some, some)],
                    grad_v.at[k, pl.ds(q * some, some)],
                    grad_sem.at[q, k],
                )
                for k in range(n_grads)
            ]
            for q in range(parts)
        ]
        outs = [
            pltpu.make_async_copy(
                out_v.at[pl.ds(q * some, some)], out_hbm.at[pl.ds(q * some, some)], out_sem.at[q]
            )
            for q in range(parts)
        ]
        for copy in first + sum(later, []):
            copy.start()

        def step(g, carry):
            at = came_ref[g]
            own = home_ref[g]
            kind = kind_ref[g]

            def moved(k):
                picked = lax.select(kind == 1, moment_v[k, own], arrived_v[at, k].astype(F32))
                return lax.select(kind == 0, jnp.zeros_like(picked), picked)

            total = grad_v[0, g].astype(F32)
            for k in range(1, n_grads):
                total = total + grad_v[k, g].astype(F32)
            first_moment = 0.9 * moved(0) + 0.1 * total
            second_moment = 0.95 * moved(1) + 0.05 * total * total
            out_v[g] = first_moment / (jnp.sqrt(second_moment) + 1.0)
            return carry

        for copy in first:
            copy.wait()
        unroll = math.gcd(some, ADAM_UNROLL)
        for q in range(parts):
            for copy in later[q]:
                copy.wait()

            def trip(i, carry, q=q):
                for u in range(unroll):
                    step(q * some + i * unroll + u, carry)
                return carry

            lax.fori_loop(0, some // unroll, trip, 0)
            outs[q].start()
        for copy in outs:
            copy.wait()

    return pl.pallas_call(
        kernel,
        out_shape=jax.ShapeDtypeStruct(moments[0].shape, F32),
        in_specs=[SMEM] * 3 + [ANY] * (n_grads + 2 + n_from),
        out_specs=ANY,
        scratch_shapes=[
            pltpu.VMEM((n_grads, slots, rows, block), BF16),
            pltpu.VMEM((2, slots, rows, block), F32),
            pltpu.VMEM((n_from * bucket, 2, rows, block), BF16),
            pltpu.VMEM((slots, rows, block), F32),
            pltpu.SemaphoreType.DMA((parts, n_grads)),
            pltpu.SemaphoreType.DMA((2,)),
            pltpu.SemaphoreType.DMA((n_from,)),
            pltpu.SemaphoreType.DMA((parts,)),
        ],
        compiler_params=pltpu.CompilerParams(vmem_limit_bytes=VMEM_LIMIT),
        cost_estimate=cost(15 * slots * rows * block, 17 * slots * rows * block),
        name="adam_step",
    )(*tables, *grads, *moments, *arrived)


def adam_ahead(tables, grads, moments):
    slots, rows, block = moments[0].shape
    n_grads = len(grads)

    def kernel(home_ref, kind_ref, *refs):
        grad_refs = refs[:n_grads]
        moment_refs = refs[n_grads : n_grads + 2]
        outs = refs[n_grads + 2 :]
        unroll = math.gcd(slots, ADAM_UNROLL)

        def trip(i, carry):
            for u in range(unroll):
                g = i * unroll + u
                own = home_ref[g]
                stays = kind_ref[g] == 1
                total = grad_refs[0][g].astype(F32)
                for ref in grad_refs[1:]:
                    total = total + ref[g].astype(F32)
                for k, (keep, term) in enumerate(((0.9, 0.1 * total), (0.95, 0.05 * total * total))):
                    mine = moment_refs[k][own]
                    outs[k][g] = keep * lax.select(stays, mine, jnp.zeros_like(mine)) + term
            return carry

        lax.fori_loop(0, slots // unroll, trip, 0)

    vmem = pl.BlockSpec(memory_space=pltpu.VMEM)
    return pl.pallas_call(
        kernel,
        out_shape=[jax.ShapeDtypeStruct(moments[0].shape, F32)] * 2,
        in_specs=[SMEM] * 2 + [vmem] * (n_grads + 2),
        out_specs=[vmem] * 2,
        compiler_params=pltpu.CompilerParams(vmem_limit_bytes=VMEM_LIMIT),
        cost_estimate=cost(10 * slots * rows * block, 22 * slots * rows * block),
        name="ahead",
    )(*tables, *grads, *moments)


def adam_finish(tables, ahead, arrived):
    slots, rows, block = ahead[0].shape
    parts = math.gcd(slots, FINISH_PARTS)
    some = slots // parts

    def kernel(came_ref, kind_ref, first_hbm, second_hbm, arrived_hbm, out_hbm, ahead_v, arrived_v, out_v, sem, more, out_sem):
        copy = pltpu.make_async_copy(arrived_hbm, arrived_v, more)
        copy.start()
        loads = []
        outs = []
        for q in range(parts):
            at = pl.ds(q * some, some)
            loads.append(
                [
                    pltpu.make_async_copy(hbm.at[at], ahead_v.at[k, at], sem.at[q, k])
                    for k, hbm in enumerate((first_hbm, second_hbm))
                ]
            )
            outs.append(pltpu.make_async_copy(out_v.at[at], out_hbm.at[at], out_sem.at[q]))
        for pair in loads:
            for load in pair:
                load.start()
        copy.wait()
        unroll = math.gcd(some, 2 * ADAM_UNROLL)
        for q in range(parts):
            for load in loads[q]:
                load.wait()

            def trip(i, carry, q=q):
                for u in range(unroll):
                    g = q * some + i * unroll + u
                    at = came_ref[g]
                    comes = kind_ref[g] == 2
                    sums = []
                    for k, keep in enumerate((0.9, 0.95)):
                        theirs = arrived_v[at, k].astype(F32)
                        sums.append(ahead_v[k, g] + keep * lax.select(comes, theirs, jnp.zeros_like(theirs)))
                    out_v[g] = sums[0] / (jnp.sqrt(sums[1]) + 1.0)
                return carry

            lax.fori_loop(0, some // unroll, trip, 0)
            outs[q].start()
        for out in outs:
            out.wait()

    return pl.pallas_call(
        kernel,
        out_shape=jax.ShapeDtypeStruct(ahead[0].shape, F32),
        in_specs=[SMEM] * 2 + [ANY] * 3,
        out_specs=ANY,
        scratch_shapes=[
            pltpu.VMEM((2, slots, rows, block), F32),
            pltpu.VMEM(arrived.shape, BF16),
            pltpu.VMEM((slots, rows, block), F32),
            pltpu.SemaphoreType.DMA((parts, 2)),
            pltpu.SemaphoreType.DMA,
            pltpu.SemaphoreType.DMA((parts,)),
        ],
        compiler_params=pltpu.CompilerParams(vmem_limit_bytes=VMEM_LIMIT),
        cost_estimate=cost(10 * slots * rows * block, 18 * slots * rows * block),
        name="finish",
    )(*tables, *ahead, arrived)


def layer(
    activations,
    cotangent,
    up_weight_blocks,
    down_weight_blocks,
    up_first_moment,
    up_second_moment,
    down_first_moment,
    down_second_moment,
    source,
    new_row,
    new_col,
    col_owner,
):
    tensor_size = lax.axis_size("tensor")
    n_dp = lax.axis_size("dp")
    nx = n_dp // 2
    my_index = lax.axis_index("tensor")
    my_dp = lax.axis_index("dp")
    slot_count, block, _ = up_weight_blocks.shape
    rows = block // n_dp
    bucket = (slot_count + tensor_size - 2) // tensor_size

    sources = source.reshape(tensor_size, slot_count)
    is_live = sources >= 0
    sender_dev = jnp.where(is_live, sources // slot_count, -1)
    sender_slot = jnp.where(is_live, sources % slot_count, 0)
    targets = jnp.arange(tensor_size, dtype=jnp.int32)[:, None]
    outgoing = is_live & (sender_dev == my_index) & (targets != my_index)
    out_flags = outgoing.astype(jnp.int32)
    out_rank = jnp.cumsum(out_flags, axis=1) - out_flags
    chosen = outgoing[:, :, None] & (
        out_rank[:, :, None] == jnp.arange(bucket, dtype=jnp.int32)[None, None, :]
    )
    send_slots = jnp.sum(jnp.where(chosen, sender_slot[:, :, None], 0), axis=1).reshape(-1)
    mine_dev = lax.dynamic_index_in_dim(sender_dev, my_index, 0, keepdims=False)
    mine_slot = lax.dynamic_index_in_dim(sender_slot, my_index, 0, keepdims=False)
    mine_live = mine_dev >= 0
    stays = mine_live & (mine_dev == my_index)
    positions = jnp.arange(slot_count, dtype=jnp.int32)
    earlier = (
        (mine_dev[:, None] == mine_dev[None, :])
        & mine_live[None, :]
        & (positions[None, :] < positions[:, None])
    )
    recv_rank = jnp.minimum(jnp.sum(earlier.astype(jnp.int32), axis=1), bucket - 1)
    home = jnp.where(stays, mine_slot, 0)
    came = jnp.where(mine_live & ~stays, mine_dev * bucket + recv_rank, 0)
    kind = jnp.where(stays, 1, jnp.where(mine_live, 2, 0)).astype(jnp.int32)
    col_count = col_owner.shape[0] // tensor_size
    col_slot = jnp.take(local_columns(col_owner), new_col)
    place = jnp.stack([my_dp // 2, my_dp % 2, my_index]).astype(jnp.int32)
    dp_index = my_dp.reshape(1).astype(jnp.int32)
    tables = (new_row, col_slot, home, came, kind)

    def exchange(packed):
        shaped = packed.reshape((tensor_size, bucket) + packed.shape[1:])
        got = lax.all_to_all(shaped, "tensor", split_axis=0, concat_axis=0, tiled=True)
        return got.reshape((tensor_size * bucket,) + packed.shape[1:])

    core_pairs = [(d, d ^ 1) for d in range(n_dp)]

    def x_pairs(j):
        return [(d, ((d // 2 + j) % nx) * 2 + d % 2) for d in range(n_dp)]

    def far_pairs(bit):
        return [(t, t ^ bit) for t in range(tensor_size)]

    def spread(own):
        parts = []
        for j in range(nx):
            mine = own
            if j:
                mine = lax.ppermute(own, "dp", x_pairs(j))
            parts += [mine, lax.ppermute(mine, "dp", core_pairs)]
        return parts

    up_pack = pack_weight(up_weight_blocks, send_slots, dp_index, rows)
    later_slots, tables, place = lax.optimization_barrier((send_slots, tables, place))
    new_row, col_slot, home, came, kind = tables
    down_pack = pack_weight(down_weight_blocks, later_slots, dp_index, rows)
    up_in = exchange(up_pack)
    down_in = exchange(down_pack)
    up_parts = spread(up_in)
    down_parts = spread(down_in)

    shard = activations.shape[1]
    stacked = shard % block == 0 and tensor_size & (tensor_size - 1) == 0
    if stacked:
        bits = [1 << k for k in reversed(range(tensor_size.bit_length() - 1))]

        def gather(own):
            held = {0: own}
            for bit in bits:
                for m in list(held):
                    held[m ^ bit] = lax.ppermute(held[m], "tensor", far_pairs(bit))
            return [held[m] for m in range(tensor_size)]

        feats = gather(activations)
        backs = gather(cotangent)
        feat_shape = (tensor_size,) + activations.shape
    else:
        feats = [lax.all_gather(activations, "tensor", axis=1, tiled=True)]
        backs = [lax.all_gather(cotangent, "tensor", axis=1, tiled=True)]
        feat_shape = (1,) + feats[0].shape
    row_blocks = feat_shape[0] * feat_shape[2] // block

    ups = (up_first_moment, up_second_moment)
    downs = (down_first_moment, down_second_moment)
    ups_pack = pack_moments(ups, send_slots)
    downs_pack = pack_moments(downs, send_slots)
    ups_in = [exchange(ups_pack)]
    downs_in = [exchange(downs_pack)]

    act, act_t, slopes, x_t, wu = forward_products(
        tables, place, feats, up_weight_blocks, up_parts, col_count, row_blocks, feat_shape
    )

    def share(grads):
        terms = []
        for j in range(nx):
            there = lax.ppermute(grads[2 * j + 1], "dp", core_pairs)
            if j == 0:
                terms += [grads[0], there]
            else:
                both = (grads[2 * j].astype(F32) + there.astype(F32)).astype(BF16)
                terms.append(lax.ppermute(both, "dp", x_pairs(j)))
        return terms

    down_grads = gradient_products(new_row, col_slot, place, backs, (act_t,), n_dp, block, feat_shape)
    down_terms = share(down_grads)
    bpre, wd = back_products(
        tables, place, backs, down_weight_blocks, down_parts, slopes, feat_shape
    )
    up_grads = gradient_products(new_row, col_slot, place, (), (x_t, bpre), n_dp, block, feat_shape)
    up_terms = share(up_grads)
    sums = []
    near = [1 << k for k in range(tensor_size.bit_length() - 1)] if stacked else []
    order = near
    for w, left, turned in ((wd, act, False), (wu, bpre, True)):
        half = tensor_size // 2
        pieces = ((0, half), (half, half)) if stacked else ((0, 1),)
        got = output_products(
            new_row, col_slot, place, w, left, turned, order, pieces, feat_shape, row_blocks
        )
        if not stacked:
            sums.append(lax.psum_scatter(got[0][0], "tensor", scatter_dimension=1, tiled=True))
            continue
        held, send = got
        held = [held]
        for step, bit in enumerate(order):
            if step:
                half = held[-1].shape[0] // 2
                send = sum(s[half : 2 * half].astype(F32) for s in held).astype(BF16)
                held = [s[:half] for s in held]
            held.append(lax.ppermute(send, "tensor", far_pairs(bit)))
        sums.append(sum(s[0].astype(F32) for s in held).astype(BF16))
    out_sum, in_sum = sums

    up_step = adam_step((home, came, kind), up_terms, ups, ups_in)
    ahead = adam_ahead((home, kind), down_terms, downs)
    down_step = adam_finish((came, kind), ahead, downs_in[0])
    return (out_sum, in_sum, up_step, down_step)


def solution(mesh):
    placed = (
        P("dp", "tensor"),
        P("dp", "tensor"),
        P("tensor", None, None),
        P("tensor", None, None),
        P("tensor", "dp", None),
        P("tensor", "dp", None),
        P("tensor", "dp", None),
        P("tensor", "dp", None),
        P(),
        P("tensor"),
        P("tensor"),
        P(),
    )
    return jax.shard_map(
        layer,
        mesh=mesh,
        in_specs=placed,
        out_specs=(
            P("dp", "tensor"),
            P("dp", "tensor"),
            P("tensor", "dp", None),
            P("tensor", "dp", None),
        ),
        check_vma=False,
    )
```

```python
import functools
import math

import jax
import jax.numpy as jnp
from jax import lax
from jax.experimental import pallas as pl
from jax.experimental.pallas import tpu as pltpu
from jax.sharding import PartitionSpec as P


gelu_scale = math.sqrt(2.0 / math.pi)
VMEM_LIMIT = 60 * 1024 * 1024
IN_UNROLL = 32
OUT_UNROLL = 56
CHUNK = 28
ADAM_UNROLL = 8
ADAM_PARTS = 4
FINISH_PARTS = 2

F32 = jnp.float32
BF16 = jnp.bfloat16
ANY = pl.BlockSpec(memory_space=pl.ANY)


def gelu_pair(pre_act):
    inner = gelu_scale * (pre_act + 0.044715 * pre_act * pre_act * pre_act)
    tangent = jnp.tanh(inner)
    gelu_value = 0.5 * pre_act * (1.0 + tangent)
    gelu_slope = 0.5 * (1.0 + tangent) + 0.5 * pre_act * (1.0 - tangent * tangent) * gelu_scale * (
        1.0 + 3.0 * 0.044715 * pre_act * pre_act
    )
    return (gelu_value, gelu_slope)


def local_columns(col_owner):
    count_all = col_owner.shape[0]
    order = jnp.arange(count_all, dtype=jnp.int32)
    same = (col_owner[None, :] == col_owner[:, None]) & (order[None, :] < order[:, None])
    return jnp.sum(same.astype(jnp.int32), axis=1)


def pack_weight(tiles, send_slots, dp_index, rows):
    slots, _, width = tiles.shape
    count = send_slots.shape[0]

    def kernel(send_ref, dp_ref, in_ref, out_ref):
        def step(i, carry):
            out_ref[i] = in_ref[send_ref[i]]
            return carry

        lax.fori_loop(0, count, step, 0, unroll=8)

    return pl.pallas_call(
        kernel,
        out_shape=jax.ShapeDtypeStruct((count, rows, width), tiles.dtype),
        grid_spec=pltpu.PrefetchScalarGridSpec(
            num_scalar_prefetch=2,
            grid=(1,),
            in_specs=[pl.BlockSpec((slots, rows, width), lambda i, s, d: (0, d[0], 0))],
            out_specs=pl.BlockSpec((count, rows, width), lambda i, s, d: (0, 0, 0)),
        ),
        compiler_params=pltpu.CompilerParams(vmem_limit_bytes=VMEM_LIMIT),
        cost_estimate=pl.CostEstimate(flops=0, transcendentals=0, bytes_accessed=4 * count * rows * width),
        name="pack_weight",
    )(send_slots, dp_index, tiles)


def pack_moments(arrays, send_slots):
    slots, rows, width = arrays[0].shape
    count = send_slots.shape[0]
    kinds = len(arrays)

    def kernel(send_ref, *refs):
        out_ref = refs[-1]

        def step(i, carry):
            s = send_ref[i]
            for k in range(kinds):
                out_ref[i, k] = refs[k][s].astype(BF16)
            return carry

        lax.fori_loop(0, count, step, 0, unroll=4)

    whole = pl.BlockSpec((slots, rows, width), lambda i, s: (0, 0, 0))
    return pl.pallas_call(
        kernel,
        out_shape=jax.ShapeDtypeStruct((count, kinds, rows, width), BF16),
        grid_spec=pltpu.PrefetchScalarGridSpec(
            num_scalar_prefetch=1,
            grid=(1,),
            in_specs=[whole] * kinds,
            out_specs=pl.BlockSpec((count, kinds, rows, width), lambda i, s: (0, 0, 0, 0)),
        ),
        compiler_params=pltpu.CompilerParams(vmem_limit_bytes=VMEM_LIMIT),
        cost_estimate=pl.CostEstimate(
            flops=0, transcendentals=0, bytes_accessed=6 * kinds * count * rows * width
        ),
        name="pack_moments",
    )(send_slots, *arrays)


def columns(ref, r, block):
    per = ref.shape[2] // block
    a = lax.div(r, per)
    off = pl.multiple_of((r - a * per) * block, block)
    return ref[a, :, pl.ds(off, block)]


def weight(own, came, home_ref, came_ref, kind_ref, g):
    kind = kind_ref[g]
    mine = own[home_ref[g]]
    at = came_ref[g]
    theirs = jnp.concatenate([came[q, at] for q in range(came.shape[0])], axis=0)
    picked = lax.select(kind == 1, mine, theirs)
    return lax.select(kind == 0, jnp.zeros_like(picked), picked)


def feature_copies(parts, place_ref, buf, sem):
    copies = []
    for m, part in enumerate(parts):
        at = (place_ref[2] ^ m) if len(parts) > 1 else 0
        copies.append(pltpu.make_async_copy(part, buf.at[at], sem.at[m]))
    return copies


def weight_copies(own, own_v, parts, parts_v, place_ref, sem):
    n_dp = len(parts)
    nx = n_dp // 2
    copies = [pltpu.make_async_copy(own, own_v, sem.at[0])]
    for j in range(nx):
        for other in range(2):
            k = 2 * j + other
            owner = lax.rem(place_ref[0] + nx - j, nx) * 2 + (place_ref[1] + other) % 2
            copies.append(pltpu.make_async_copy(parts[k], parts_v.at[owner], sem.at[1 + k]))
    return copies


def forward_kernel(n_feat, n_dp, row_blocks, *refs):
    row_ref, col_ref, home_ref, came_ref, kind_ref, place_ref = refs[:6]
    feats = refs[6 : 6 + n_feat]
    up_hbm = refs[6 + n_feat]
    parts = refs[7 + n_feat : 7 + n_feat + n_dp]
    act, act_t, slopes, x_t, wu_hbm, x_v, up_v, up_a, wu, pre, feat_sem, in_sem, out_sem = refs[7 + n_feat + n_dp :]
    slots, block, _ = up_v.shape
    copies = feature_copies(feats, place_ref, x_v, feat_sem)
    copies += weight_copies(up_hbm, up_v, parts, up_a, place_ref, in_sem)
    for copy in copies:
        copy.start()
    pre[...] = jnp.zeros(pre.shape, F32)
    for copy in copies:
        copy.wait()
    unroll = math.gcd(slots, IN_UNROLL)

    def step(i, carry):
        got = []
        for u in range(unroll):
            g = i * unroll + u
            w = weight(up_v, up_a, home_ref, came_ref, kind_ref, g)
            wu[g] = w
            got.append(jnp.dot(columns(x_v, row_ref[g], block), w, preferred_element_type=F32))
        for u in range(unroll):
            c = col_ref[i * unroll + u]
            pre[c] = pre[c] + got[u]
        return carry

    lax.fori_loop(0, slots // unroll, step, 0)
    keep = pltpu.make_async_copy(wu, wu_hbm, out_sem)
    keep.start()

    def turn(r, carry):
        x_t[r] = columns(x_v, r, block).T
        return carry

    lax.fori_loop(0, row_blocks, turn, 0)

    def bend(c, carry):
        value, slope = gelu_pair(pre[c])
        narrow = value.astype(BF16)
        act[c] = narrow
        act_t[c] = narrow.T
        slopes[c] = slope
        return carry

    lax.fori_loop(0, pre.shape[0], bend, 0)
    keep.wait()


def back_kernel(n_feat, n_dp, *refs):
    row_ref, col_ref, home_ref, came_ref, kind_ref, place_ref = refs[:6]
    feats = refs[6 : 6 + n_feat]
    down_hbm = refs[6 + n_feat]
    parts = refs[7 + n_feat : 7 + n_feat + n_dp]
    slopes_hbm, bpre, wd_hbm, back_v, down_v, down_a, wd, back, slopes, feat_sem, in_sem, slope_sem, keep_sem = refs[
        7 + n_feat + n_dp :
    ]
    slots, block, _ = down_v.shape
    copies = feature_copies(feats, place_ref, back_v, feat_sem)
    copies += weight_copies(down_hbm, down_v, parts, down_a, place_ref, in_sem)
    copies.append(pltpu.make_async_copy(slopes_hbm, slopes, slope_sem))
    for copy in copies:
        copy.start()
    back[...] = jnp.zeros(back.shape, F32)
    for copy in copies:
        copy.wait()
    unroll = math.gcd(slots, IN_UNROLL)

    def backward(i, carry):
        got = []
        for u in range(unroll):
            g = i * unroll + u
            w = weight(down_v, down_a, home_ref, came_ref, kind_ref, g)
            wd[g] = w
            got.append(
                lax.dot_general(
                    columns(back_v, row_ref[g], block), w, (((1,), (1,)), ((), ())), preferred_element_type=F32
                )
            )
        for u in range(unroll):
            c = col_ref[i * unroll + u]
            back[c] = back[c] + got[u]
        return carry

    lax.fori_loop(0, slots // unroll, backward, 0)
    keep = pltpu.make_async_copy(wd, wd_hbm, keep_sem)
    keep.start()

    def bend(c, carry):
        bpre[c] = (back[c] * slopes[c]).astype(BF16)
        return carry

    lax.fori_loop(0, slopes.shape[0], bend, 0)
    keep.wait()


def gradient_kernel(n_feat, n_dp, *refs):
    row_ref, col_ref, place_ref = refs[:3]
    feats = refs[3 : 3 + n_feat]
    left = refs[3 + n_feat]
    right = None if n_feat else refs[4]
    start = 4 + n_feat if n_feat else 5
    grad_refs = refs[start : start + n_dp]
    stage, out_sem = refs[start + n_dp : start + n_dp + 2]
    slots = row_ref.shape[0]
    chunk, block = stage.shape[1:3]
    rows = block // n_dp
    nx = n_dp // 2
    if n_feat:
        back_v, feat_sem = refs[start + n_dp + 2 :]
        copies = feature_copies(feats, place_ref, back_v, feat_sem)
        for copy in copies:
            copy.start()
        for copy in copies:
            copy.wait()

    def ship(i, slot):
        out = []
        for j in range(nx):
            for other in range(2):
                owner = lax.rem(place_ref[0] + j, nx) * 2 + (place_ref[1] + other) % 2
                at = pl.multiple_of(owner * rows, rows)
                out.append(
                    pltpu.make_async_copy(
                        stage.at[slot, :, pl.ds(at, rows), :],
                        grad_refs[2 * j + other].at[pl.ds(i * chunk, chunk)],
                        out_sem.at[slot, 2 * j + other],
                    )
                )
        return out

    def step(i, carry):
        slot = lax.rem(i, 2)

        @pl.when(i >= 2)
        def _():
            for copy in ship(i - 2, slot):
                copy.wait()

        for u in range(chunk):
            g = i * chunk + u
            r = row_ref[g]
            c = col_ref[g]
            if n_feat:
                product = jnp.dot(left[c], columns(back_v, r, block), preferred_element_type=F32)
            else:
                product = jnp.dot(left[r], right[c], preferred_element_type=F32)
            stage[slot, u] = product.astype(BF16)
        for copy in ship(i, slot):
            copy.start()
        return carry

    chunks = slots // chunk
    lax.fori_loop(0, chunks, step, 0)
    for i in range(max(chunks - 2, 0), chunks):
        for copy in ship(i, i % 2):
            copy.wait()


def output_kernel(pieces, turned, bits, *refs):
    row_ref, col_ref, place_ref = refs[:3]
    w_hbm, left = refs[3:5]
    outs = refs[5 : 5 + len(pieces)]
    w_v, acc, staged, in_sem, out_sem = refs[5 + len(pieces) :]
    slots, block, _ = w_v.shape
    parts = 4
    some = slots // parts
    loads = []
    for k in range(parts):
        at = pl.ds(k * some, some)
        loads.append(pltpu.make_async_copy(w_hbm.at[at], w_v.at[at], in_sem.at[k]))
    for copy in loads:
        copy.start()
    acc[...] = jnp.zeros(acc.shape, F32)
    unroll = math.gcd(some, OUT_UNROLL)
    dims = (((1,), (1 if turned else 0,)), ((), ()))

    def step(i, carry):
        got = []
        for u in range(unroll):
            g = i * unroll + u
            got.append(lax.dot_general(left[col_ref[g]], w_v[g], dims, preferred_element_type=F32))
        for u in range(unroll):
            r = row_ref[i * unroll + u]
            acc[r] = acc[r] + got[u]
        return carry

    for k in range(parts):
        loads[k].wait()
        lax.fori_loop(k * some // unroll, (k + 1) * some // unroll, step, 0)

    count = staged.shape[0]
    per = staged.shape[2] // block
    for a in range(count):
        if count == 1:
            at = 0
        else:
            far = place_ref[2] ^ a
            at = 0
            for b, bit in enumerate(bits):
                at = at + lax.div(far, bit) % 2 * (count >> (b + 1))
        for q in range(per):
            staged[at, :, q * block : (q + 1) * block] = acc[a * per + q].astype(BF16)
    copies = [
        pltpu.make_async_copy(staged.at[pl.ds(start, size)], out, out_sem.at[k])
        for k, ((start, size), out) in enumerate(zip(pieces, outs))
    ]
    for copy in copies:
        copy.start()
    for copy in copies:
        copy.wait()


VMEM = pl.BlockSpec(memory_space=pltpu.VMEM)
SMEM = pl.BlockSpec(memory_space=pltpu.SMEM)


def cost(flops, size):
    return pl.CostEstimate(flops=flops, transcendentals=0, bytes_accessed=size)


def forward_products(tables, place, feats, up, parts, col_count, row_blocks, feat_shape):
    slots, block, _ = up.shape
    n_dp, n_feat = len(parts), len(feats)
    tokens = feat_shape[1]
    return pl.pallas_call(
        functools.partial(forward_kernel, n_feat, n_dp, row_blocks),
        out_shape=[
            jax.ShapeDtypeStruct((col_count, tokens, block), BF16),
            jax.ShapeDtypeStruct((col_count, block, tokens), BF16),
            jax.ShapeDtypeStruct((col_count, tokens, block), F32),
            jax.ShapeDtypeStruct((row_blocks, block, tokens), BF16),
            jax.ShapeDtypeStruct(up.shape, BF16),
        ],
        in_specs=[SMEM] * 6 + [ANY] * (n_feat + 1 + n_dp),
        out_specs=[VMEM] * 4 + [ANY],
        scratch_shapes=[
            pltpu.VMEM(feat_shape, BF16),
            pltpu.VMEM(up.shape, BF16),
            pltpu.VMEM((n_dp,) + parts[0].shape, BF16),
            pltpu.VMEM(up.shape, BF16),
            pltpu.VMEM((col_count, tokens, block), F32),
            pltpu.SemaphoreType.DMA((n_feat,)),
            pltpu.SemaphoreType.DMA((1 + n_dp,)),
            pltpu.SemaphoreType.DMA,
        ],
        compiler_params=pltpu.CompilerParams(vmem_limit_bytes=VMEM_LIMIT),
        cost_estimate=cost(2 * slots * tokens * block * block, 12 * slots * block * block),
        name="forward_products",
    )(*tables, place, *feats, up, *parts)


def back_products(tables, place, feats, down, parts, slopes, feat_shape):
    slots, block, _ = down.shape
    n_dp, n_feat = len(parts), len(feats)
    tokens = slopes.shape[1]
    return pl.pallas_call(
        functools.partial(back_kernel, n_feat, n_dp),
        out_shape=[jax.ShapeDtypeStruct(slopes.shape, BF16), jax.ShapeDtypeStruct(down.shape, BF16)],
        in_specs=[SMEM] * 6 + [ANY] * (n_feat + 2 + n_dp),
        out_specs=[VMEM, ANY],
        scratch_shapes=[
            pltpu.VMEM(feat_shape, BF16),
            pltpu.VMEM(down.shape, BF16),
            pltpu.VMEM((n_dp,) + parts[0].shape, BF16),
            pltpu.VMEM(down.shape, BF16),
            pltpu.VMEM(slopes.shape, F32),
            pltpu.VMEM(slopes.shape, F32),
            pltpu.SemaphoreType.DMA((n_feat,)),
            pltpu.SemaphoreType.DMA((1 + n_dp,)),
            pltpu.SemaphoreType.DMA,
            pltpu.SemaphoreType.DMA,
        ],
        compiler_params=pltpu.CompilerParams(vmem_limit_bytes=VMEM_LIMIT),
        cost_estimate=cost(2 * slots * tokens * block * block, 12 * slots * block * block),
        name="back_products",
    )(*tables, place, *feats, down, *parts, slopes)


def gradient_products(row, col, place, feats, blocks, n_dp, block, feat_shape):
    slots = row.shape[0]
    n_feat = len(feats)
    chunk = math.gcd(slots, CHUNK)
    tokens = feat_shape[1]
    extra = [pltpu.VMEM(feat_shape, BF16), pltpu.SemaphoreType.DMA((n_feat,))] if n_feat else []
    return pl.pallas_call(
        functools.partial(gradient_kernel, n_feat, n_dp),
        out_shape=[jax.ShapeDtypeStruct((slots, block // n_dp, block), BF16)] * n_dp,
        in_specs=[SMEM] * 3 + [ANY] * n_feat + [VMEM] * len(blocks),
        out_specs=[ANY] * n_dp,
        scratch_shapes=[
            pltpu.VMEM((2, chunk, block, block), BF16),
            pltpu.SemaphoreType.DMA((2, n_dp)),
        ]
        + extra,
        compiler_params=pltpu.CompilerParams(vmem_limit_bytes=VMEM_LIMIT),
        cost_estimate=cost(2 * slots * tokens * block * block, 3 * slots * block * block),
        name="gradient_products",
    )(row, col, place, *feats, *blocks)


def output_products(row, col, place, w, left, turned, bits, pieces, feat_shape, row_blocks):
    slots, block, _ = w.shape
    count, tokens, shard = feat_shape
    return pl.pallas_call(
        functools.partial(output_kernel, pieces, turned, bits),
        out_shape=[jax.ShapeDtypeStruct((size, tokens, shard), BF16) for _, size in pieces],
        in_specs=[SMEM] * 3 + [ANY, VMEM],
        out_specs=[ANY] * len(pieces),
        scratch_shapes=[
            pltpu.VMEM(w.shape, BF16),
            pltpu.VMEM((row_blocks, tokens, block), F32),
            pltpu.VMEM((count, tokens, shard), BF16),
            pltpu.SemaphoreType.DMA((4,)),
            pltpu.SemaphoreType.DMA((len(pieces),)),
        ],
        compiler_params=pltpu.CompilerParams(vmem_limit_bytes=VMEM_LIMIT),
        cost_estimate=cost(2 * slots * tokens * block * block, 4 * slots * block * block),
        name="output_products",
    )(row, col, place, w, left)


def adam_step(tables, grads, moments, arrived):
    slots, rows, block = moments[0].shape
    n_grads = len(grads)
    n_from = len(arrived)
    bucket = arrived[0].shape[0]
    parts = math.gcd(slots, ADAM_PARTS)
    some = slots // parts

    def kernel(home_ref, came_ref, kind_ref, *refs):
        grad_refs = refs[:n_grads]
        moment_refs = refs[n_grads : n_grads + 2]
        arrived_refs = refs[n_grads + 2 : n_grads + 2 + n_from]
        out_hbm, grad_v, moment_v, arrived_v, out_v, grad_sem, moment_sem, arrived_sem, out_sem = refs[
            n_grads + 2 + n_from :
        ]
        first = [
            pltpu.make_async_copy(moment_refs[k], moment_v.at[k], moment_sem.at[k]) for k in range(2)
        ] + [
            pltpu.make_async_copy(arrived_refs[m], arrived_v.at[pl.ds(m * bucket, bucket)], arrived_sem.at[m])
            for m in range(n_from)
        ]
        later = [
            [
                pltpu.make_async_copy(
                    grad_refs[k].at[pl.ds(q * some, some)],
                    grad_v.at[k, pl.ds(q * some, some)],
                    grad_sem.at[q, k],
                )
                for k in range(n_grads)
            ]
            for q in range(parts)
        ]
        outs = [
            pltpu.make_async_copy(
                out_v.at[pl.ds(q * some, some)], out_hbm.at[pl.ds(q * some, some)], out_sem.at[q]
            )
            for q in range(parts)
        ]
        for copy in first + sum(later, []):
            copy.start()

        def step(g, carry):
            at = came_ref[g]
            own = home_ref[g]
            kind = kind_ref[g]

            def moved(k):
                picked = lax.select(kind == 1, moment_v[k, own], arrived_v[at, k].astype(F32))
                return lax.select(kind == 0, jnp.zeros_like(picked), picked)

            total = grad_v[0, g].astype(F32)
            for k in range(1, n_grads):
                total = total + grad_v[k, g].astype(F32)
            first_moment = 0.9 * moved(0) + 0.1 * total
            second_moment = 0.95 * moved(1) + 0.05 * total * total
            out_v[g] = first_moment / (jnp.sqrt(second_moment) + 1.0)
            return carry

        for copy in first:
            copy.wait()
        unroll = math.gcd(some, ADAM_UNROLL)
        for q in range(parts):
            for copy in later[q]:
                copy.wait()

            def trip(i, carry, q=q):
                for u in range(unroll):
                    step(q * some + i * unroll + u, carry)
                return carry

            lax.fori_loop(0, some // unroll, trip, 0)
            outs[q].start()
        for copy in outs:
            copy.wait()

    return pl.pallas_call(
        kernel,
        out_shape=jax.ShapeDtypeStruct(moments[0].shape, F32),
        in_specs=[SMEM] * 3 + [ANY] * (n_grads + 2 + n_from),
        out_specs=ANY,
        scratch_shapes=[
            pltpu.VMEM((n_grads, slots, rows, block), BF16),
            pltpu.VMEM((2, slots, rows, block), F32),
            pltpu.VMEM((n_from * bucket, 2, rows, block), BF16),
            pltpu.VMEM((slots, rows, block), F32),
            pltpu.SemaphoreType.DMA((parts, n_grads)),
            pltpu.SemaphoreType.DMA((2,)),
            pltpu.SemaphoreType.DMA((n_from,)),
            pltpu.SemaphoreType.DMA((parts,)),
        ],
        compiler_params=pltpu.CompilerParams(vmem_limit_bytes=VMEM_LIMIT),
        cost_estimate=cost(15 * slots * rows * block, 17 * slots * rows * block),
        name="adam_step",
    )(*tables, *grads, *moments, *arrived)


def adam_ahead(tables, grads, moments):
    slots, rows, block = moments[0].shape
    n_grads = len(grads)

    def kernel(home_ref, kind_ref, *refs):
        grad_refs = refs[:n_grads]
        moment_refs = refs[n_grads : n_grads + 2]
        outs = refs[n_grads + 2 :]
        unroll = math.gcd(slots, ADAM_UNROLL)

        def trip(i, carry):
            for u in range(unroll):
                g = i * unroll + u
                own = home_ref[g]
                stays = kind_ref[g] == 1
                total = grad_refs[0][g].astype(F32)
                for ref in grad_refs[1:]:
                    total = total + ref[g].astype(F32)
                for k, (keep, term) in enumerate(((0.9, 0.1 * total), (0.95, 0.05 * total * total))):
                    mine = moment_refs[k][own]
                    outs[k][g] = keep * lax.select(stays, mine, jnp.zeros_like(mine)) + term
            return carry

        lax.fori_loop(0, slots // unroll, trip, 0)

    vmem = pl.BlockSpec(memory_space=pltpu.VMEM)
    return pl.pallas_call(
        kernel,
        out_shape=[jax.ShapeDtypeStruct(moments[0].shape, F32)] * 2,
        in_specs=[SMEM] * 2 + [vmem] * (n_grads + 2),
        out_specs=[vmem] * 2,
        compiler_params=pltpu.CompilerParams(vmem_limit_bytes=VMEM_LIMIT),
        cost_estimate=cost(10 * slots * rows * block, 22 * slots * rows * block),
        name="ahead",
    )(*tables, *grads, *moments)


def adam_finish(tables, ahead, arrived):
    slots, rows, block = ahead[0].shape
    parts = math.gcd(slots, FINISH_PARTS)
    some = slots // parts

    def kernel(came_ref, kind_ref, first_hbm, second_hbm, arrived_hbm, out_hbm, ahead_v, arrived_v, out_v, sem, more, out_sem):
        copy = pltpu.make_async_copy(arrived_hbm, arrived_v, more)
        copy.start()
        loads = []
        outs = []
        for q in range(parts):
            at = pl.ds(q * some, some)
            loads.append(
                [
                    pltpu.make_async_copy(hbm.at[at], ahead_v.at[k, at], sem.at[q, k])
                    for k, hbm in enumerate((first_hbm, second_hbm))
                ]
            )
            outs.append(pltpu.make_async_copy(out_v.at[at], out_hbm.at[at], out_sem.at[q]))
        for pair in loads:
            for load in pair:
                load.start()
        copy.wait()
        unroll = math.gcd(some, 2 * ADAM_UNROLL)
        for q in range(parts):
            for load in loads[q]:
                load.wait()

            def trip(i, carry, q=q):
                for u in range(unroll):
                    g = q * some + i * unroll + u
                    at = came_ref[g]
                    comes = kind_ref[g] == 2
                    sums = []
                    for k, keep in enumerate((0.9, 0.95)):
                        theirs = arrived_v[at, k].astype(F32)
                        sums.append(ahead_v[k, g] + keep * lax.select(comes, theirs, jnp.zeros_like(theirs)))
                    out_v[g] = sums[0] / (jnp.sqrt(sums[1]) + 1.0)
                return carry

            lax.fori_loop(0, some // unroll, trip, 0)
            outs[q].start()
        for out in outs:
            out.wait()

    return pl.pallas_call(
        kernel,
        out_shape=jax.ShapeDtypeStruct(ahead[0].shape, F32),
        in_specs=[SMEM] * 2 + [ANY] * 3,
        out_specs=ANY,
        scratch_shapes=[
            pltpu.VMEM((2, slots, rows, block), F32),
            pltpu.VMEM(arrived.shape, BF16),
            pltpu.VMEM((slots, rows, block), F32),
            pltpu.SemaphoreType.DMA((parts, 2)),
            pltpu.SemaphoreType.DMA,
            pltpu.SemaphoreType.DMA((parts,)),
        ],
        compiler_params=pltpu.CompilerParams(vmem_limit_bytes=VMEM_LIMIT),
        cost_estimate=cost(10 * slots * rows * block, 18 * slots * rows * block),
        name="finish",
    )(*tables, *ahead, arrived)


def layer(
    activations,
    cotangent,
    up_weight_blocks,
    down_weight_blocks,
    up_first_moment,
    up_second_moment,
    down_first_moment,
    down_second_moment,
    source,
    new_row,
    new_col,
    col_owner,
):
    tensor_size = lax.axis_size("tensor")
    n_dp = lax.axis_size("dp")
    nx = n_dp // 2
    my_index = lax.axis_index("tensor")
    my_dp = lax.axis_index("dp")
    slot_count, block, _ = up_weight_blocks.shape
    rows = block // n_dp
    bucket = (slot_count + tensor_size - 2) // tensor_size

    sources = source.reshape(tensor_size, slot_count)
    is_live = sources >= 0
    sender_dev = jnp.where(is_live, sources // slot_count, -1)
    sender_slot = jnp.where(is_live, sources % slot_count, 0)
    targets = jnp.arange(tensor_size, dtype=jnp.int32)[:, None]
    outgoing = is_live & (sender_dev == my_index) & (targets != my_index)
    out_flags = outgoing.astype(jnp.int32)
    out_rank = jnp.cumsum(out_flags, axis=1) - out_flags
    chosen = outgoing[:, :, None] & (
        out_rank[:, :, None] == jnp.arange(bucket, dtype=jnp.int32)[None, None, :]
    )
    send_slots = jnp.sum(jnp.where(chosen, sender_slot[:, :, None], 0), axis=1).reshape(-1)
    mine_dev = lax.dynamic_index_in_dim(sender_dev, my_index, 0, keepdims=False)
    mine_slot = lax.dynamic_index_in_dim(sender_slot, my_index, 0, keepdims=False)
    mine_live = mine_dev >= 0
    stays = mine_live & (mine_dev == my_index)
    positions = jnp.arange(slot_count, dtype=jnp.int32)
    earlier = (
        (mine_dev[:, None] == mine_dev[None, :])
        & mine_live[None, :]
        & (positions[None, :] < positions[:, None])
    )
    recv_rank = jnp.minimum(jnp.sum(earlier.astype(jnp.int32), axis=1), bucket - 1)
    home = jnp.where(stays, mine_slot, 0)
    came = jnp.where(mine_live & ~stays, mine_dev * bucket + recv_rank, 0)
    kind = jnp.where(stays, 1, jnp.where(mine_live, 2, 0)).astype(jnp.int32)
    col_count = col_owner.shape[0] // tensor_size
    col_slot = jnp.take(local_columns(col_owner), new_col)
    place = jnp.stack([my_dp // 2, my_dp % 2, my_index]).astype(jnp.int32)
    dp_index = my_dp.reshape(1).astype(jnp.int32)
    tables = (new_row, col_slot, home, came, kind)

    def exchange(packed):
        shaped = packed.reshape((tensor_size, bucket) + packed.shape[1:])
        got = lax.all_to_all(shaped, "tensor", split_axis=0, concat_axis=0, tiled=True)
        return got.reshape((tensor_size * bucket,) + packed.shape[1:])

    core_pairs = [(d, d ^ 1) for d in range(n_dp)]

    def x_pairs(j):
        return [(d, ((d // 2 + j) % nx) * 2 + d % 2) for d in range(n_dp)]

    def far_pairs(bit):
        return [(t, t ^ bit) for t in range(tensor_size)]

    def spread(own):
        parts = []
        for j in range(nx):
            mine = own
            if j:
                mine = lax.ppermute(own, "dp", x_pairs(j))
            parts += [mine, lax.ppermute(mine, "dp", core_pairs)]
        return parts

    up_pack = pack_weight(up_weight_blocks, send_slots, dp_index, rows)
    later_slots, tables, place = lax.optimization_barrier((send_slots, tables, place))
    new_row, col_slot, home, came, kind = tables
    down_pack = pack_weight(down_weight_blocks, later_slots, dp_index, rows)
    up_in = exchange(up_pack)
    down_in = exchange(down_pack)
    up_parts = spread(up_in)
    down_parts = spread(down_in)

    shard = activations.shape[1]
    stacked = shard % block == 0 and tensor_size & (tensor_size - 1) == 0
    if stacked:
        bits = [1 << k for k in reversed(range(tensor_size.bit_length() - 1))]

        def gather(own):
            held = {0: own}
            for bit in bits:
                for m in list(held):
                    held[m ^ bit] = lax.ppermute(held[m], "tensor", far_pairs(bit))
            return [held[m] for m in range(tensor_size)]

        feats = gather(activations)
        backs = gather(cotangent)
        feat_shape = (tensor_size,) + activations.shape
    else:
        feats = [lax.all_gather(activations, "tensor", axis=1, tiled=True)]
        backs = [lax.all_gather(cotangent, "tensor", axis=1, tiled=True)]
        feat_shape = (1,) + feats[0].shape
    row_blocks = feat_shape[0] * feat_shape[2] // block

    ups = (up_first_moment, up_second_moment)
    downs = (down_first_moment, down_second_moment)
    ups_pack = pack_moments(ups, send_slots)
    downs_pack = pack_moments(downs, send_slots)
    ups_in = [exchange(ups_pack)]
    downs_in = [exchange(downs_pack)]

    act, act_t, slopes, x_t, wu = forward_products(
        tables, place, feats, up_weight_blocks, up_parts, col_count, row_blocks, feat_shape
    )

    def share(grads):
        terms = []
        for j in range(nx):
            there = lax.ppermute(grads[2 * j + 1], "dp", core_pairs)
            if j == 0:
                terms += [grads[0], there]
            else:
                both = (grads[2 * j].astype(F32) + there.astype(F32)).astype(BF16)
                terms.append(lax.ppermute(both, "dp", x_pairs(j)))
        return terms

    down_grads = gradient_products(new_row, col_slot, place, backs, (act_t,), n_dp, block, feat_shape)
    down_terms = share(down_grads)
    bpre, wd = back_products(
        tables, place, backs, down_weight_blocks, down_parts, slopes, feat_shape
    )
    up_grads = gradient_products(new_row, col_slot, place, (), (x_t, bpre), n_dp, block, feat_shape)
    up_terms = share(up_grads)
    sums = []
    near = [1 << k for k in range(tensor_size.bit_length() - 1)] if stacked else []
    order = near
    for w, left, turned in ((wd, act, False), (wu, bpre, True)):
        half = tensor_size // 2
        pieces = ((0, half), (half, half)) if stacked else ((0, 1),)
        got = output_products(
            new_row, col_slot, place, w, left, turned, order, pieces, feat_shape, row_blocks
        )
        if not stacked:
            sums.append(lax.psum_scatter(got[0][0], "tensor", scatter_dimension=1, tiled=True))
            continue
        held, send = got
        held = [held]
        for step, bit in enumerate(order):
            if step:
                half = held[-1].shape[0] // 2
                send = sum(s[half : 2 * half].astype(F32) for s in held).astype(BF16)
                held = [s[:half] for s in held]
            held.append(lax.ppermute(send, "tensor", far_pairs(bit)))
        sums.append(sum(s[0].astype(F32) for s in held).astype(BF16))
    out_sum, in_sum = sums

    up_step = adam_step((home, came, kind), up_terms, ups, ups_in)
    ahead = adam_ahead((home, kind), down_terms, downs)
    down_step = adam_finish((came, kind), ahead, downs_in[0])
    return (out_sum, in_sum, up_step, down_step)


def solution(mesh):
    placed = (
        P("dp", "tensor"),
        P("dp", "tensor"),
        P("tensor", None, None),
        P("tensor", None, None),
        P("tensor", "dp", None),
        P("tensor", "dp", None),
        P("tensor", "dp", None),
        P("tensor", "dp", None),
        P(),
        P("tensor"),
        P("tensor"),
        P(),
    )
    return jax.shard_map(
        layer,
        mesh=mesh,
        in_specs=placed,
        out_specs=(
            P("dp", "tensor"),
            P("dp", "tensor"),
            P("tensor", "dp", None),
            P("tensor", "dp", None),
        ),
        check_vma=False,
    )
```
